32 devices in a mesh: fsdp: 16 (over z, x, core), seq: 2 (over y).
Axes of the slice: x: 2, y: 2, z: 4, core: 2. Of those that a mesh axis runs over, the one named last changes fastest.
Arguments:
- clips: bfloat16 [32, 1024, 1024], P('fsdp', 'seq'), may hold values from -6 to 6
- cotangent: bfloat16 [32, 1024, 1024], P('fsdp', 'seq'), may hold values from -6 to 6
- valid: int32 [32], P('fsdp'), may hold values 0 or 1
- norm1_gain: bfloat16 [1024], P('fsdp'), may hold values from 0.5 to 1.5
- norm1_bias: bfloat16 [1024], P('fsdp'), may hold values from -1.5 to 1.5
- query_weight: bfloat16 [1024, 1024], P('fsdp'), may hold values from -0.1875 to 0.1875
- key_weight: bfloat16 [1024, 1024], P('fsdp'), may hold values from -0.1875 to 0.1875
- value_weight: bfloat16 [1024, 1024], P('fsdp'), may hold values from -0.1875 to 0.1875
- query_bias: bfloat16 [1024], P('fsdp'), may hold values from -1.5 to 1.5
- value_bias: bfloat16 [1024], P('fsdp'), may hold values from -1.5 to 1.5
- proj_weight: bfloat16 [1024, 1024], P('fsdp'), may hold values from -2 to 2
- proj_bias: bfloat16 [1024], P('fsdp'), may hold values from -1.5 to 1.5
- norm2_gain: bfloat16 [1024], P('fsdp'), may hold values from 0.5 to 1.5
- norm2_bias: bfloat16 [1024], P('fsdp'), may hold values from -1.5 to 1.5
- fc1_weight: bfloat16 [1024, 4096], P('fsdp'), may hold values from -0.1875 to 0.1875
- fc1_bias: bfloat16 [4096], P('fsdp'), may hold values from -1.5 to 1.5
- fc2_weight: bfloat16 [4096, 1024], P('fsdp'), may hold values from -0.09375 to 0.09375
- fc2_bias: bfloat16 [1024], P('fsdp'), may hold values from -1.5 to 1.5
Outputs:
- layer_out: bfloat16 [32, 1024, 1024], P('fsdp', 'seq')
- grad_clips: float32 [32, 1024, 1024], P('fsdp', 'seq')
- grad_norm1_gain: float32 [1024], P('fsdp')
- grad_norm1_bias: float32 [1024], P('fsdp')
- grad_query_weight: float32 [1024, 1024], P('fsdp')
- grad_key_weight: float32 [1024, 1024], P('fsdp')
- grad_value_weight: float32 [1024, 1024], P('fsdp')
- grad_query_bias: float32 [1024], P('fsdp')
- grad_value_bias: float32 [1024], P('fsdp')
- grad_proj_weight: float32 [1024, 1024], P('fsdp')
- grad_proj_bias: float32 [1024], P('fsdp')
- grad_norm2_gain: float32 [1024], P('fsdp')
- grad_norm2_bias: float32 [1024], P('fsdp')
- grad_fc1_weight: float32 [1024, 4096], P('fsdp')
- grad_fc1_bias: float32 [4096], P('fsdp')
- grad_fc2_weight: float32 [4096, 1024], P('fsdp')
- grad_fc2_bias: float32 [1024], P('fsdp')
The draws below stay inside these ranges and needn't reach their ends.
Inputs may be any that keep to these rules, and one draw needn't show every extreme that they name: Padding clips (valid 0) contribute nothing to any gradient.
All inputs are finite; a program needn't handle non-finite values. No bound on the sum of `valid` on one device may be relied on, other than what follows from the above.
Results may differ from the reference program's by a relative error of at most 0.023.
Values may be sent and summed in bfloat16 or wider, within the bound.
A program may use at most 256 MiB of HBM per device.

```python
import jax
import jax.numpy as jnp
from jax import lax

D = 1024
H = 16
HD = 64
FF = 4096
CLIP_LEN = 1024
QBLK = 512
CLIPS = 32


def touch_ends(result, rng, low, largest):
    longest = result.shape.index(max(result.shape))
    spots = []
    for shift in (0, 1):
        where = [jax.random.randint(jax.random.fold_in(rng, axis), (), 0, length) for axis, length in enumerate(result.shape)]
        where[longest] = (where[longest] + shift) % result.shape[longest]
        spots.append(tuple(where))
    return result.at[spots[0]].set(low).at[spots[1]].set(largest)


def block_scale(stream_key, extent, split, least, largest):
    level = 1.0
    for dim, shards_of in split:
        draws = jax.random.uniform(jax.random.fold_in(jax.random.fold_in(stream_key, 6), dim), (shards_of,), jnp.float32, least / len(split), largest / len(split))
        level = level * jnp.repeat(jnp.exp(draws), extent[dim] // shards_of).reshape((-1,) + (1,) * (len(extent) - 1 - dim))
    return level


def scatter_about(stream_key, extent, width, reach, pieces=(), held_as=jnp.bfloat16):
    values = width * jax.random.normal(stream_key, extent, jnp.float32)
    if pieces:
        values = values * block_scale(stream_key, extent, pieces, -0.22, 0.18)
    return jnp.clip(values, -reach, reach).astype(held_as)


def setup_inputs(seed: int = 0) -> dict:
    splits = jax.random.split(jax.random.key(seed), 19)
    clips = scatter_about(splits[0], (CLIPS, CLIP_LEN, D), 1.0, 6.0, ((0, 16), (1, 2)))
    cotangent = scatter_about(splits[1], (CLIPS, CLIP_LEN, D), 1.0, 6.0, ((0, 16), (1, 2)))
    valid = touch_ends((jax.random.randint(splits[2], (CLIPS,), 0, 3) < 2).astype(jnp.int32), jax.random.fold_in(splits[2], 1), 0, 1)
    norm1_gain = jnp.clip(1.0 + 0.1 * jax.random.normal(splits[3], (D,), jnp.float32), 0.5, 1.5).astype(jnp.bfloat16)
    norm1_bias = scatter_about(splits[4], (D,), 0.3, 1.5, ((0, 16),))
    query_weight = scatter_about(splits[5], (D, D), D ** -0.5, 0.1875, ((0, 16),))
    key_weight = scatter_about(splits[6], (D, D), D ** -0.5, 0.1875, ((0, 16),))
    value_weight = scatter_about(splits[7], (D, D), D ** -0.5, 0.1875, ((0, 16),))
    query_bias = scatter_about(splits[8], (D,), 0.3, 1.5, ((0, 16),))
    value_bias = scatter_about(splits[9], (D,), 0.3, 1.5, ((0, 16),))
    proj_weight = scatter_about(splits[10], (D, D), (8 * D // CLIP_LEN) ** -0.5, 2.0, ((0, 16),))
    proj_bias = scatter_about(splits[11], (D,), 0.3, 1.5, ((0, 16),))
    norm2_gain = jnp.clip(1.0 + 0.1 * jax.random.normal(splits[12], (D,), jnp.float32), 0.5, 1.5).astype(jnp.bfloat16)
    norm2_bias = scatter_about(splits[13], (D,), 0.3, 1.5, ((0, 16),))
    fc1_weight = scatter_about(splits[14], (D, FF), D ** -0.5, 0.1875, ((0, 16),))
    fc1_bias = scatter_about(splits[15], (FF,), 0.3, 1.5, ((0, 16),))
    fc2_weight = scatter_about(splits[16], (FF, D), FF ** -0.5, 0.09375, ((0, 16),))
    fc2_bias = scatter_about(splits[17], (D,), 0.3, 1.5, ((0, 16),))
    return dict(clips=clips, cotangent=cotangent, valid=valid, norm1_gain=norm1_gain, norm1_bias=norm1_bias, query_weight=query_weight, key_weight=key_weight, value_weight=value_weight, query_bias=query_bias, value_bias=value_bias, proj_weight=proj_weight, proj_bias=proj_bias, norm2_gain=norm2_gain, norm2_bias=norm2_bias, fc1_weight=fc1_weight, fc1_bias=fc1_bias, fc2_weight=fc2_weight, fc2_bias=fc2_bias)


@jax.custom_vjp
def low(v):
    return lax.optimization_barrier(v.astype(jnp.bfloat16)).astype(jnp.float32)

@jax.custom_vjp
def low_back(v):
    return v

def low_keep(v):
    return (low(v), None)

def low_pass(kept, grad):
    return (grad,)

def back_keep(v):
    return (v, None)

def back_low(kept, grad):
    return (low(grad),)
low.defvjp(low_keep, low_pass)
low_back.defvjp(back_keep, back_low)
norm_eps = 1e-06

def product(left, right):
    return jnp.dot(left, right, precision=lax.Precision.HIGHEST)

def layer_norm(values_in, gain, shift):
    row_mean = lax.optimization_barrier(jnp.mean(values_in, axis=-1, keepdims=True))
    centred = values_in - row_mean
    spread = lax.optimization_barrier(jnp.mean(centred * centred, axis=-1, keepdims=True))
    return centred * lax.rsqrt(spread + norm_eps) * gain + shift

def score_block(query_rows, key_heads, value_heads):
    scores = jnp.einsum('qhd,khd->hqk', query_rows, key_heads, precision=lax.Precision.HIGHEST) * HD ** (-0.5)
    scores = low_back(scores)
    weights = low(jax.nn.softmax(scores, axis=-1))
    return jnp.einsum('hqk,khd->qhd', weights, value_heads, precision=lax.Precision.HIGHEST)

def layer(clip_in, params):
    norm1_gain, norm1_bias, query_weight, key_weight, value_weight, query_bias, value_bias, proj_weight, proj_bias, norm2_gain, norm2_bias, fc1_weight, fc1_bias, fc2_weight, fc2_bias = params
    length = clip_in.shape[0]
    normed = low(layer_norm(clip_in, norm1_gain, norm1_bias))
    queries = low(low_back(product(normed, query_weight) + query_bias))
    keys_all = low(low_back(product(normed, key_weight)))
    values_all = low(low_back(product(normed, value_weight) + value_bias))
    query_blocks = queries.reshape(length // QBLK, QBLK, H, HD)
    key_heads = keys_all.reshape(length, H, HD)
    value_heads = values_all.reshape(length, H, HD)
    mixed = lax.map(jax.checkpoint(lambda query_rows: score_block(query_rows, key_heads, value_heads)), query_blocks)
    attended = low(low_back(mixed.reshape(length, H * HD)))
    branch = low_back(product(attended, proj_weight) + proj_bias)
    middle = clip_in + branch
    normed_two = low(layer_norm(middle, norm2_gain, norm2_bias))
    hidden_pre = low_back(product(normed_two, fc1_weight) + fc1_bias)
    hidden = low(jax.nn.gelu(hidden_pre, approximate=False))
    mlp_out = low_back(product(hidden, fc2_weight) + fc2_bias)
    return middle + mlp_out

def reference(clips, cotangent, valid, norm1_gain, norm1_bias, query_weight, key_weight, value_weight, query_bias, value_bias, proj_weight, proj_bias, norm2_gain, norm2_bias, fc1_weight, fc1_bias, fc2_weight, fc2_bias):
    params = (norm1_gain.astype(jnp.float32), norm1_bias.astype(jnp.float32), query_weight.astype(jnp.float32), key_weight.astype(jnp.float32), value_weight.astype(jnp.float32), query_bias.astype(jnp.float32), value_bias.astype(jnp.float32), proj_weight.astype(jnp.float32), proj_bias.astype(jnp.float32), norm2_gain.astype(jnp.float32), norm2_bias.astype(jnp.float32), fc1_weight.astype(jnp.float32), fc1_bias.astype(jnp.float32), fc2_weight.astype(jnp.float32), fc2_bias.astype(jnp.float32))

    def one_clip(running, block_item):
        clip_in, clip_cot, clip_flag = block_item
        output, pullback = jax.vjp(layer, clip_in.astype(jnp.float32), params)
        grad_in, grad_params = pullback(clip_cot.astype(jnp.float32) * clip_flag.astype(jnp.float32))
        running = tuple((older + newer for older, newer in zip(running, grad_params)))
        return (running, (output.astype(jnp.bfloat16), grad_in))
    start = tuple((jnp.zeros_like(weight_in) for weight_in in params))
    summed, (outputs, grad_clips) = lax.scan(one_clip, start, (clips, cotangent, valid))
    return (outputs, grad_clips, summed[0], summed[1], summed[2], summed[3], summed[4], summed[5], summed[6], summed[7], summed[8], summed[9], summed[10], summed[11], summed[12], summed[13], summed[14])
```

```python
import jax
import jax.numpy as jnp
from jax import lax
from jax.experimental import pallas as pl
from jax.experimental.pallas import tpu as pltpu
from jax.sharding import PartitionSpec as P

H = 16
QBLK = 512


norm_eps = 1e-06
root_half = 0.7071067811865476
inv_root_tau = 0.3989422804014327


def matmul(left, right):
    return jnp.dot(left, right, preferred_element_type=jnp.float32)


def matmul_nt(left, right):
    return lax.dot_general(
        left, right, (((1,), (1,)), ((), ())), preferred_element_type=jnp.float32
    )


def matmul_tn(left, right):
    return lax.dot_general(
        left, right, (((0,), (0,)), ((), ())), preferred_element_type=jnp.float32
    )


def layer_norm(values_in, gain, shift):
    row_mean = jnp.mean(values_in, axis=-1, keepdims=True)
    centred = values_in - row_mean
    inverse = lax.rsqrt(jnp.mean(centred * centred, axis=-1, keepdims=True) + norm_eps)
    scaled = centred * inverse
    return (scaled * gain + shift, scaled, inverse)


def layer_norm_back(upstream, scaled, inverse, gain):
    dscaled = upstream * gain
    inner = (
        dscaled
        - jnp.mean(dscaled, axis=-1, keepdims=True)
        - scaled * jnp.mean(dscaled * scaled, axis=-1, keepdims=True)
    )
    return (inverse * inner, jnp.sum(upstream * scaled, axis=0), jnp.sum(upstream, axis=0))


def gelu_value(pre_act):
    return 0.5 * pre_act * (1.0 + lax.erf(pre_act * root_half))


def gelu_slope(pre_act):
    return 0.5 * (1.0 + lax.erf(pre_act * root_half)) + pre_act * inv_root_tau * jnp.exp(
        -0.5 * pre_act * pre_act
    )


def attend(queries, keys_all, values_all, head_count):
    length = queries.shape[0]
    head_width = queries.shape[1] // head_count
    score_scale = head_width ** (-0.5)
    query_heads = queries.reshape(length // QBLK, QBLK, head_count, head_width)
    key_heads = keys_all.reshape(length, head_count, head_width)
    value_heads = values_all.reshape(length, head_count, head_width)

    def one_block(query_rows):
        scores = (
            jnp.einsum("qhd,khd->hqk", query_rows, key_heads, preferred_element_type=jnp.float32)
            * score_scale
        )
        peak = jnp.max(scores, axis=-1, keepdims=True)
        raised = jnp.exp(scores - peak)
        row_total = jnp.sum(raised, axis=-1, keepdims=True)
        weights = (raised / row_total).astype(jnp.bfloat16)
        mixed = jnp.einsum("hqk,khd->qhd", weights, value_heads, preferred_element_type=jnp.float32)
        return (mixed.astype(jnp.bfloat16), (peak + jnp.log(row_total))[:, :, 0])

    mixed, log_totals = lax.map(one_block, query_heads)
    return (mixed.reshape(length, head_count * head_width), log_totals)


def attend_back(queries, keys_all, values_all, log_totals, upstream, head_count):
    length = queries.shape[0]
    head_width = queries.shape[1] // head_count
    score_scale = head_width ** (-0.5)
    query_heads = queries.reshape(length // QBLK, QBLK, head_count, head_width)
    upstream_heads = upstream.reshape(length // QBLK, QBLK, head_count, head_width)
    key_heads = keys_all.reshape(length, head_count, head_width)
    value_heads = values_all.reshape(length, head_count, head_width)

    def one_block(running, block_item):
        key_grad, value_grad = running
        query_rows, log_rows, grad_rows = block_item
        scores = (
            jnp.einsum("qhd,khd->hqk", query_rows, key_heads, preferred_element_type=jnp.float32)
            * score_scale
        )
        weights = jnp.exp(scores - log_rows[:, :, None])
        weights_low = weights.astype(jnp.bfloat16)
        grad_weights = jnp.einsum(
            "qhd,khd->hqk", grad_rows, value_heads, preferred_element_type=jnp.float32
        )
        inner = jnp.sum(grad_weights * weights, axis=-1, keepdims=True)
        grad_scores = (weights * (grad_weights - inner)).astype(jnp.bfloat16)
        query_grad = (
            jnp.einsum("hqk,khd->qhd", grad_scores, key_heads, preferred_element_type=jnp.float32)
            * score_scale
        )
        key_grad = (
            key_grad
            + jnp.einsum(
                "hqk,qhd->khd", grad_scores, query_rows, preferred_element_type=jnp.float32
            )
            * score_scale
        )
        value_grad = value_grad + jnp.einsum(
            "hqk,qhd->khd", weights_low, grad_rows, preferred_element_type=jnp.float32
        )
        return ((key_grad, value_grad), query_grad.astype(jnp.bfloat16))

    zeros_heads = jnp.zeros((length, head_count, head_width), jnp.float32)
    (key_grad, value_grad), query_grad = lax.scan(
        one_block, (zeros_heads, zeros_heads), (query_heads, log_totals, upstream_heads)
    )
    width_all = head_count * head_width
    return (
        query_grad.reshape(length, width_all),
        key_grad.reshape(length, width_all).astype(jnp.bfloat16),
        value_grad.reshape(length, width_all).astype(jnp.bfloat16),
    )


def fetch(shards):
    return (
        lax.all_gather(shards[0], "fsdp", axis=0, tiled=True),
        lax.all_gather(shards[1], "fsdp", axis=0, tiled=True),
        lax.all_gather(shards[2], "fsdp", axis=0, tiled=True),
        lax.all_gather(shards[3], "fsdp", axis=0, tiled=True),
        lax.all_gather(shards[4], "fsdp", axis=0, tiled=True),
        lax.all_gather(shards[5], "fsdp", axis=0, tiled=True),
        lax.all_gather(shards[6], "fsdp", axis=0, tiled=True),
        lax.all_gather(shards[7], "fsdp", axis=0, tiled=True),
        lax.all_gather(shards[8], "fsdp", axis=0, tiled=True),
        lax.all_gather(shards[9], "fsdp", axis=0, tiled=True),
        lax.all_gather(shards[10], "fsdp", axis=0, tiled=True),
        lax.all_gather(shards[11], "fsdp", axis=0, tiled=True),
        lax.all_gather(shards[12], "fsdp", axis=0, tiled=True),
        lax.all_gather(shards[13], "fsdp", axis=0, tiled=True),
        lax.all_gather(shards[14], "fsdp", axis=0, tiled=True),
    )


def settle(grads):
    shares = (
        lax.psum_scatter(
            grads[0].astype(jnp.bfloat16), "fsdp", scatter_dimension=0, tiled=True
        ).astype(jnp.float32),
        lax.psum_scatter(
            grads[1].astype(jnp.bfloat16), "fsdp", scatter_dimension=0, tiled=True
        ).astype(jnp.float32),
        lax.psum_scatter(
            grads[2].astype(jnp.bfloat16), "fsdp", scatter_dimension=0, tiled=True
        ).astype(jnp.float32),
        lax.psum_scatter(
            grads[3].astype(jnp.bfloat16), "fsdp", scatter_dimension=0, tiled=True
        ).astype(jnp.float32),
        lax.psum_scatter(
            grads[4].astype(jnp.bfloat16), "fsdp", scatter_dimension=0, tiled=True
        ).astype(jnp.float32),
        lax.psum_scatter(
            grads[5].astype(jnp.bfloat16), "fsdp", scatter_dimension=0, tiled=True
        ).astype(jnp.float32),
        lax.psum_scatter(
            grads[6].astype(jnp.bfloat16), "fsdp", scatter_dimension=0, tiled=True
        ).astype(jnp.float32),
        lax.psum_scatter(
            grads[7].astype(jnp.bfloat16), "fsdp", scatter_dimension=0, tiled=True
        ).astype(jnp.float32),
        lax.psum_scatter(
            grads[8].astype(jnp.bfloat16), "fsdp", scatter_dimension=0, tiled=True
        ).astype(jnp.float32),
        lax.psum_scatter(
            grads[9].astype(jnp.bfloat16), "fsdp", scatter_dimension=0, tiled=True
        ).astype(jnp.float32),
        lax.psum_scatter(
            grads[10].astype(jnp.bfloat16), "fsdp", scatter_dimension=0, tiled=True
        ).astype(jnp.float32),
        lax.psum_scatter(
            grads[11].astype(jnp.bfloat16), "fsdp", scatter_dimension=0, tiled=True
        ).astype(jnp.float32),
        lax.psum_scatter(
            grads[12].astype(jnp.bfloat16), "fsdp", scatter_dimension=0, tiled=True
        ).astype(jnp.float32),
        lax.psum_scatter(
            grads[13].astype(jnp.bfloat16), "fsdp", scatter_dimension=0, tiled=True
        ).astype(jnp.float32),
        lax.psum_scatter(
            grads[14].astype(jnp.bfloat16), "fsdp", scatter_dimension=0, tiled=True
        ).astype(jnp.float32),
    )
    return (
        lax.psum(shares[0].astype(jnp.bfloat16), "seq").astype(jnp.float32),
        lax.psum(shares[1].astype(jnp.bfloat16), "seq").astype(jnp.float32),
        lax.psum(shares[2].astype(jnp.bfloat16), "seq").astype(jnp.float32),
        lax.psum(shares[3].astype(jnp.bfloat16), "seq").astype(jnp.float32),
        lax.psum(shares[4].astype(jnp.bfloat16), "seq").astype(jnp.float32),
        lax.psum(shares[5].astype(jnp.bfloat16), "seq").astype(jnp.float32),
        lax.psum(shares[6].astype(jnp.bfloat16), "seq").astype(jnp.float32),
        lax.psum(shares[7].astype(jnp.bfloat16), "seq").astype(jnp.float32),
        lax.psum(shares[8].astype(jnp.bfloat16), "seq").astype(jnp.float32),
        lax.psum(shares[9].astype(jnp.bfloat16), "seq").astype(jnp.float32),
        lax.psum(shares[10].astype(jnp.bfloat16), "seq").astype(jnp.float32),
        lax.psum(shares[11].astype(jnp.bfloat16), "seq").astype(jnp.float32),
        lax.psum(shares[12].astype(jnp.bfloat16), "seq").astype(jnp.float32),
        lax.psum(shares[13].astype(jnp.bfloat16), "seq").astype(jnp.float32),
        lax.psum(shares[14].astype(jnp.bfloat16), "seq").astype(jnp.float32),
    )


def one_clip(clip_in, clip_cot, clip_flag, gathered, head_count):
    (
        norm1_gain,
        norm1_bias,
        query_weight,
        key_weight,
        value_weight,
        query_bias,
        value_bias,
        proj_weight,
        proj_bias,
        norm2_gain,
        norm2_bias,
        fc1_weight,
        fc1_bias,
        fc2_weight,
        fc2_bias,
    ) = gathered
    gain_one = norm1_gain.astype(jnp.float32)
    gain_two = norm2_gain.astype(jnp.float32)
    tokens_in = clip_in.astype(jnp.float32)
    normed, scaled_one, inverse_one = layer_norm(
        tokens_in, gain_one, norm1_bias.astype(jnp.float32)
    )
    normed_low = normed.astype(jnp.bfloat16)
    queries = (matmul(normed_low, query_weight) + query_bias.astype(jnp.float32)).astype(
        jnp.bfloat16
    )
    keys_all = matmul(normed_low, key_weight).astype(jnp.bfloat16)
    values_all = (matmul(normed_low, value_weight) + value_bias.astype(jnp.float32)).astype(
        jnp.bfloat16
    )
    query_heads, key_heads, value_heads = (
        lax.all_to_all(queries, "seq", split_axis=1, concat_axis=0, tiled=True),
        lax.all_to_all(keys_all, "seq", split_axis=1, concat_axis=0, tiled=True),
        lax.all_to_all(values_all, "seq", split_axis=1, concat_axis=0, tiled=True),
    )
    mixed_heads, log_totals = attend(query_heads, key_heads, value_heads, head_count)
    attended = lax.all_to_all(mixed_heads, "seq", split_axis=0, concat_axis=1, tiled=True)
    middle = tokens_in + matmul(attended, proj_weight) + proj_bias.astype(jnp.float32)
    normed_two, scaled_two, inverse_two = layer_norm(
        middle, gain_two, norm2_bias.astype(jnp.float32)
    )
    normed_two_low = normed_two.astype(jnp.bfloat16)
    hidden_pre = matmul(normed_two_low, fc1_weight) + fc1_bias.astype(jnp.float32)
    hidden_low = gelu_value(hidden_pre).astype(jnp.bfloat16)
    output = middle + matmul(hidden_low, fc2_weight) + fc2_bias.astype(jnp.float32)
    grad_out = clip_cot.astype(jnp.float32) * clip_flag.astype(jnp.float32)
    grad_mlp = grad_out.astype(jnp.bfloat16)
    grad_fc2_weight = matmul_tn(hidden_low, grad_mlp)
    grad_fc2_bias = jnp.sum(grad_mlp.astype(jnp.float32), axis=0)
    grad_pre = (matmul_nt(grad_mlp, fc2_weight) * gelu_slope(hidden_pre)).astype(jnp.bfloat16)
    grad_fc1_weight = matmul_tn(normed_two_low, grad_pre)
    grad_fc1_bias = jnp.sum(grad_pre.astype(jnp.float32), axis=0)
    grad_norm_two = matmul_nt(grad_pre, fc1_weight)
    grad_ln_two, grad_norm2_gain, grad_norm2_bias = layer_norm_back(
        grad_norm_two, scaled_two, inverse_two, gain_two
    )
    grad_middle = grad_out + grad_ln_two
    grad_branch = grad_middle.astype(jnp.bfloat16)
    grad_proj_weight = matmul_tn(attended, grad_branch)
    grad_proj_bias = jnp.sum(grad_branch.astype(jnp.float32), axis=0)
    grad_att = matmul_nt(grad_branch, proj_weight).astype(jnp.bfloat16)
    grad_att_heads = lax.all_to_all(grad_att, "seq", split_axis=1, concat_axis=0, tiled=True)
    query_grad, key_grad, value_grad = attend_back(
        query_heads, key_heads, value_heads, log_totals, grad_att_heads, head_count
    )
    grad_queries, grad_keys, grad_values = (
        lax.all_to_all(query_grad, "seq", split_axis=0, concat_axis=1, tiled=True),
        lax.all_to_all(key_grad, "seq", split_axis=0, concat_axis=1, tiled=True),
        lax.all_to_all(value_grad, "seq", split_axis=0, concat_axis=1, tiled=True),
    )
    grad_query_weight = matmul_tn(normed_low, grad_queries)
    grad_key_weight = matmul_tn(normed_low, grad_keys)
    grad_value_weight = matmul_tn(normed_low, grad_values)
    grad_query_bias = jnp.sum(grad_queries.astype(jnp.float32), axis=0)
    grad_value_bias = jnp.sum(grad_values.astype(jnp.float32), axis=0)
    grad_norm_one = (
        matmul_nt(grad_queries, query_weight)
        + matmul_nt(grad_keys, key_weight)
        + matmul_nt(grad_values, value_weight)
    )
    grad_ln_one, grad_norm1_gain, grad_norm1_bias = layer_norm_back(
        grad_norm_one, scaled_one, inverse_one, gain_one
    )
    grad_in = grad_middle + grad_ln_one
    grads = (
        grad_norm1_gain,
        grad_norm1_bias,
        grad_query_weight,
        grad_key_weight,
        grad_value_weight,
        grad_query_bias,
        grad_value_bias,
        grad_proj_weight,
        grad_proj_bias,
        grad_norm2_gain,
        grad_norm2_bias,
        grad_fc1_weight,
        grad_fc1_bias,
        grad_fc2_weight,
        grad_fc2_bias,
    )
    return (output.astype(jnp.bfloat16), grad_in, grads)


def body(
    clips,
    cotangent,
    valid,
    norm1_gain,
    norm1_bias,
    query_weight,
    key_weight,
    value_weight,
    query_bias,
    value_bias,
    proj_weight,
    proj_bias,
    norm2_gain,
    norm2_bias,
    fc1_weight,
    fc1_bias,
    fc2_weight,
    fc2_bias,
):
    shards = (
        norm1_gain,
        norm1_bias,
        query_weight,
        key_weight,
        value_weight,
        query_bias,
        value_bias,
        proj_weight,
        proj_bias,
        norm2_gain,
        norm2_bias,
        fc1_weight,
        fc1_bias,
        fc2_weight,
        fc2_bias,
    )
    slot_count = clips.shape[0]
    head_count = H // lax.axis_size("seq")
    summed = None
    outputs = []
    grad_list = []
    for batch_slot in range(slot_count):
        gathered = fetch(shards)
        output, grad_in, grads = one_clip(
            clips[batch_slot], cotangent[batch_slot], valid[batch_slot], gathered, head_count
        )
        summed = (
            grads
            if summed is None
            else tuple((older + newer for older, newer in zip(summed, grads)))
        )
        outputs.append(output)
        grad_list.append(grad_in)
    summed = settle(summed)
    return (
        jnp.stack(outputs),
        jnp.stack(grad_list),
        summed[0],
        summed[1],
        summed[2],
        summed[3],
        summed[4],
        summed[5],
        summed[6],
        summed[7],
        summed[8],
        summed[9],
        summed[10],
        summed[11],
        summed[12],
        summed[13],
        summed[14],
    )


T, D, FF, NTILE = 1024, 1024, 4096, 8

log2_e = 1.4426950408889634
HD = 64
F32, BF16 = jnp.float32, jnp.bfloat16
ANY = pl.BlockSpec(memory_space=pl.ANY)


def dot(left, right, cl=1, cr=0):
    return lax.dot_general(left, right, (((cl,), (cr,)), ((), ())), preferred_element_type=F32)


def fwd_compute(x_v, sm_v, wqkv, wp_v, w1_v, w2_v, n1t, qkvt, ot, lse_v, mid, n2, acc, hst, gst, b1_v, smt,
                get_tile, put_tile, hooks):
    T, D = x_v.shape
    tile = hst.shape[2]
    FF = w1_v.shape[1]
    heads = D // HD
    smt[...] = jnp.transpose(sm_v[...])

    def ln1(i, c):
        r = pl.multiple_of(i * 256, 256)
        v = x_v[pl.ds(r, 256), :].astype(F32)
        m = jnp.mean(v, axis=-1, keepdims=True)
        d = v - m
        s = d * lax.rsqrt(jnp.mean(d * d, axis=-1, keepdims=True) + norm_eps)
        n1t[:, pl.ds(r, 256)] = jnp.transpose((s * sm_v[0:1, :] + sm_v[1:2, :]).astype(BF16))
        return c

    lax.fori_loop(0, T // 256, ln1, 0)
    hooks.before_qkv()
    half = D // 2
    for j in range(3):
        for o in range(2):
            v = dot(wqkv[j, :, o * half:(o + 1) * half], n1t[...], 0, 0)
            if j != 1:
                v = v + smt[o * half:(o + 1) * half, (2 if j == 0 else 3):(3 if j == 0 else 4)]
            qkvt[j, o * half:(o + 1) * half, :] = v.astype(BF16)
        hooks.qkv_tick(j)

    qb = T // 2
    ones = jnp.ones((16, T), BF16)

    def head(h, c):
        r = pl.multiple_of(h * HD, HD)
        kh = qkvt[1, pl.ds(r, HD), :]
        vh = jnp.concatenate([qkvt[2, pl.ds(r, HD), :], ones], axis=0)
        for b in range(2):
            qh = qkvt[0, pl.ds(r, HD), b * qb:(b + 1) * qb]
            s = dot(kh, qh, 0, 0)
            m = jnp.max(s, axis=0, keepdims=True)
            p = jnp.exp2((s - m) * (log2_e * HD ** -0.5)).astype(BF16)
            o = dot(vh, p)
            total = o[HD:HD + 1, :]
            ot[pl.ds(r, HD), b * qb:(b + 1) * qb] = (o[:HD, :] / total).astype(BF16)
            lse_v[pl.ds(h, 1), b * qb:(b + 1) * qb] = m * HD ** -0.5 + jnp.log(total)
        return c

    def pair(i, c):
        head(2 * i, c)
        head(2 * i + 1, c)
        hooks.attn_tick(i)
        return c

    lax.fori_loop(0, heads // 2, pair, 0)
    hooks.before_proj()

    def proj(i, c):
        r = pl.multiple_of(i * 512, 512)
        v = dot(ot[:, pl.ds(r, 512)], wp_v[...], 0, 0) + x_v[pl.ds(r, 512), :].astype(F32) + sm_v[4:5, :]
        mid[pl.ds(r, 512), :] = v
        m = jnp.mean(v, axis=-1, keepdims=True)
        d = v - m
        s = d * lax.rsqrt(jnp.mean(d * d, axis=-1, keepdims=True) + norm_eps)
        n2[pl.ds(r, 512), :] = (s * sm_v[5:6, :] + sm_v[6:7, :]).astype(BF16)
        acc[pl.ds(r, 512), :] = v + sm_v[7:8, :]
        return c

    lax.fori_loop(0, T // 512, proj, 0)
    for k in range(FF // tile):
        kk = k * tile
        b1_v[k:k + 1, :] = sm_v[8 + kk // D:9 + kk // D, kk % D:kk % D + tile]
    hooks.before_mlp()

    def mlp(j, c):
        t = get_tile(j)
        slot = j % 2
        col = pl.multiple_of(t * tile, tile)
        hooks.mlp_tick(j)

        def rows(i, c2):
            r = pl.multiple_of(i * 512, 512)
            u = dot(n2[pl.ds(r, 512), :], w1_v[:, pl.ds(col, tile)]) + b1_v[pl.ds(t, 1), :]
            cdf = 0.5 + 0.5 * lax.erf(u * root_half)
            hb = (u * cdf).astype(BF16)
            hst[slot, pl.ds(r, 512), :] = hb
            gst[slot, pl.ds(r, 512), :] = (cdf + (u * inv_root_tau) * jnp.exp2(u * u * (-0.5 * log2_e))).astype(BF16)
            acc[pl.ds(r, 512), :] += dot(hb, w2_v[pl.ds(col, tile), :])
            return c2

        lax.fori_loop(0, T // 512, rows, 0)
        put_tile(j, t, slot)
        return c

    lax.fori_loop(0, FF // tile, mlp, 0)


class NoHooks:
    def __getattr__(self, name):
        return lambda *a: None


def split3(v):
    hi = v.astype(BF16)
    r = v - hi.astype(F32)
    md = r.astype(BF16)
    lo = (r - md.astype(F32)).astype(BF16)
    return hi, md, lo


def aug_rows(v):
    hi, md, lo = split3(v)
    z = jnp.zeros((13, v.shape[1]), BF16)
    return jnp.concatenate([hi, md, lo, z], axis=0)


def bwd_mlp(g, n2, gacc, h, gp, w1t, w2t, sg_v, j, t, col_slot, put_w2, put_w1):
    gb = g[...]
    put_w2(dot(h[col_slot], gb, 0, 0).astype(BF16))
    pre = (dot(gb, w2t[col_slot], 1, 1) * gp[col_slot].astype(F32)).astype(BF16)
    gp[col_slot] = pre
    sg_v[pl.ds(t, 1), :] = jnp.sum(pre.astype(F32), axis=0, keepdims=True)
    put_w1(dot(n2[...], pre, 0, 0).astype(BF16))
    v = dot(pre, w1t[col_slot], 1, 1)

    @pl.when(j == 0)
    def _():
        gacc[...] = v

    @pl.when(j > 0)
    def _():
        gacc[...] += v


def ln_back(up, v, gain):
    m = jnp.mean(v, axis=-1, keepdims=True)
    d = v - m
    r = lax.rsqrt(jnp.mean(d * d, axis=-1, keepdims=True) + norm_eps)
    xh = d * r
    s = up * gain
    back = r * (s - jnp.mean(s, axis=-1, keepdims=True) - xh * jnp.mean(s * xh, axis=-1, keepdims=True))
    return back, jnp.sum(up * xh, axis=0, keepdims=True), jnp.sum(up, axis=0, keepdims=True)


def bwd_head(h, qkvt, ot, dot_v, lse_v):
    T = ot.shape[1]
    qb = T // 2
    scale = HD ** -0.5
    r = pl.multiple_of(h * HD, HD)
    rows = pl.ds(r, HD)
    ones = jnp.ones((16, T), BF16)
    kh = qkvt[1, rows, :]
    ka = jnp.concatenate([kh, ones], axis=0)
    va = jnp.concatenate([qkvt[2, rows, :], ones], axis=0)
    dk = dv = None
    for b in range(2):
        cols = slice(b * qb, (b + 1) * qb)
        qh = qkvt[0, rows, cols] * jnp.asarray(scale, BF16)
        do = dot_v[rows, cols]
        delta = jnp.sum(do.astype(F32) * ot[rows, cols].astype(F32), axis=0, keepdims=True)
        qa = jnp.concatenate([qh, aug_rows(-lse_v[pl.ds(h, 1), cols])], axis=0)
        da = jnp.concatenate([do, aug_rows(-delta)], axis=0)
        p = jnp.exp2(dot(qa, ka, 0, 0) * log2_e)
        ds = (p * dot(da, va, 0, 0)).astype(BF16)
        ndv = dot(do, p.astype(BF16))
        ndk = dot(qh, ds)
        dv = ndv if dv is None else dv + ndv
        dk = ndk if dk is None else dk + ndk
        qkvt[0, rows, cols] = (dot(kh, ds, 1, 1) * scale).astype(BF16)
    qkvt[1, rows, :] = dk.astype(BF16)
    qkvt[2, rows, :] = dv.astype(BF16)


def fwd_kernel(x,sm,wqkv,wp,w1,w2, out,n1t_o,qkvt_o,ot_o,lse_o,mid_o,n2_o,h_o,g_o, x_v,sm_v,wqkv_v,wp_v,w1_v,w2_v,n1t,qkvt,ot,lse_v,mid,n2,acc,hst,gst,b1_v,smt,sem,osem,tsem):
    ins=[(x,x_v),(sm,sm_v),(wqkv,wqkv_v),(wp,wp_v),(w1,w1_v),(w2,w2_v)]
    cps=[pltpu.make_async_copy(a,b,sem.at[i]) for i,(a,b) in enumerate(ins)]
    for c in cps: c.start()
    for c in cps: c.wait()
    tile=hst.shape[2]
    def tcp(j,t,slot,k):
        return pltpu.make_async_copy((hst,gst)[k].at[slot],(h_o,g_o)[k].at[t],tsem.at[slot,k])
    class Hk(NoHooks):
        def mlp_tick(self,j):
            @pl.when(j>=2)
            def _():
                for k in range(2): tcp(j-2,j-2,j%2,k).wait()
    def put(j,t,slot):
        for k in range(2): tcp(j,t,slot,k).start()
    fwd_compute(x_v,sm_v,wqkv_v,wp_v,w1_v,w2_v,n1t,qkvt,ot,lse_v,mid,n2,acc,hst,gst,b1_v,smt,lambda j:j,put,Hk())
    for j in (6,7):
        for k in range(2): tcp(j,j,j%2,k).wait()
    x_v[...]=acc[...].astype(BF16)
    outs=[(x_v,out),(n1t,n1t_o),(qkvt,qkvt_o),(ot,ot_o),(lse_v,lse_o),(mid,mid_o),(n2,n2_o)]
    cps=[pltpu.make_async_copy(a,b,osem.at[i]) for i,(a,b) in enumerate(outs)]
    for c in cps: c.start()
    for c in cps: c.wait()


def bwd_kernel(cot,x,sm,wqkv,wp,w1,w2,n1t,qkvt,ot,lse,mid,n2,hs,gs, gx,dqkv,dwp,dw1,dw2,sg,
  g_v,n2_v,gacc,h_v,gp_v,w1_v,w2_v,b1g,mid_v,qkvt_v,ot_v,do_v,lse_v,n1t_v,x_v,sm_v,sg_v,st_v,gx_v,sem,tsem,osem,msem,xsem):
    def cp(a,b,i):
        return pltpu.make_async_copy(a,b,sem.at[i])
    first=[cp(cot,g_v,0),cp(n2,n2_v,1),cp(sm,sm_v,2)]
    later=[cp(qkvt,qkvt_v,3),cp(ot,ot_v,4),cp(lse,lse_v,5),cp(n1t,n1t_v,6),cp(x,x_v,7)]
    def tl(t,s):
        c=pl.multiple_of(t*512,512)
        return [pltpu.make_async_copy(hs.at[t],h_v.at[s],tsem.at[s,0]),pltpu.make_async_copy(gs.at[t],gp_v.at[s],tsem.at[s,1]),
          pltpu.make_async_copy(w1.at[:,pl.ds(c,512)],w1_v.at[s],tsem.at[s,2]),pltpu.make_async_copy(w2.at[pl.ds(c,512),:],w2_v.at[s],tsem.at[s,3])]
    for c in first: c.start()
    for c in tl(0,0): c.start()
    for c in later: c.start()
    for c in first: c.wait()
    sg_v[...]=jnp.zeros_like(sg_v)
    sg_v[7:8,:]=jnp.sum(g_v[...].astype(F32),axis=0,keepdims=True)
    def wcp(k,t):
        c=pl.multiple_of(t*512,512)
        return pltpu.make_async_copy(st_v.at[k],dw2.at[pl.ds(c,512),:],osem.at[k]) if k==0 else pltpu.make_async_copy(st_v.at[k].reshape(1024,512) if False else n_st(k),dw1.at[:,pl.ds(c,512)],osem.at[k])
    def n_st(k): return st1_v
    st1_v=gx_v
    def tile(j,c):
        s=j%2
        @pl.when(j+1<NTILE)
        def _():
            for c_ in tl(j+1,1-s): c_.start()
        for c_ in tl(j,s): c_.wait()
        def p2(v):
            @pl.when(j>0)
            def _(): wcp(0,j-1).wait()
            st_v[0]=v; wcp(0,j).start()
        def p1(v):
            @pl.when(j>0)
            def _(): wcp(1,j-1).wait()
            st1_v[...]=v; wcp(1,j).start()
        bwd_mlp(g_v,n2_v,gacc,h_v,gp_v,w1_v,w2_v,b1g,j,j,s,p2,p1)
        return c
    lax.fori_loop(0,NTILE,tile,0)
    wcp(0,NTILE-1).wait(); wcp(1,NTILE-1).wait()
    for k in range(NTILE):
        kk=k*512
        sg_v[8+kk//D:9+kk//D,kk%D:kk%D+512]=b1g[k:k+1,:]
    wpl=[pltpu.make_async_copy(wp.at[i*512:(i+1)*512,:],w2_v.at[i],tsem.at[i,3]) for i in range(2)]
    for c in wpl: c.start()
    wl=[]
    for j in range(3):
        for i in range(2):
            wl.append(pltpu.make_async_copy(wqkv.at[j,:,i*512:(i+1)*512],(h_v,gp_v,w1_v)[j].at[i],tsem.at[i,j]))
    for c in wl: c.start()
    def ml(i,s): return pltpu.make_async_copy(mid.at[pl.ds(pl.multiple_of(i*256,256),256),:],mid_v.at[s],msem.at[s])
    ml(0,0).start()
    def ln2(i,c):
        r=pl.multiple_of(i*256,256); s=i%2
        @pl.when(i<3)
        def _(): ml(i+1,1-s).start()
        ml(i,s).wait()
        back,dg,db=ln_back(gacc[pl.ds(r,256),:],mid_v[s],sm_v[5:6,:])
        gm=g_v[pl.ds(r,256),:].astype(F32)+back
        gacc[pl.ds(r,256),:]=gm
        gb=gm.astype(BF16)
        g_v[pl.ds(r,256),:]=gb
        sg_v[5:6,:]+=dg; sg_v[6:7,:]+=db; sg_v[4:5,:]+=jnp.sum(gb.astype(F32),axis=0,keepdims=True)
        return c
    lax.fori_loop(0,4,ln2,0)
    for c in later: c.wait()
    for c in wpl: c.wait()
    for i in range(2):
        st_v[i]=dot(ot_v[i*512:(i+1)*512,:],g_v[...]).astype(BF16)
        do_v[i*512:(i+1)*512,:]=dot(w2_v[i],g_v[...],1,1).astype(BF16)
    op=[pltpu.make_async_copy(st_v.at[i],dwp.at[i*512:(i+1)*512,:],osem.at[i]) for i in range(2)]
    for c in op: c.start()
    def hd(h,c):
        bwd_head(h,qkvt_v,ot_v,do_v,lse_v)
        return c
    lax.fori_loop(0,16,hd,0)
    for c in op: c.wait()
    for c in wl: c.wait()
    ones=jnp.ones((16,T),BF16)
    for j in (0,2):
        sg_v[(2,None,3)[j]:(3,None,4)[j],:]=dot(ones,qkvt_v[j],1,1)[0:1,:]
    def ocp(j,i): return pltpu.make_async_copy(st_v.at[i],dqkv.at[j,i*512:(i+1)*512,:],osem.at[i])
    for j in range(3):
        for i in range(2):
            if j>0: ocp(j-1,i).wait()
            st_v[i]=dot(n1t_v[i*512:(i+1)*512,:],qkvt_v[j],1,1).astype(BF16)
            ocp(j,i).start()
    for i in range(2): ocp(2,i).wait()
    def xcp(i,s): return pltpu.make_async_copy(mid_v.at[s],gx.at[pl.ds(pl.multiple_of(i*256,256),256),:],xsem.at[s])
    def fin(i,c):
        r=pl.multiple_of(i*256,256); s=i%2
        up=None
        for j,b in enumerate((h_v,gp_v,w1_v)):
            for k in range(2):
                v=dot(qkvt_v[j,k*512:(k+1)*512,pl.ds(r,256)],b[k],0,1)
                up=v if up is None else up+v
        back,dg,db=ln_back(up,x_v[pl.ds(r,256),:].astype(F32),sm_v[0:1,:])
        @pl.when(i>=2)
        def _(): xcp(i-2,s).wait()
        mid_v[s]=gacc[pl.ds(r,256),:]+back
        xcp(i,s).start()
        sg_v[0:1,:]+=dg; sg_v[1:2,:]+=db
        return c
    lax.fori_loop(0,4,fin,0)
    xcp(2,0).wait(); xcp(3,1).wait()
    c=pltpu.make_async_copy(sg_v,sg,sem.at[0]); c.start(); c.wait()


S = jax.ShapeDtypeStruct
V = pltpu.VMEM

def fwd_call():
    return pl.pallas_call(fwd_kernel,name="k1",in_specs=[ANY]*6,out_specs=[ANY]*9,
     out_shape=[S((T,D),BF16),S((D,T),BF16),S((3,D,T),BF16),S((D,T),BF16),S((16,T),F32),S((T,D),F32),S((T,D),BF16),S((8,T,512),BF16),S((8,T,512),BF16)],
     scratch_shapes=[pltpu.VMEM((T,D),BF16),pltpu.VMEM((16,D),F32),pltpu.VMEM((3,D,D),BF16),pltpu.VMEM((D,D),BF16),pltpu.VMEM((D,FF),BF16),pltpu.VMEM((FF,D),BF16),
      pltpu.VMEM((D,T),BF16),pltpu.VMEM((3,D,T),BF16),pltpu.VMEM((D,T),BF16),pltpu.VMEM((16,T),F32),pltpu.VMEM((T,D),F32),pltpu.VMEM((T,D),BF16),pltpu.VMEM((T,D),F32),
      pltpu.VMEM((2,T,512),BF16),pltpu.VMEM((2,T,512),BF16),pltpu.VMEM((8,512),F32),pltpu.VMEM((D,16),F32),
      pltpu.SemaphoreType.DMA((8,)),pltpu.SemaphoreType.DMA((8,)),pltpu.SemaphoreType.DMA((2,2))],
     compiler_params=pltpu.CompilerParams(vmem_limit_bytes=63<<20))


def bwd_call():
    return pl.pallas_call(bwd_kernel,name="k2",in_specs=[ANY]*15,out_specs=[ANY]*6,
     out_shape=[S((T,D),F32),S((3,D,D),BF16),S((D,D),BF16),S((D,FF),BF16),S((FF,D),BF16),S((16,D),F32)],
     scratch_shapes=[V((T,D),BF16),V((T,D),BF16),V((T,D),F32),V((2,T,512),BF16),V((2,T,512),BF16),V((2,D,512),BF16),V((2,512,D),BF16),V((8,512),F32),V((2,256,D),F32),
      V((3,D,T),BF16),V((D,T),BF16),V((D,T),BF16),V((16,T),F32),V((D,T),BF16),V((T,D),BF16),V((16,D),F32),V((16,D),F32),V((2,512,D),BF16),V((D,512),BF16),
      pltpu.SemaphoreType.DMA((8,)),pltpu.SemaphoreType.DMA((2,4)),pltpu.SemaphoreType.DMA((2,)),pltpu.SemaphoreType.DMA((2,)),pltpu.SemaphoreType.DMA((2,))],
     compiler_params=pltpu.CompilerParams(vmem_limit_bytes=63<<20))


def fast_body(clips, cotangent, valid, *shards):
    me = lax.axis_index("fsdp")
    mine = lax.axis_index("seq")
    x = lax.all_to_all(clips, "seq", split_axis=0, concat_axis=1, tiled=True)[0]
    flag = valid[mine].astype(jnp.bfloat16)
    cot = lax.all_to_all(cotangent, "seq", split_axis=0, concat_axis=1, tiled=True)[0] * flag
    (g1, b1, wq, wk, wv, bq, bv, wp, bp, g2, b2, w1, fb1, w2, fb2) = shards
    gather = lambda v, axis=0: lax.all_gather(v, "fsdp", axis=axis, tiled=True)
    packed = gather(jnp.concatenate([g1, b1, bq, bv, bp, g2, b2, fb2, fb1])[None])
    n = g1.shape[0]
    vecs = packed[:, : 8 * n].reshape(-1, 8, n).transpose(1, 0, 2).reshape(8, -1)
    fvec = packed[:, 8 * n :].reshape(-1, D)
    sm = jnp.concatenate([vecs, fvec, jnp.zeros((4, D), jnp.bfloat16)]).astype(jnp.float32)
    wqkv = gather(jnp.stack([wq, wk, wv]), 1)
    wp_all, w1_all, w2_all = gather(wp), gather(w1), gather(w2)
    out, *saved = fwd_call()(x, sm, wqkv, wp_all, w1_all, w2_all)
    gx, dqkv, dwp, dw1, dw2, sg = bwd_call()(cot, x, sm, wqkv, wp_all, w1_all, w2_all, *saved)
    back = lambda v: lax.all_to_all(v[None], "seq", split_axis=1, concat_axis=0, tiled=True)

    def total(v, axis=0):
        part = lax.psum_scatter(v, "fsdp", scatter_dimension=axis, tiled=True)
        return lax.psum(part, "seq").astype(jnp.float32)

    dw2, dw1, dqkv, dwp = total(dw2), total(dw1), total(dqkv, 1), total(dwp)
    sg = lax.psum(sg, ("fsdp", "seq"))
    own = lax.dynamic_slice(sg[:8], (0, me * n), (8, n))
    m = fb1.shape[0]
    dfb1 = lax.dynamic_slice(sg[8:12].reshape(-1), (me * m,), (m,))
    gx = back(gx.astype(jnp.bfloat16)).astype(jnp.float32)
    return (back(out), gx, own[0], own[1], dqkv[0], dqkv[1], dqkv[2], own[2], own[3], dwp, own[4], own[5], own[6], dw1, dfb1, dw2, own[7])


def solution(mesh):
    in_specs = (
        P("fsdp", "seq", None),
        P("fsdp", "seq", None),
        P("fsdp"),
        P("fsdp"),
        P("fsdp"),
        P("fsdp", None),
        P("fsdp", None),
        P("fsdp", None),
        P("fsdp"),
        P("fsdp"),
        P("fsdp", None),
        P("fsdp"),
        P("fsdp"),
        P("fsdp"),
        P("fsdp", None),
        P("fsdp"),
        P("fsdp", None),
        P("fsdp"),
    )
    out_specs = (
        P("fsdp", "seq", None),
        P("fsdp", "seq", None),
        P("fsdp"),
        P("fsdp"),
        P("fsdp", None),
        P("fsdp", None),
        P("fsdp", None),
        P("fsdp"),
        P("fsdp"),
        P("fsdp", None),
        P("fsdp"),
        P("fsdp"),
        P("fsdp"),
        P("fsdp", None),
        P("fsdp"),
        P("fsdp", None),
        P("fsdp"),
    )
    quick = mesh.shape["seq"] == 2 and mesh.shape["fsdp"] == 16
    return jax.shard_map(fast_body if quick else body, mesh=mesh, in_specs=in_specs, out_specs=out_specs, check_vma=False)
```

```python
import functools
import jax
import jax.numpy as jnp
from jax import lax
from jax.experimental import pallas as pl
from jax.experimental.pallas import tpu as pltpu
from jax.sharding import PartitionSpec as P

H = 16
QBLK = 512


norm_eps = 1e-06
root_half = 0.7071067811865476
inv_root_tau = 0.3989422804014327


def matmul(left, right):
    return jnp.dot(left, right, preferred_element_type=jnp.float32)


def matmul_nt(left, right):
    return lax.dot_general(
        left, right, (((1,), (1,)), ((), ())), preferred_element_type=jnp.float32
    )


def matmul_tn(left, right):
    return lax.dot_general(
        left, right, (((0,), (0,)), ((), ())), preferred_element_type=jnp.float32
    )


def layer_norm(values_in, gain, shift):
    row_mean = jnp.mean(values_in, axis=-1, keepdims=True)
    centred = values_in - row_mean
    inverse = lax.rsqrt(jnp.mean(centred * centred, axis=-1, keepdims=True) + norm_eps)
    scaled = centred * inverse
    return (scaled * gain + shift, scaled, inverse)


def layer_norm_back(upstream, scaled, inverse, gain):
    dscaled = upstream * gain
    inner = (
        dscaled
        - jnp.mean(dscaled, axis=-1, keepdims=True)
        - scaled * jnp.mean(dscaled * scaled, axis=-1, keepdims=True)
    )
    return (inverse * inner, jnp.sum(upstream * scaled, axis=0), jnp.sum(upstream, axis=0))


def gelu_value(pre_act):
    return 0.5 * pre_act * (1.0 + lax.erf(pre_act * root_half))


def gelu_slope(pre_act):
    return 0.5 * (1.0 + lax.erf(pre_act * root_half)) + pre_act * inv_root_tau * jnp.exp(
        -0.5 * pre_act * pre_act
    )


def attend(queries, keys_all, values_all, head_count):
    length = queries.shape[0]
    head_width = queries.shape[1] // head_count
    score_scale = head_width ** (-0.5)
    query_heads = queries.reshape(length // QBLK, QBLK, head_count, head_width)
    key_heads = keys_all.reshape(length, head_count, head_width)
    value_heads = values_all.reshape(length, head_count, head_width)

    def one_block(query_rows):
        scores = (
            jnp.einsum("qhd,khd->hqk", query_rows, key_heads, preferred_element_type=jnp.float32)
            * score_scale
        )
        peak = jnp.max(scores, axis=-1, keepdims=True)
        raised = jnp.exp(scores - peak)
        row_total = jnp.sum(raised, axis=-1, keepdims=True)
        weights = (raised / row_total).astype(jnp.bfloat16)
        mixed = jnp.einsum("hqk,khd->qhd", weights, value_heads, preferred_element_type=jnp.float32)
        return (mixed.astype(jnp.bfloat16), (peak + jnp.log(row_total))[:, :, 0])

    mixed, log_totals = lax.map(one_block, query_heads)
    return (mixed.reshape(length, head_count * head_width), log_totals)


def attend_back(queries, keys_all, values_all, log_totals, upstream, head_count):
    length = queries.shape[0]
    head_width = queries.shape[1] // head_count
    score_scale = head_width ** (-0.5)
    query_heads = queries.reshape(length // QBLK, QBLK, head_count, head_width)
    upstream_heads = upstream.reshape(length // QBLK, QBLK, head_count, head_width)
    key_heads = keys_all.reshape(length, head_count, head_width)
    value_heads = values_all.reshape(length, head_count, head_width)

    def one_block(running, block_item):
        key_grad, value_grad = running
        query_rows, log_rows, grad_rows = block_item
        scores = (
            jnp.einsum("qhd,khd->hqk", query_rows, key_heads, preferred_element_type=jnp.float32)
            * score_scale
        )
        weights = jnp.exp(scores - log_rows[:, :, None])
        weights_low = weights.astype(jnp.bfloat16)
        grad_weights = jnp.einsum(
            "qhd,khd->hqk", grad_rows, value_heads, preferred_element_type=jnp.float32
        )
        inner = jnp.sum(grad_weights * weights, axis=-1, keepdims=True)
        grad_scores = (weights * (grad_weights - inner)).astype(jnp.bfloat16)
        query_grad = (
            jnp.einsum("hqk,khd->qhd", grad_scores, key_heads, preferred_element_type=jnp.float32)
            * score_scale
        )
        key_grad = (
            key_grad
            + jnp.einsum(
                "hqk,qhd->khd", grad_scores, query_rows, preferred_element_type=jnp.float32
            )
            * score_scale
        )
        value_grad = value_grad + jnp.einsum(
            "hqk,qhd->khd", weights_low, grad_rows, preferred_element_type=jnp.float32
        )
        return ((key_grad, value_grad), query_grad.astype(jnp.bfloat16))

    zeros_heads = jnp.zeros((length, head_count, head_width), jnp.float32)
    (key_grad, value_grad), query_grad = lax.scan(
        one_block, (zeros_heads, zeros_heads), (query_heads, log_totals, upstream_heads)
    )
    width_all = head_count * head_width
    return (
        query_grad.reshape(length, width_all),
        key_grad.reshape(length, width_all).astype(jnp.bfloat16),
        value_grad.reshape(length, width_all).astype(jnp.bfloat16),
    )


def fetch(shards):
    return (
        lax.all_gather(shards[0], "fsdp", axis=0, tiled=True),
        lax.all_gather(shards[1], "fsdp", axis=0, tiled=True),
        lax.all_gather(shards[2], "fsdp", axis=0, tiled=True),
        lax.all_gather(shards[3], "fsdp", axis=0, tiled=True),
        lax.all_gather(shards[4], "fsdp", axis=0, tiled=True),
        lax.all_gather(shards[5], "fsdp", axis=0, tiled=True),
        lax.all_gather(shards[6], "fsdp", axis=0, tiled=True),
        lax.all_gather(shards[7], "fsdp", axis=0, tiled=True),
        lax.all_gather(shards[8], "fsdp", axis=0, tiled=True),
        lax.all_gather(shards[9], "fsdp", axis=0, tiled=True),
        lax.all_gather(shards[10], "fsdp", axis=0, tiled=True),
        lax.all_gather(shards[11], "fsdp", axis=0, tiled=True),
        lax.all_gather(shards[12], "fsdp", axis=0, tiled=True),
        lax.all_gather(shards[13], "fsdp", axis=0, tiled=True),
        lax.all_gather(shards[14], "fsdp", axis=0, tiled=True),
    )


def settle(grads):
    shares = (
        lax.psum_scatter(
            grads[0].astype(jnp.bfloat16), "fsdp", scatter_dimension=0, tiled=True
        ).astype(jnp.float32),
        lax.psum_scatter(
            grads[1].astype(jnp.bfloat16), "fsdp", scatter_dimension=0, tiled=True
        ).astype(jnp.float32),
        lax.psum_scatter(
            grads[2].astype(jnp.bfloat16), "fsdp", scatter_dimension=0, tiled=True
        ).astype(jnp.float32),
        lax.psum_scatter(
            grads[3].astype(jnp.bfloat16), "fsdp", scatter_dimension=0, tiled=True
        ).astype(jnp.float32),
        lax.psum_scatter(
            grads[4].astype(jnp.bfloat16), "fsdp", scatter_dimension=0, tiled=True
        ).astype(jnp.float32),
        lax.psum_scatter(
            grads[5].astype(jnp.bfloat16), "fsdp", scatter_dimension=0, tiled=True
        ).astype(jnp.float32),
        lax.psum_scatter(
            grads[6].astype(jnp.bfloat16), "fsdp", scatter_dimension=0, tiled=True
        ).astype(jnp.float32),
        lax.psum_scatter(
            grads[7].astype(jnp.bfloat16), "fsdp", scatter_dimension=0, tiled=True
        ).astype(jnp.float32),
        lax.psum_scatter(
            grads[8].astype(jnp.bfloat16), "fsdp", scatter_dimension=0, tiled=True
        ).astype(jnp.float32),
        lax.psum_scatter(
            grads[9].astype(jnp.bfloat16), "fsdp", scatter_dimension=0, tiled=True
        ).astype(jnp.float32),
        lax.psum_scatter(
            grads[10].astype(jnp.bfloat16), "fsdp", scatter_dimension=0, tiled=True
        ).astype(jnp.float32),
        lax.psum_scatter(
            grads[11].astype(jnp.bfloat16), "fsdp", scatter_dimension=0, tiled=True
        ).astype(jnp.float32),
        lax.psum_scatter(
            grads[12].astype(jnp.bfloat16), "fsdp", scatter_dimension=0, tiled=True
        ).astype(jnp.float32),
        lax.psum_scatter(
            grads[13].astype(jnp.bfloat16), "fsdp", scatter_dimension=0, tiled=True
        ).astype(jnp.float32),
        lax.psum_scatter(
            grads[14].astype(jnp.bfloat16), "fsdp", scatter_dimension=0, tiled=True
        ).astype(jnp.float32),
    )
    return (
        lax.psum(shares[0].astype(jnp.bfloat16), "seq").astype(jnp.float32),
        lax.psum(shares[1].astype(jnp.bfloat16), "seq").astype(jnp.float32),
        lax.psum(shares[2].astype(jnp.bfloat16), "seq").astype(jnp.float32),
        lax.psum(shares[3].astype(jnp.bfloat16), "seq").astype(jnp.float32),
        lax.psum(shares[4].astype(jnp.bfloat16), "seq").astype(jnp.float32),
        lax.psum(shares[5].astype(jnp.bfloat16), "seq").astype(jnp.float32),
        lax.psum(shares[6].astype(jnp.bfloat16), "seq").astype(jnp.float32),
        lax.psum(shares[7].astype(jnp.bfloat16), "seq").astype(jnp.float32),
        lax.psum(shares[8].astype(jnp.bfloat16), "seq").astype(jnp.float32),
        lax.psum(shares[9].astype(jnp.bfloat16), "seq").astype(jnp.float32),
        lax.psum(shares[10].astype(jnp.bfloat16), "seq").astype(jnp.float32),
        lax.psum(shares[11].astype(jnp.bfloat16), "seq").astype(jnp.float32),
        lax.psum(shares[12].astype(jnp.bfloat16), "seq").astype(jnp.float32),
        lax.psum(shares[13].astype(jnp.bfloat16), "seq").astype(jnp.float32),
        lax.psum(shares[14].astype(jnp.bfloat16), "seq").astype(jnp.float32),
    )


def one_clip(clip_in, clip_cot, clip_flag, gathered, head_count):
    (
        norm1_gain,
        norm1_bias,
        query_weight,
        key_weight,
        value_weight,
        query_bias,
        value_bias,
        proj_weight,
        proj_bias,
        norm2_gain,
        norm2_bias,
        fc1_weight,
        fc1_bias,
        fc2_weight,
        fc2_bias,
    ) = gathered
    gain_one = norm1_gain.astype(jnp.float32)
    gain_two = norm2_gain.astype(jnp.float32)
    tokens_in = clip_in.astype(jnp.float32)
    normed, scaled_one, inverse_one = layer_norm(
        tokens_in, gain_one, norm1_bias.astype(jnp.float32)
    )
    normed_low = normed.astype(jnp.bfloat16)
    queries = (matmul(normed_low, query_weight) + query_bias.astype(jnp.float32)).astype(
        jnp.bfloat16
    )
    keys_all = matmul(normed_low, key_weight).astype(jnp.bfloat16)
    values_all = (matmul(normed_low, value_weight) + value_bias.astype(jnp.float32)).astype(
        jnp.bfloat16
    )
    query_heads, key_heads, value_heads = (
        lax.all_to_all(queries, "seq", split_axis=1, concat_axis=0, tiled=True),
        lax.all_to_all(keys_all, "seq", split_axis=1, concat_axis=0, tiled=True),
        lax.all_to_all(values_all, "seq", split_axis=1, concat_axis=0, tiled=True),
    )
    mixed_heads, log_totals = attend(query_heads, key_heads, value_heads, head_count)
    attended = lax.all_to_all(mixed_heads, "seq", split_axis=0, concat_axis=1, tiled=True)
    middle = tokens_in + matmul(attended, proj_weight) + proj_bias.astype(jnp.float32)
    normed_two, scaled_two, inverse_two = layer_norm(
        middle, gain_two, norm2_bias.astype(jnp.float32)
    )
    normed_two_low = normed_two.astype(jnp.bfloat16)
    hidden_pre = matmul(normed_two_low, fc1_weight) + fc1_bias.astype(jnp.float32)
    hidden_low = gelu_value(hidden_pre).astype(jnp.bfloat16)
    output = middle + matmul(hidden_low, fc2_weight) + fc2_bias.astype(jnp.float32)
    grad_out = clip_cot.astype(jnp.float32) * clip_flag.astype(jnp.float32)
    grad_mlp = grad_out.astype(jnp.bfloat16)
    grad_fc2_weight = matmul_tn(hidden_low, grad_mlp)
    grad_fc2_bias = jnp.sum(grad_mlp.astype(jnp.float32), axis=0)
    grad_pre = (matmul_nt(grad_mlp, fc2_weight) * gelu_slope(hidden_pre)).astype(jnp.bfloat16)
    grad_fc1_weight = matmul_tn(normed_two_low, grad_pre)
    grad_fc1_bias = jnp.sum(grad_pre.astype(jnp.float32), axis=0)
    grad_norm_two = matmul_nt(grad_pre, fc1_weight)
    grad_ln_two, grad_norm2_gain, grad_norm2_bias = layer_norm_back(
        grad_norm_two, scaled_two, inverse_two, gain_two
    )
    grad_middle = grad_out + grad_ln_two
    grad_branch = grad_middle.astype(jnp.bfloat16)
    grad_proj_weight = matmul_tn(attended, grad_branch)
    grad_proj_bias = jnp.sum(grad_branch.astype(jnp.float32), axis=0)
    grad_att = matmul_nt(grad_branch, proj_weight).astype(jnp.bfloat16)
    grad_att_heads = lax.all_to_all(grad_att, "seq", split_axis=1, concat_axis=0, tiled=True)
    query_grad, key_grad, value_grad = attend_back(
        query_heads, key_heads, value_heads, log_totals, grad_att_heads, head_count
    )
    grad_queries, grad_keys, grad_values = (
        lax.all_to_all(query_grad, "seq", split_axis=0, concat_axis=1, tiled=True),
        lax.all_to_all(key_grad, "seq", split_axis=0, concat_axis=1, tiled=True),
        lax.all_to_all(value_grad, "seq", split_axis=0, concat_axis=1, tiled=True),
    )
    grad_query_weight = matmul_tn(normed_low, grad_queries)
    grad_key_weight = matmul_tn(normed_low, grad_keys)
    grad_value_weight = matmul_tn(normed_low, grad_values)
    grad_query_bias = jnp.sum(grad_queries.astype(jnp.float32), axis=0)
    grad_value_bias = jnp.sum(grad_values.astype(jnp.float32), axis=0)
    grad_norm_one = (
        matmul_nt(grad_queries, query_weight)
        + matmul_nt(grad_keys, key_weight)
        + matmul_nt(grad_values, value_weight)
    )
    grad_ln_one, grad_norm1_gain, grad_norm1_bias = layer_norm_back(
        grad_norm_one, scaled_one, inverse_one, gain_one
    )
    grad_in = grad_middle + grad_ln_one
    grads = (
        grad_norm1_gain,
        grad_norm1_bias,
        grad_query_weight,
        grad_key_weight,
        grad_value_weight,
        grad_query_bias,
        grad_value_bias,
        grad_proj_weight,
        grad_proj_bias,
        grad_norm2_gain,
        grad_norm2_bias,
        grad_fc1_weight,
        grad_fc1_bias,
        grad_fc2_weight,
        grad_fc2_bias,
    )
    return (output.astype(jnp.bfloat16), grad_in, grads)


def body(
    clips,
    cotangent,
    valid,
    norm1_gain,
    norm1_bias,
    query_weight,
    key_weight,
    value_weight,
    query_bias,
    value_bias,
    proj_weight,
    proj_bias,
    norm2_gain,
    norm2_bias,
    fc1_weight,
    fc1_bias,
    fc2_weight,
    fc2_bias,
):
    shards = (
        norm1_gain,
        norm1_bias,
        query_weight,
        key_weight,
        value_weight,
        query_bias,
        value_bias,
        proj_weight,
        proj_bias,
        norm2_gain,
        norm2_bias,
        fc1_weight,
        fc1_bias,
        fc2_weight,
        fc2_bias,
    )
    slot_count = clips.shape[0]
    head_count = H // lax.axis_size("seq")
    summed = None
    outputs = []
    grad_list = []
    for batch_slot in range(slot_count):
        gathered = fetch(shards)
        output, grad_in, grads = one_clip(
            clips[batch_slot], cotangent[batch_slot], valid[batch_slot], gathered, head_count
        )
        summed = (
            grads
            if summed is None
            else tuple((older + newer for older, newer in zip(summed, grads)))
        )
        outputs.append(output)
        grad_list.append(grad_in)
    summed = settle(summed)
    return (
        jnp.stack(outputs),
        jnp.stack(grad_list),
        summed[0],
        summed[1],
        summed[2],
        summed[3],
        summed[4],
        summed[5],
        summed[6],
        summed[7],
        summed[8],
        summed[9],
        summed[10],
        summed[11],
        summed[12],
        summed[13],
        summed[14],
    )


T, D, FF, NTILE = 1024, 1024, 4096, 8

log2_e = 1.4426950408889634
HD = 64
F32, BF16 = jnp.float32, jnp.bfloat16
ANY = pl.BlockSpec(memory_space=pl.ANY)


def dot(left, right, cl=1, cr=0):
    return lax.dot_general(left, right, (((cl,), (cr,)), ((), ())), preferred_element_type=F32)


def split3(v):
    hi = v.astype(BF16)
    r = v - hi.astype(F32)
    md = r.astype(BF16)
    lo = (r - md.astype(F32)).astype(BF16)
    return hi, md, lo


def aug_rows(v):
    hi, md, lo = split3(v)
    z = jnp.zeros((13, v.shape[1]), BF16)
    return jnp.concatenate([hi, md, lo, z], axis=0)


def bwd_mlp(g, n2, gacc, h, gp, w1t, w2t, sg_v, j, t, col_slot, put_w2, put_w1):
    gb = g[...]
    put_w2(dot(h[col_slot], gb, 0, 0).astype(BF16))
    pre = (dot(gb, w2t[col_slot], 1, 1) * gp[col_slot].astype(F32)).astype(BF16)
    gp[col_slot] = pre
    sg_v[pl.ds(t, 1), :] = jnp.sum(pre.astype(F32), axis=0, keepdims=True)
    put_w1(dot(n2[...], pre, 0, 0).astype(BF16))
    v = dot(pre, w1t[col_slot], 1, 1)

    @pl.when(j == 0)
    def _():
        gacc[...] = v

    @pl.when(j > 0)
    def _():
        gacc[...] += v


def ln_back(up, v, gain):
    m = jnp.mean(v, axis=-1, keepdims=True)
    d = v - m
    r = lax.rsqrt(jnp.mean(d * d, axis=-1, keepdims=True) + norm_eps)
    xh = d * r
    s = up * gain
    back = r * (s - jnp.mean(s, axis=-1, keepdims=True) - xh * jnp.mean(s * xh, axis=-1, keepdims=True))
    return back, jnp.sum(up * xh, axis=0, keepdims=True), jnp.sum(up, axis=0, keepdims=True)


def bwd_head(h, qkvt, ot, dot_v, lse_v):
    T = ot.shape[1]
    qb = T // 2
    scale = HD ** -0.5
    r = pl.multiple_of(h * HD, HD)
    rows = pl.ds(r, HD)
    ones = jnp.ones((16, T), BF16)
    kh = qkvt[1, rows, :]
    ka = jnp.concatenate([kh, ones], axis=0)
    va = jnp.concatenate([qkvt[2, rows, :], ones], axis=0)
    dk = dv = None
    for b in range(2):
        cols = slice(b * qb, (b + 1) * qb)
        qh = qkvt[0, rows, cols] * jnp.asarray(scale, BF16)
        do = dot_v[rows, cols]
        delta = jnp.sum(do.astype(F32) * ot[rows, cols].astype(F32), axis=0, keepdims=True)
        qa = jnp.concatenate([qh, aug_rows(-lse_v[pl.ds(h, 1), cols])], axis=0)
        da = jnp.concatenate([do, aug_rows(-delta)], axis=0)
        p = jnp.exp2(dot(qa, ka, 0, 0) * log2_e)
        ds = (p * dot(da, va, 0, 0)).astype(BF16)
        ndv = dot(do, p.astype(BF16))
        ndk = dot(qh, ds)
        dv = ndv if dv is None else dv + ndv
        dk = ndk if dk is None else dk + ndk
        qkvt[0, rows, cols] = (dot(kh, ds, 1, 1) * scale).astype(BF16)
    qkvt[1, rows, :] = dk.astype(BF16)
    qkvt[2, rows, :] = dv.astype(BF16)


MESH = pl.DeviceIdType.MESH


class Place:
    def __init__(self, size):
        f = lax.axis_index("fsdp")
        self.f, self.core, chip = f, f % 2, f // 2
        self.deep, self.count = size // 4, size // 2
        x, z = chip % 2, chip // 2
        self.pos = z + x * (2 * self.deep - 1 - 2 * z)
        self.mate = f + 1 - 2 * self.core
        self.y = lax.axis_index("seq")

    def chip(self, off):
        pos = (self.pos + self.count + off) % self.count
        hi = pos // self.deep
        return 2 * (pos + hi * (2 * self.deep - 1 - 2 * pos)) + hi

    def side(self, d):
        return {"fsdp": 2 * self.chip((1, -1)[d]) + self.core}

    def partner(self):
        return {"fsdp": self.mate}

    def across(self):
        return {"seq": 1 - self.y}

    def barrier(self):
        sem = pltpu.get_barrier_semaphore()
        for dev in (self.side(0), self.side(1), self.partner(), self.across()):
            pl.semaphore_signal(sem, inc=1, device_id=dev, device_id_type=MESH)
        pl.semaphore_wait(sem, 4)


def remote(src, dst, ss, rs, dev):
    return pltpu.make_async_remote_copy(src_ref=src, dst_ref=dst, send_sem=ss, recv_sem=rs, device_id=dev, device_id_type=MESH)


class Gather:
    def __init__(self, place, view, rsem, psem):
        self.pl, self.view, self.rsem, self.psem = place, view, rsem, psem
        self.last = place.count // 2 - 1

    def part(self, d, s):
        return d if s == self.last else 2

    def block(self, d, s, ahead):
        k = s + ahead
        return self.pl.chip(-k if d == 0 else k)

    def ring(self, d, s, ahead=0):
        v = self.view(2 * self.block(d, s, ahead) + self.pl.core, self.part(d, s))
        return remote(v, v, self.rsem.at[0, d, s], self.rsem.at[1, d, s], self.pl.side(d))

    def mate(self, slot, chip, part, core):
        v = self.view(2 * chip + core, part)
        return remote(v, v, self.psem.at[0, slot], self.psem.at[1, slot], self.pl.partner())

    def slots(self, s):
        return [(1 + 2 * s + d, self.block(d, s, 1), self.part(d, s)) for d in range(2)]

    def start(self):
        for d in range(2):
            self.ring(d, 0).start()
        self.mate(0, self.pl.chip(0), 2, self.pl.core).start()

    def step(self, s):
        for d in range(2):
            self.ring(d, s, 1).wait_recv()
            if s < self.last:
                self.ring(d, s + 1).start()
        for slot, chip, part in self.slots(s):
            self.mate(slot, chip, part, self.pl.core).start()

    def own_mate(self):
        self.mate(0, self.pl.chip(0), 2, 1 - self.pl.core).wait_recv()

    def step_mate(self, s):
        for slot, chip, part in self.slots(s):
            self.mate(slot, chip, part, 1 - self.pl.core).wait_recv()

    def all_mates(self):
        self.own_mate()
        for s in range(self.last + 1):
            self.step_mate(s)

    def drain(self):
        for s in range(self.last + 1):
            for d in range(2):
                self.ring(d, s).wait_send()
            for slot, chip, part in self.slots(s):
                self.mate(slot, chip, part, self.pl.core).wait_send()
        self.mate(0, self.pl.chip(0), 2, self.pl.core).wait_send()


def fwd_body(size, clips, cot, sml, wq, wk, wv, wp, w1, w2,
             out_o, cot_o, x_o, sm_o, wqkv_o, wp_o, w1_o, w2_o, n1t_o, qkvt_o, ot_o, lse_o, mid_o, n2_o, h_o, g_o,
             x_v, smb, sm_v, wqkv_v, wp_v, w1_v, w2_v, n1t, qkvt, ot, lse_v, mid, n2, acc, hst, gst, b1_v, smt,
             rsem, psem, xsem, lsem, osem, tsem):
    here = Place(size)
    T, D = x_v.shape
    FF = w1_v.shape[1]
    tile = hst.shape[2]
    heads = D // HD
    half = T // 2
    nd, nf = D // size, FF // size
    y = here.y
    ymine = pl.ds(pl.multiple_of(y * half, half), half)
    yother = pl.ds(pl.multiple_of((1 - y) * half, half), half)

    def local(a, b, i):
        return pltpu.make_async_copy(a, b, lsem.at[i])

    def rows(ref, n, lead):
        def view(f, part):
            k = n if part == 2 else n // 2
            at = pl.ds(pl.multiple_of(f * n + (n // 2 if part == 1 else 0), k), k)
            return ref.at[:, at, :] if lead else ref.at[at, :]
        return view

    def smview(f, part):
        if part == 2:
            return smb.at[f]
        return smb.at[f, :, part * (D // 2):(part + 1) * (D // 2)]

    views = [smview, rows(wqkv_v, nd, True), rows(wp_v, nd, False), rows(w1_v, nd, False), rows(w2_v, nf, False)]
    ga, gq, gp, g1, g2 = [Gather(here, v, rsem.at[i], psem.at[i]) for i, v in enumerate(views)]
    own = pl.ds(pl.multiple_of(here.f * nd, nd), nd)
    ownf = pl.ds(pl.multiple_of(here.f * nf, nf), nf)
    loc = [local(sml, smb.at[here.f], 0)]
    loc += [local(w, wqkv_v.at[j, own, :], 1 + j) for j, w in enumerate((wq, wk, wv))]
    loc += [local(wp, wp_v.at[own, :], 4), local(w1, w1_v.at[own, :], 5), local(w2, w2_v.at[ownf, :], 6), local(clips.at[y], x_v.at[ymine, :], 7)]
    for c in loc:
        c.start()
    here.barrier()
    xsend = remote(clips.at[1 - y], x_v.at[ymine, :], xsem.at[0, 0], xsem.at[0, 1], here.across())
    xrecv = remote(clips.at[1 - y], x_v.at[yother, :], xsem.at[0, 0], xsem.at[0, 1], here.across())
    csend = remote(cot.at[1 - y], cot_o, xsem.at[1, 0], xsem.at[1, 1], here.across())
    xsend.start()
    csend.start()
    for c in loc[:4]:
        c.wait()
    ga.start()
    gq.start()
    for c in loc[4:]:
        c.wait()

    def ln1(i, c):
        r = pl.multiple_of(i * 256, 256)
        v = x_v[pl.ds(r, 256), :].astype(F32)
        m = jnp.mean(v, axis=-1, keepdims=True)
        d = v - m
        mid[pl.ds(r, 256), :] = d * lax.rsqrt(jnp.mean(d * d, axis=-1, keepdims=True) + norm_eps)
        return c

    per = half // 256
    lax.fori_loop(y * per, y * per + per, ln1, 0)
    for s in range(ga.last + 1):
        ga.step(s)
        gq.step(s)
        if s == ga.last - 1:
            gp.start()
            g1.start()
    xrecv.wait_recv()
    lax.fori_loop((1 - y) * per, (1 - y) * per + per, ln1, 0)
    ga.all_mates()
    sm_v[...] = jnp.sum(smb[...].astype(F32), axis=0)
    smt[...] = jnp.transpose(sm_v[...])

    def ln1b(i, c):
        r = pl.multiple_of(i * 256, 256)
        n1t[:, pl.ds(r, 256)] = jnp.transpose((mid[pl.ds(r, 256), :] * sm_v[0:1, :] + sm_v[1:2, :]).astype(BF16))
        return c

    lax.fori_loop(0, T // 256, ln1b, 0)
    gq.all_mates()
    outs = []

    def save(a, b):
        c = pltpu.make_async_copy(a, b, osem.at[len(outs)])
        outs.append(c)
        c.start()

    save(wqkv_v, wqkv_o)
    save(x_v, x_o)
    save(sm_v, sm_o)
    save(n1t, n1t_o)
    hd = D // 2
    for j in range(3):
        for o in range(2):
            v = dot(wqkv_v[j, :, o * hd:(o + 1) * hd], n1t[...], 0, 0)
            if j != 1:
                v = v + smt[o * hd:(o + 1) * hd, (2 if j == 0 else 3):(3 if j == 0 else 4)]
            qkvt[j, o * hd:(o + 1) * hd, :] = v.astype(BF16)
    save(qkvt, qkvt_o)
    qb = T // 2
    ones = jnp.ones((16, T), BF16)

    def head(h, c):
        r = pl.multiple_of(h * HD, HD)
        kh = qkvt[1, pl.ds(r, HD), :]
        vh = jnp.concatenate([qkvt[2, pl.ds(r, HD), :], ones], axis=0)
        for b in range(2):
            qh = qkvt[0, pl.ds(r, HD), b * qb:(b + 1) * qb]
            s = dot(kh, qh, 0, 0)
            m = jnp.max(s, axis=0, keepdims=True)
            p = jnp.exp2((s - m) * (log2_e * HD ** -0.5)).astype(BF16)
            o = dot(vh, p)
            total = o[HD:HD + 1, :]
            ot[pl.ds(r, HD), b * qb:(b + 1) * qb] = (o[:HD, :] / total).astype(BF16)
            lse_v[pl.ds(h, 1), b * qb:(b + 1) * qb] = m * HD ** -0.5 + jnp.log(total)
        return c

    cuts = (0, 3 * heads // 16, 10 * heads // 16, heads)
    for s in range(3):
        lax.fori_loop(cuts[s], cuts[s + 1], head, 0)
        gp.step(s)
        g1.step(s)
        if s == 1:
            g2.start()
    save(ot, ot_o)
    save(lse_v, lse_o)
    for s in range(3, gp.last + 1):
        gp.step(s)
    gp.all_mates()
    save(wp_v, wp_o)

    def proj(i, c):
        r = pl.multiple_of(i * 512, 512)
        v = dot(ot[:, pl.ds(r, 512)], wp_v[...], 0, 0) + x_v[pl.ds(r, 512), :].astype(F32) + sm_v[4:5, :]
        mid[pl.ds(r, 512), :] = v
        m = jnp.mean(v, axis=-1, keepdims=True)
        d = v - m
        s = d * lax.rsqrt(jnp.mean(d * d, axis=-1, keepdims=True) + norm_eps)
        n2[pl.ds(r, 512), :] = (s * sm_v[5:6, :] + sm_v[6:7, :]).astype(BF16)
        acc[pl.ds(r, 512), :] = v + sm_v[7:8, :]
        return c

    lax.fori_loop(0, T // 512, proj, 0)
    save(mid, mid_o)
    save(n2, n2_o)
    for k in range(FF // tile):
        kk = k * tile
        b1_v[k:k + 1, :] = sm_v[8 + kk // D:9 + kk // D, kk % D:kk % D + tile]
    for s in range(3, g1.last + 1):
        g1.step(s)
    g2.step(0)
    g1.all_mates()
    g2.own_mate()
    g2.step_mate(0)
    save(w1_v, w1_o)
    saves = {}
    order = [0]
    for k in range(1, here.count // 2):
        order += [-k, k]
    order.append(here.count // 2)

    def tcp(k, slot, t):
        return pltpu.make_async_copy((hst, gst)[k].at[slot], (h_o, g_o)[k].at[t], tsem.at[k, slot])

    def wcp(j, t):
        at = pl.ds(pl.multiple_of(t * tile, tile), tile)
        return pltpu.make_async_copy(w2_v.at[at, :], w2_o.at[at, :], tsem.at[2, j])

    for j, off in enumerate(order):
        t = here.chip(off)
        slot = j % 2
        if j >= 3 and j % 2 == 1:
            g2.step(j // 2)
            g2.step_mate(j // 2)
        wcp(j, t).start()
        if j >= 2:
            for k in range(2):
                tcp(k, slot, here.chip(order[j - 2])).wait()
        col = pl.multiple_of(t * tile, tile)

        def mlp(i, c, t=t, slot=slot, col=col):
            r = pl.multiple_of(i * 512, 512)
            u = dot(n2[pl.ds(r, 512), :], w1_v[:, pl.ds(col, tile)]) + b1_v[pl.ds(t, 1), :]
            cdf = 0.5 + 0.5 * lax.erf(u * root_half)
            hb = (u * cdf).astype(BF16)
            hst[slot, pl.ds(r, 512), :] = hb
            gst[slot, pl.ds(r, 512), :] = (cdf + (u * inv_root_tau) * jnp.exp2(u * u * (-0.5 * log2_e))).astype(BF16)
            acc[pl.ds(r, 512), :] += dot(hb, w2_v[pl.ds(col, tile), :])
            return c

        lax.fori_loop(0, T // 512, mlp, 0)
        for k in range(2):
            tcp(k, slot, t).start()
    for j in range(len(order) - 2, len(order)):
        for k in range(2):
            tcp(k, j % 2, here.chip(order[j])).wait()
    outs[3].wait()
    n1t[...] = acc[...].astype(BF16)
    save(n1t, out_o)
    for j, off in enumerate(order):
        wcp(j, here.chip(off)).wait()
    for i, c in enumerate(outs):
        if i != 3:
            c.wait()
    for g in (ga, gq, gp, g1, g2):
        g.drain()
    xsend.wait_send()
    csend.wait_send()
    remote(cot.at[1 - y], cot_o, xsem.at[1, 0], xsem.at[1, 1], here.across()).wait_recv()


S = jax.ShapeDtypeStruct
V = pltpu.VMEM


def fwd_call(size, T, D, FF):
    tile = 2 * FF // size
    heads = D // HD
    small = (16, D)
    dma = pltpu.SemaphoreType.DMA
    steps = size // 4
    return pl.pallas_call(
        functools.partial(fwd_body, size),
        name="forward",
        in_specs=[ANY] * 9,
        out_specs=[ANY] * 16,
        out_shape=[S((T, D), BF16), S((T // 2, D), BF16), S((T, D), BF16), S(small, F32), S((3, D, D), BF16), S((D, D), BF16), S((D, FF), BF16), S((FF, D), BF16),
                   S((D, T), BF16), S((3, D, T), BF16), S((D, T), BF16), S((heads, T), F32), S((T, D), F32), S((T, D), BF16), S((FF // tile, T, tile), BF16), S((FF // tile, T, tile), BF16)],
        scratch_shapes=[V((T, D), BF16), V((size,) + small, BF16), V(small, F32), V((3, D, D), BF16), V((D, D), BF16), V((D, FF), BF16), V((FF, D), BF16),
                        V((D, T), BF16), V((3, D, T), BF16), V((D, T), BF16), V((heads, T), F32), V((T, D), F32), V((T, D), BF16), V((T, D), F32),
                        V((2, T, tile), BF16), V((2, T, tile), BF16), V((FF // tile, tile), F32), V((D, 16), F32),
                        dma((5, 2, 2, steps)), dma((5, 2, 2 * steps + 1)), dma((2, 2)), dma((8,)), dma((12,)), dma((3, max(2, FF // tile)))],
        compiler_params=pltpu.CompilerParams(vmem_limit_bytes=63 << 20, collective_id=0, has_side_effects=True),
    )


def bwd_kernel(cot,x,sm,wqkv,wp,w1,w2,n1t,qkvt,ot,lse,mid,n2,hs,gs, gx,dqkv,dwp,dw1,dw2,sg,
  g_v,n2_v,gacc,h_v,gp_v,w1_v,w2_v,b1g,mid_v,qkvt_v,ot_v,do_v,lse_v,n1t_v,x_v,sm_v,sg_v,st_v,gx_v,sem,tsem,osem,msem,xsem):
    def cp(a,b,i):
        return pltpu.make_async_copy(a,b,sem.at[i])
    first=[cp(cot,g_v,0),cp(n2,n2_v,1),cp(sm,sm_v,2)]
    later=[cp(qkvt,qkvt_v,3),cp(ot,ot_v,4),cp(lse,lse_v,5),cp(n1t,n1t_v,6),cp(x,x_v,7)]
    def tl(t,s):
        c=pl.multiple_of(t*512,512)
        return [pltpu.make_async_copy(hs.at[t],h_v.at[s],tsem.at[s,0]),pltpu.make_async_copy(gs.at[t],gp_v.at[s],tsem.at[s,1]),
          pltpu.make_async_copy(w1.at[:,pl.ds(c,512)],w1_v.at[s],tsem.at[s,2]),pltpu.make_async_copy(w2.at[pl.ds(c,512),:],w2_v.at[s],tsem.at[s,3])]
    for c in first: c.start()
    for c in tl(0,0): c.start()
    for c in later: c.start()
    for c in first: c.wait()
    sg_v[...]=jnp.zeros_like(sg_v)
    sg_v[7:8,:]=jnp.sum(g_v[...].astype(F32),axis=0,keepdims=True)
    def wcp(k,t):
        c=pl.multiple_of(t*512,512)
        return pltpu.make_async_copy(st_v.at[k],dw2.at[pl.ds(c,512),:],osem.at[k]) if k==0 else pltpu.make_async_copy(st_v.at[k].reshape(1024,512) if False else n_st(k),dw1.at[:,pl.ds(c,512)],osem.at[k])
    def n_st(k): return st1_v
    st1_v=gx_v
    def tile(j,c):
        s=j%2
        @pl.when(j+1<NTILE)
        def _():
            for c_ in tl(j+1,1-s): c_.start()
        for c_ in tl(j,s): c_.wait()
        def p2(v):
            @pl.when(j>0)
            def _(): wcp(0,j-1).wait()
            st_v[0]=v; wcp(0,j).start()
        def p1(v):
            @pl.when(j>0)
            def _(): wcp(1,j-1).wait()
            st1_v[...]=v; wcp(1,j).start()
        bwd_mlp(g_v,n2_v,gacc,h_v,gp_v,w1_v,w2_v,b1g,j,j,s,p2,p1)
        return c
    lax.fori_loop(0,NTILE,tile,0)
    wcp(0,NTILE-1).wait(); wcp(1,NTILE-1).wait()
    for k in range(NTILE):
        kk=k*512
        sg_v[8+kk//D:9+kk//D,kk%D:kk%D+512]=b1g[k:k+1,:]
    wpl=[pltpu.make_async_copy(wp.at[i*512:(i+1)*512,:],w2_v.at[i],tsem.at[i,3]) for i in range(2)]
    for c in wpl: c.start()
    wl=[]
    for j in range(3):
        for i in range(2):
            wl.append(pltpu.make_async_copy(wqkv.at[j,:,i*512:(i+1)*512],(h_v,gp_v,w1_v)[j].at[i],tsem.at[i,j]))
    for c in wl: c.start()
    def ml(i,s): return pltpu.make_async_copy(mid.at[pl.ds(pl.multiple_of(i*256,256),256),:],mid_v.at[s],msem.at[s])
    ml(0,0).start()
    def ln2(i,c):
        r=pl.multiple_of(i*256,256); s=i%2
        @pl.when(i<3)
        def _(): ml(i+1,1-s).start()
        ml(i,s).wait()
        back,dg,db=ln_back(gacc[pl.ds(r,256),:],mid_v[s],sm_v[5:6,:])
        gm=g_v[pl.ds(r,256),:].astype(F32)+back
        gacc[pl.ds(r,256),:]=gm
        gb=gm.astype(BF16)
        g_v[pl.ds(r,256),:]=gb
        sg_v[5:6,:]+=dg; sg_v[6:7,:]+=db; sg_v[4:5,:]+=jnp.sum(gb.astype(F32),axis=0,keepdims=True)
        return c
    lax.fori_loop(0,4,ln2,0)
    for c in later: c.wait()
    for c in wpl: c.wait()
    for i in range(2):
        st_v[i]=dot(ot_v[i*512:(i+1)*512,:],g_v[...]).astype(BF16)
        do_v[i*512:(i+1)*512,:]=dot(w2_v[i],g_v[...],1,1).astype(BF16)
    op=[pltpu.make_async_copy(st_v.at[i],dwp.at[i*512:(i+1)*512,:],osem.at[i]) for i in range(2)]
    for c in op: c.start()
    def hd(h,c):
        bwd_head(h,qkvt_v,ot_v,do_v,lse_v)
        return c
    lax.fori_loop(0,16,hd,0)
    for c in op: c.wait()
    for c in wl: c.wait()
    ones=jnp.ones((16,T),BF16)
    for j in (0,2):
        sg_v[(2,None,3)[j]:(3,None,4)[j],:]=dot(ones,qkvt_v[j],1,1)[0:1,:]
    def ocp(j,i): return pltpu.make_async_copy(st_v.at[i],dqkv.at[j,i*512:(i+1)*512,:],osem.at[i])
    for j in range(3):
        for i in range(2):
            if j>0: ocp(j-1,i).wait()
            st_v[i]=dot(n1t_v[i*512:(i+1)*512,:],qkvt_v[j],1,1).astype(BF16)
            ocp(j,i).start()
    for i in range(2): ocp(2,i).wait()
    def xcp(i,s): return pltpu.make_async_copy(mid_v.at[s],gx.at[pl.ds(pl.multiple_of(i*256,256),256),:],xsem.at[s])
    def fin(i,c):
        r=pl.multiple_of(i*256,256); s=i%2
        up=None
        for j,b in enumerate((h_v,gp_v,w1_v)):
            for k in range(2):
                v=dot(qkvt_v[j,k*512:(k+1)*512,pl.ds(r,256)],b[k],0,1)
                up=v if up is None else up+v
        back,dg,db=ln_back(up,x_v[pl.ds(r,256),:].astype(F32),sm_v[0:1,:])
        @pl.when(i>=2)
        def _(): xcp(i-2,s).wait()
        mid_v[s]=gacc[pl.ds(r,256),:]+back
        xcp(i,s).start()
        sg_v[0:1,:]+=dg; sg_v[1:2,:]+=db
        return c
    lax.fori_loop(0,4,fin,0)
    xcp(2,0).wait(); xcp(3,1).wait()
    c=pltpu.make_async_copy(sg_v,sg,sem.at[0]); c.start(); c.wait()


def bwd_call():
    return pl.pallas_call(bwd_kernel,name="k2",in_specs=[ANY]*15,out_specs=[ANY]*6,
     out_shape=[S((T,D),F32),S((3,D,D),BF16),S((D,D),BF16),S((D,FF),BF16),S((FF,D),BF16),S((16,D),F32)],
     scratch_shapes=[V((T,D),BF16),V((T,D),BF16),V((T,D),F32),V((2,T,512),BF16),V((2,T,512),BF16),V((2,D,512),BF16),V((2,512,D),BF16),V((8,512),F32),V((2,256,D),F32),
      V((3,D,T),BF16),V((D,T),BF16),V((D,T),BF16),V((16,T),F32),V((D,T),BF16),V((T,D),BF16),V((16,D),F32),V((16,D),F32),V((2,512,D),BF16),V((D,512),BF16),
      pltpu.SemaphoreType.DMA((8,)),pltpu.SemaphoreType.DMA((2,4)),pltpu.SemaphoreType.DMA((2,)),pltpu.SemaphoreType.DMA((2,)),pltpu.SemaphoreType.DMA((2,))],
     compiler_params=pltpu.CompilerParams(vmem_limit_bytes=63<<20))


def fast_body(clips, cotangent, valid, *shards):
    size = lax.axis_size("fsdp")
    me = lax.axis_index("fsdp")
    mine = lax.axis_index("seq")
    (g1, b1, wq, wk, wv, bq, bv, wp, bp, g2, b2, w1, fb1, w2, fb2) = shards
    n, m = g1.shape[0], fb1.shape[0]
    vecs = jnp.stack([g1, b1, bq, bv, bp, g2, b2, fb2])
    sml = lax.dynamic_update_slice(jnp.zeros((8, D), vecs.dtype), vecs, (0, me * n))
    fsm = lax.dynamic_update_slice(jnp.zeros((FF,), vecs.dtype), fb1, (me * m,)).reshape(-1, D)
    sml = jnp.concatenate([sml, fsm, jnp.zeros((8 - FF // D, D), vecs.dtype)])
    out, cot_in, x, sm, wqkv, wp_all, w1_all, w2_all, *saved = fwd_call(size, T, D, FF)(clips, cotangent, sml, wq, wk, wv, wp, w1, w2)
    both = jnp.concatenate([cotangent[mine], cot_in])
    cot = jnp.where(mine == 0, both, jnp.roll(both, T // 2, axis=0)) * valid[mine].astype(jnp.bfloat16)
    gx, dqkv, dwp, dw1, dw2, sg = bwd_call()(cot, x, sm, wqkv, wp_all, w1_all, w2_all, *saved)
    back = lambda v: lax.all_to_all(v[None], "seq", split_axis=1, concat_axis=0, tiled=True)

    def total(v, axis=0):
        part = lax.psum_scatter(v, "fsdp", scatter_dimension=axis, tiled=True)
        return lax.psum(part, "seq").astype(jnp.float32)

    dw2, dw1, dqkv, dwp = total(dw2), total(dw1), total(dqkv, 1), total(dwp)
    sg = lax.psum(sg, ("fsdp", "seq"))
    own = lax.dynamic_slice(sg[:8], (0, me * n), (8, n))
    m = fb1.shape[0]
    dfb1 = lax.dynamic_slice(sg[8:12].reshape(-1), (me * m,), (m,))
    gx = back(gx.astype(jnp.bfloat16)).astype(jnp.float32)
    return (back(out), gx, own[0], own[1], dqkv[0], dqkv[1], dqkv[2], own[2], own[3], dwp, own[4], own[5], own[6], dw1, dfb1, dw2, own[7])


def solution(mesh):
    in_specs = (
        P("fsdp", "seq", None),
        P("fsdp", "seq", None),
        P("fsdp"),
        P("fsdp"),
        P("fsdp"),
        P("fsdp", None),
        P("fsdp", None),
        P("fsdp", None),
        P("fsdp"),
        P("fsdp"),
        P("fsdp", None),
        P("fsdp"),
        P("fsdp"),
        P("fsdp"),
        P("fsdp", None),
        P("fsdp"),
        P("fsdp", None),
        P("fsdp"),
    )
    out_specs = (
        P("fsdp", "seq", None),
        P("fsdp", "seq", None),
        P("fsdp"),
        P("fsdp"),
        P("fsdp", None),
        P("fsdp", None),
        P("fsdp", None),
        P("fsdp"),
        P("fsdp"),
        P("fsdp", None),
        P("fsdp"),
        P("fsdp"),
        P("fsdp"),
        P("fsdp", None),
        P("fsdp"),
        P("fsdp", None),
        P("fsdp"),
    )
    quick = mesh.shape["seq"] == 2 and mesh.shape["fsdp"] == 16
    return jax.shard_map(fast_body if quick else body, mesh=mesh, in_specs=in_specs, out_specs=out_specs, check_vma=False)
```

```python
import functools
import jax
import jax.numpy as jnp
from jax import lax
from jax.experimental import pallas as pl
from jax.experimental.pallas import tpu as pltpu
from jax.sharding import PartitionSpec as P

H = 16
QBLK = 512


norm_eps = 1e-06
root_half = 0.7071067811865476
inv_root_tau = 0.3989422804014327


def matmul(left, right):
    return jnp.dot(left, right, preferred_element_type=jnp.float32)


def matmul_nt(left, right):
    return lax.dot_general(
        left, right, (((1,), (1,)), ((), ())), preferred_element_type=jnp.float32
    )


def matmul_tn(left, right):
    return lax.dot_general(
        left, right, (((0,), (0,)), ((), ())), preferred_element_type=jnp.float32
    )


def layer_norm(values_in, gain, shift):
    row_mean = jnp.mean(values_in, axis=-1, keepdims=True)
    centred = values_in - row_mean
    inverse = lax.rsqrt(jnp.mean(centred * centred, axis=-1, keepdims=True) + norm_eps)
    scaled = centred * inverse
    return (scaled * gain + shift, scaled, inverse)


def layer_norm_back(upstream, scaled, inverse, gain):
    dscaled = upstream * gain
    inner = (
        dscaled
        - jnp.mean(dscaled, axis=-1, keepdims=True)
        - scaled * jnp.mean(dscaled * scaled, axis=-1, keepdims=True)
    )
    return (inverse * inner, jnp.sum(upstream * scaled, axis=0), jnp.sum(upstream, axis=0))


def gelu_value(pre_act):
    return 0.5 * pre_act * (1.0 + lax.erf(pre_act * root_half))


def gelu_slope(pre_act):
    return 0.5 * (1.0 + lax.erf(pre_act * root_half)) + pre_act * inv_root_tau * jnp.exp(
        -0.5 * pre_act * pre_act
    )


def attend(queries, keys_all, values_all, head_count):
    length = queries.shape[0]
    head_width = queries.shape[1] // head_count
    score_scale = head_width ** (-0.5)
    query_heads = queries.reshape(length // QBLK, QBLK, head_count, head_width)
    key_heads = keys_all.reshape(length, head_count, head_width)
    value_heads = values_all.reshape(length, head_count, head_width)

    def one_block(query_rows):
        scores = (
            jnp.einsum("qhd,khd->hqk", query_rows, key_heads, preferred_element_type=jnp.float32)
            * score_scale
        )
        peak = jnp.max(scores, axis=-1, keepdims=True)
        raised = jnp.exp(scores - peak)
        row_total = jnp.sum(raised, axis=-1, keepdims=True)
        weights = (raised / row_total).astype(jnp.bfloat16)
        mixed = jnp.einsum("hqk,khd->qhd", weights, value_heads, preferred_element_type=jnp.float32)
        return (mixed.astype(jnp.bfloat16), (peak + jnp.log(row_total))[:, :, 0])

    mixed, log_totals = lax.map(one_block, query_heads)
    return (mixed.reshape(length, head_count * head_width), log_totals)


def attend_back(queries, keys_all, values_all, log_totals, upstream, head_count):
    length = queries.shape[0]
    head_width = queries.shape[1] // head_count
    score_scale = head_width ** (-0.5)
    query_heads = queries.reshape(length // QBLK, QBLK, head_count, head_width)
    upstream_heads = upstream.reshape(length // QBLK, QBLK, head_count, head_width)
    key_heads = keys_all.reshape(length, head_count, head_width)
    value_heads = values_all.reshape(length, head_count, head_width)

    def one_block(running, block_item):
        key_grad, value_grad = running
        query_rows, log_rows, grad_rows = block_item
        scores = (
            jnp.einsum("qhd,khd->hqk", query_rows, key_heads, preferred_element_type=jnp.float32)
            * score_scale
        )
        weights = jnp.exp(scores - log_rows[:, :, None])
        weights_low = weights.astype(jnp.bfloat16)
        grad_weights = jnp.einsum(
            "qhd,khd->hqk", grad_rows, value_heads, preferred_element_type=jnp.float32
        )
        inner = jnp.sum(grad_weights * weights, axis=-1, keepdims=True)
        grad_scores = (weights * (grad_weights - inner)).astype(jnp.bfloat16)
        query_grad = (
            jnp.einsum("hqk,khd->qhd", grad_scores, key_heads, preferred_element_type=jnp.float32)
            * score_scale
        )
        key_grad = (
            key_grad
            + jnp.einsum(
                "hqk,qhd->khd", grad_scores, query_rows, preferred_element_type=jnp.float32
            )
            * score_scale
        )
        value_grad = value_grad + jnp.einsum(
            "hqk,qhd->khd", weights_low, grad_rows, preferred_element_type=jnp.float32
        )
        return ((key_grad, value_grad), query_grad.astype(jnp.bfloat16))

    zeros_heads = jnp.zeros((length, head_count, head_width), jnp.float32)
    (key_grad, value_grad), query_grad = lax.scan(
        one_block, (zeros_heads, zeros_heads), (query_heads, log_totals, upstream_heads)
    )
    width_all = head_count * head_width
    return (
        query_grad.reshape(length, width_all),
        key_grad.reshape(length, width_all).astype(jnp.bfloat16),
        value_grad.reshape(length, width_all).astype(jnp.bfloat16),
    )


def fetch(shards):
    return (
        lax.all_gather(shards[0], "fsdp", axis=0, tiled=True),
        lax.all_gather(shards[1], "fsdp", axis=0, tiled=True),
        lax.all_gather(shards[2], "fsdp", axis=0, tiled=True),
        lax.all_gather(shards[3], "fsdp", axis=0, tiled=True),
        lax.all_gather(shards[4], "fsdp", axis=0, tiled=True),
        lax.all_gather(shards[5], "fsdp", axis=0, tiled=True),
        lax.all_gather(shards[6], "fsdp", axis=0, tiled=True),
        lax.all_gather(shards[7], "fsdp", axis=0, tiled=True),
        lax.all_gather(shards[8], "fsdp", axis=0, tiled=True),
        lax.all_gather(shards[9], "fsdp", axis=0, tiled=True),
        lax.all_gather(shards[10], "fsdp", axis=0, tiled=True),
        lax.all_gather(shards[11], "fsdp", axis=0, tiled=True),
        lax.all_gather(shards[12], "fsdp", axis=0, tiled=True),
        lax.all_gather(shards[13], "fsdp", axis=0, tiled=True),
        lax.all_gather(shards[14], "fsdp", axis=0, tiled=True),
    )


def settle(grads):
    shares = (
        lax.psum_scatter(
            grads[0].astype(jnp.bfloat16), "fsdp", scatter_dimension=0, tiled=True
        ).astype(jnp.float32),
        lax.psum_scatter(
            grads[1].astype(jnp.bfloat16), "fsdp", scatter_dimension=0, tiled=True
        ).astype(jnp.float32),
        lax.psum_scatter(
            grads[2].astype(jnp.bfloat16), "fsdp", scatter_dimension=0, tiled=True
        ).astype(jnp.float32),
        lax.psum_scatter(
            grads[3].astype(jnp.bfloat16), "fsdp", scatter_dimension=0, tiled=True
        ).astype(jnp.float32),
        lax.psum_scatter(
            grads[4].astype(jnp.bfloat16), "fsdp", scatter_dimension=0, tiled=True
        ).astype(jnp.float32),
        lax.psum_scatter(
            grads[5].astype(jnp.bfloat16), "fsdp", scatter_dimension=0, tiled=True
        ).astype(jnp.float32),
        lax.psum_scatter(
            grads[6].astype(jnp.bfloat16), "fsdp", scatter_dimension=0, tiled=True
        ).astype(jnp.float32),
        lax.psum_scatter(
            grads[7].astype(jnp.bfloat16), "fsdp", scatter_dimension=0, tiled=True
        ).astype(jnp.float32),
        lax.psum_scatter(
            grads[8].astype(jnp.bfloat16), "fsdp", scatter_dimension=0, tiled=True
        ).astype(jnp.float32),
        lax.psum_scatter(
            grads[9].astype(jnp.bfloat16), "fsdp", scatter_dimension=0, tiled=True
        ).astype(jnp.float32),
        lax.psum_scatter(
            grads[10].astype(jnp.bfloat16), "fsdp", scatter_dimension=0, tiled=True
        ).astype(jnp.float32),
        lax.psum_scatter(
            grads[11].astype(jnp.bfloat16), "fsdp", scatter_dimension=0, tiled=True
        ).astype(jnp.float32),
        lax.psum_scatter(
            grads[12].astype(jnp.bfloat16), "fsdp", scatter_dimension=0, tiled=True
        ).astype(jnp.float32),
        lax.psum_scatter(
            grads[13].astype(jnp.bfloat16), "fsdp", scatter_dimension=0, tiled=True
        ).astype(jnp.float32),
        lax.psum_scatter(
            grads[14].astype(jnp.bfloat16), "fsdp", scatter_dimension=0, tiled=True
        ).astype(jnp.float32),
    )
    return (
        lax.psum(shares[0].astype(jnp.bfloat16), "seq").astype(jnp.float32),
        lax.psum(shares[1].astype(jnp.bfloat16), "seq").astype(jnp.float32),
        lax.psum(shares[2].astype(jnp.bfloat16), "seq").astype(jnp.float32),
        lax.psum(shares[3].astype(jnp.bfloat16), "seq").astype(jnp.float32),
        lax.psum(shares[4].astype(jnp.bfloat16), "seq").astype(jnp.float32),
        lax.psum(shares[5].astype(jnp.bfloat16), "seq").astype(jnp.float32),
        lax.psum(shares[6].astype(jnp.bfloat16), "seq").astype(jnp.float32),
        lax.psum(shares[7].astype(jnp.bfloat16), "seq").astype(jnp.float32),
        lax.psum(shares[8].astype(jnp.bfloat16), "seq").astype(jnp.float32),
        lax.psum(shares[9].astype(jnp.bfloat16), "seq").astype(jnp.float32),
        lax.psum(shares[10].astype(jnp.bfloat16), "seq").astype(jnp.float32),
        lax.psum(shares[11].astype(jnp.bfloat16), "seq").astype(jnp.float32),
        lax.psum(shares[12].astype(jnp.bfloat16), "seq").astype(jnp.float32),
        lax.psum(shares[13].astype(jnp.bfloat16), "seq").astype(jnp.float32),
        lax.psum(shares[14].astype(jnp.bfloat16), "seq").astype(jnp.float32),
    )


def one_clip(clip_in, clip_cot, clip_flag, gathered, head_count):
    (
        norm1_gain,
        norm1_bias,
        query_weight,
        key_weight,
        value_weight,
        query_bias,
        value_bias,
        proj_weight,
        proj_bias,
        norm2_gain,
        norm2_bias,
        fc1_weight,
        fc1_bias,
        fc2_weight,
        fc2_bias,
    ) = gathered
    gain_one = norm1_gain.astype(jnp.float32)
    gain_two = norm2_gain.astype(jnp.float32)
    tokens_in = clip_in.astype(jnp.float32)
    normed, scaled_one, inverse_one = layer_norm(
        tokens_in, gain_one, norm1_bias.astype(jnp.float32)
    )
    normed_low = normed.astype(jnp.bfloat16)
    queries = (matmul(normed_low, query_weight) + query_bias.astype(jnp.float32)).astype(
        jnp.bfloat16
    )
    keys_all = matmul(normed_low, key_weight).astype(jnp.bfloat16)
    values_all = (matmul(normed_low, value_weight) + value_bias.astype(jnp.float32)).astype(
        jnp.bfloat16
    )
    query_heads, key_heads, value_heads = (
        lax.all_to_all(queries, "seq", split_axis=1, concat_axis=0, tiled=True),
        lax.all_to_all(keys_all, "seq", split_axis=1, concat_axis=0, tiled=True),
        lax.all_to_all(values_all, "seq", split_axis=1, concat_axis=0, tiled=True),
    )
    mixed_heads, log_totals = attend(query_heads, key_heads, value_heads, head_count)
    attended = lax.all_to_all(mixed_heads, "seq", split_axis=0, concat_axis=1, tiled=True)
    middle = tokens_in + matmul(attended, proj_weight) + proj_bias.astype(jnp.float32)
    normed_two, scaled_two, inverse_two = layer_norm(
        middle, gain_two, norm2_bias.astype(jnp.float32)
    )
    normed_two_low = normed_two.astype(jnp.bfloat16)
    hidden_pre = matmul(normed_two_low, fc1_weight) + fc1_bias.astype(jnp.float32)
    hidden_low = gelu_value(hidden_pre).astype(jnp.bfloat16)
    output = middle + matmul(hidden_low, fc2_weight) + fc2_bias.astype(jnp.float32)
    grad_out = clip_cot.astype(jnp.float32) * clip_flag.astype(jnp.float32)
    grad_mlp = grad_out.astype(jnp.bfloat16)
    grad_fc2_weight = matmul_tn(hidden_low, grad_mlp)
    grad_fc2_bias = jnp.sum(grad_mlp.astype(jnp.float32), axis=0)
    grad_pre = (matmul_nt(grad_mlp, fc2_weight) * gelu_slope(hidden_pre)).astype(jnp.bfloat16)
    grad_fc1_weight = matmul_tn(normed_two_low, grad_pre)
    grad_fc1_bias = jnp.sum(grad_pre.astype(jnp.float32), axis=0)
    grad_norm_two = matmul_nt(grad_pre, fc1_weight)
    grad_ln_two, grad_norm2_gain, grad_norm2_bias = layer_norm_back(
        grad_norm_two, scaled_two, inverse_two, gain_two
    )
    grad_middle = grad_out + grad_ln_two
    grad_branch = grad_middle.astype(jnp.bfloat16)
    grad_proj_weight = matmul_tn(attended, grad_branch)
    grad_proj_bias = jnp.sum(grad_branch.astype(jnp.float32), axis=0)
    grad_att = matmul_nt(grad_branch, proj_weight).astype(jnp.bfloat16)
    grad_att_heads = lax.all_to_all(grad_att, "seq", split_axis=1, concat_axis=0, tiled=True)
    query_grad, key_grad, value_grad = attend_back(
        query_heads, key_heads, value_heads, log_totals, grad_att_heads, head_count
    )
    grad_queries, grad_keys, grad_values = (
        lax.all_to_all(query_grad, "seq", split_axis=0, concat_axis=1, tiled=True),
        lax.all_to_all(key_grad, "seq", split_axis=0, concat_axis=1, tiled=True),
        lax.all_to_all(value_grad, "seq", split_axis=0, concat_axis=1, tiled=True),
    )
    grad_query_weight = matmul_tn(normed_low, grad_queries)
    grad_key_weight = matmul_tn(normed_low, grad_keys)
    grad_value_weight = matmul_tn(normed_low, grad_values)
    grad_query_bias = jnp.sum(grad_queries.astype(jnp.float32), axis=0)
    grad_value_bias = jnp.sum(grad_values.astype(jnp.float32), axis=0)
    grad_norm_one = (
        matmul_nt(grad_queries, query_weight)
        + matmul_nt(grad_keys, key_weight)
        + matmul_nt(grad_values, value_weight)
    )
    grad_ln_one, grad_norm1_gain, grad_norm1_bias = layer_norm_back(
        grad_norm_one, scaled_one, inverse_one, gain_one
    )
    grad_in = grad_middle + grad_ln_one
    grads = (
        grad_norm1_gain,
        grad_norm1_bias,
        grad_query_weight,
        grad_key_weight,
        grad_value_weight,
        grad_query_bias,
        grad_value_bias,
        grad_proj_weight,
        grad_proj_bias,
        grad_norm2_gain,
        grad_norm2_bias,
        grad_fc1_weight,
        grad_fc1_bias,
        grad_fc2_weight,
        grad_fc2_bias,
    )
    return (output.astype(jnp.bfloat16), grad_in, grads)


def body(
    clips,
    cotangent,
    valid,
    norm1_gain,
    norm1_bias,
    query_weight,
    key_weight,
    value_weight,
    query_bias,
    value_bias,
    proj_weight,
    proj_bias,
    norm2_gain,
    norm2_bias,
    fc1_weight,
    fc1_bias,
    fc2_weight,
    fc2_bias,
):
    shards = (
        norm1_gain,
        norm1_bias,
        query_weight,
        key_weight,
        value_weight,
        query_bias,
        value_bias,
        proj_weight,
        proj_bias,
        norm2_gain,
        norm2_bias,
        fc1_weight,
        fc1_bias,
        fc2_weight,
        fc2_bias,
    )
    slot_count = clips.shape[0]
    head_count = H // lax.axis_size("seq")
    summed = None
    outputs = []
    grad_list = []
    for batch_slot in range(slot_count):
        gathered = fetch(shards)
        output, grad_in, grads = one_clip(
            clips[batch_slot], cotangent[batch_slot], valid[batch_slot], gathered, head_count
        )
        summed = (
            grads
            if summed is None
            else tuple((older + newer for older, newer in zip(summed, grads)))
        )
        outputs.append(output)
        grad_list.append(grad_in)
    summed = settle(summed)
    return (
        jnp.stack(outputs),
        jnp.stack(grad_list),
        summed[0],
        summed[1],
        summed[2],
        summed[3],
        summed[4],
        summed[5],
        summed[6],
        summed[7],
        summed[8],
        summed[9],
        summed[10],
        summed[11],
        summed[12],
        summed[13],
        summed[14],
    )


T, D, FF, NTILE = 1024, 1024, 4096, 8

log2_e = 1.4426950408889634
HD = 64
F32, BF16 = jnp.float32, jnp.bfloat16
ANY = pl.BlockSpec(memory_space=pl.ANY)


def dot(left, right, cl=1, cr=0):
    return lax.dot_general(left, right, (((cl,), (cr,)), ((), ())), preferred_element_type=F32)


def split3(v):
    hi = v.astype(BF16)
    r = v - hi.astype(F32)
    md = r.astype(BF16)
    lo = (r - md.astype(F32)).astype(BF16)
    return hi, md, lo


def aug_rows(v):
    hi, md, lo = split3(v)
    z = jnp.zeros((13, v.shape[1]), BF16)
    return jnp.concatenate([hi, md, lo, z], axis=0)


def ln_back(up, v, gain):
    m = jnp.mean(v, axis=-1, keepdims=True)
    d = v - m
    r = lax.rsqrt(jnp.mean(d * d, axis=-1, keepdims=True) + norm_eps)
    xh = d * r
    s = up * gain
    back = r * (s - jnp.mean(s, axis=-1, keepdims=True) - xh * jnp.mean(s * xh, axis=-1, keepdims=True))
    return back, jnp.sum(up * xh, axis=0, keepdims=True), jnp.sum(up, axis=0, keepdims=True)


def bwd_head(h, qkvt, ot, dot_v, lse_v):
    T = ot.shape[1]
    qb = T // 2
    scale = HD ** -0.5
    r = pl.multiple_of(h * HD, HD)
    rows = pl.ds(r, HD)
    ones = jnp.ones((16, T), BF16)
    kh = qkvt[1, rows, :]
    ka = jnp.concatenate([kh, ones], axis=0)
    va = jnp.concatenate([qkvt[2, rows, :], ones], axis=0)
    dk = dv = None
    for b in range(2):
        cols = slice(b * qb, (b + 1) * qb)
        qh = qkvt[0, rows, cols] * jnp.asarray(scale, BF16)
        do = dot_v[rows, cols]
        delta = jnp.sum(do.astype(F32) * ot[rows, cols].astype(F32), axis=0, keepdims=True)
        qa = jnp.concatenate([qh, aug_rows(-lse_v[pl.ds(h, 1), cols])], axis=0)
        da = jnp.concatenate([do, aug_rows(-delta)], axis=0)
        p = jnp.exp2(dot(qa, ka, 0, 0) * log2_e)
        ds = (p * dot(da, va, 0, 0)).astype(BF16)
        ndv = dot(do, p.astype(BF16))
        ndk = dot(qh, ds)
        dv = ndv if dv is None else dv + ndv
        dk = ndk if dk is None else dk + ndk
        qkvt[0, rows, cols] = (dot(kh, ds, 1, 1) * scale).astype(BF16)
    qkvt[1, rows, :] = dk.astype(BF16)
    qkvt[2, rows, :] = dv.astype(BF16)


MESH = pl.DeviceIdType.MESH


class Place:
    def __init__(self, size):
        f = lax.axis_index("fsdp")
        self.f, self.core, chip = f, f % 2, f // 2
        self.deep, self.count = size // 4, size // 2
        x, z = chip % 2, chip // 2
        self.pos = z + x * (2 * self.deep - 1 - 2 * z)
        self.mate = f + 1 - 2 * self.core
        self.y = lax.axis_index("seq")

    def chip(self, off):
        pos = (self.pos + self.count + off) % self.count
        hi = pos // self.deep
        return 2 * (pos + hi * (2 * self.deep - 1 - 2 * pos)) + hi

    def side(self, d):
        return {"fsdp": 2 * self.chip((1, -1)[d]) + self.core}

    def partner(self):
        return {"fsdp": self.mate}

    def across(self):
        return {"seq": 1 - self.y}

    def barrier(self):
        sem = pltpu.get_barrier_semaphore()
        for dev in (self.side(0), self.side(1), self.partner(), self.across()):
            pl.semaphore_signal(sem, inc=1, device_id=dev, device_id_type=MESH)
        pl.semaphore_wait(sem, 4)


def remote(src, dst, ss, rs, dev):
    return pltpu.make_async_remote_copy(src_ref=src, dst_ref=dst, send_sem=ss, recv_sem=rs, device_id=dev, device_id_type=MESH)


class Gather:
    def __init__(self, place, view, rsem, psem):
        self.pl, self.view, self.rsem, self.psem = place, view, rsem, psem
        self.last = place.count // 2 - 1

    def part(self, d, s):
        return d if s == self.last else 2

    def block(self, d, s, ahead):
        k = s + ahead
        return self.pl.chip(-k if d == 0 else k)

    def ring(self, d, s, ahead=0):
        v = self.view(2 * self.block(d, s, ahead) + self.pl.core, self.part(d, s))
        return remote(v, v, self.rsem.at[0, d, s], self.rsem.at[1, d, s], self.pl.side(d))

    def mate(self, slot, chip, part, core):
        v = self.view(2 * chip + core, part)
        return remote(v, v, self.psem.at[0, slot], self.psem.at[1, slot], self.pl.partner())

    def slots(self, s):
        return [(1 + 2 * s + d, self.block(d, s, 1), self.part(d, s)) for d in range(2)]

    def start(self):
        for d in range(2):
            self.ring(d, 0).start()
        self.mate(0, self.pl.chip(0), 2, self.pl.core).start()

    def step(self, s):
        for d in range(2):
            self.ring(d, s, 1).wait_recv()
            if s < self.last:
                self.ring(d, s + 1).start()
        for slot, chip, part in self.slots(s):
            self.mate(slot, chip, part, self.pl.core).start()

    def own_mate(self):
        self.mate(0, self.pl.chip(0), 2, 1 - self.pl.core).wait_recv()

    def step_mate(self, s):
        for slot, chip, part in self.slots(s):
            self.mate(slot, chip, part, 1 - self.pl.core).wait_recv()

    def all_mates(self):
        self.own_mate()
        for s in range(self.last + 1):
            self.step_mate(s)

    def drain(self):
        for s in range(self.last + 1):
            for d in range(2):
                self.ring(d, s).wait_send()
            for slot, chip, part in self.slots(s):
                self.mate(slot, chip, part, self.pl.core).wait_send()
        self.mate(0, self.pl.chip(0), 2, self.pl.core).wait_send()


def fwd_body(size, clips, cot, sml, wq, wk, wv, wp, w1, w2,
             out_o, cot_o, x_o, sm_o, wqkv_o, wp_o, w1_o, w2_o, n1t_o, qkvt_o, ot_o, lse_o, mid_o, n2_o, h_o, g_o,
             x_v, smb, sm_v, wqkv_v, wp_v, w1_v, w2_v, n1t, qkvt, ot, lse_v, mid, n2, acc, hst, gst, b1_v, smt,
             rsem, psem, xsem, lsem, osem, tsem):
    here = Place(size)
    T, D = x_v.shape
    FF = w1_v.shape[1]
    tile = hst.shape[2]
    heads = D // HD
    half = T // 2
    nd, nf = D // size, FF // size
    y = here.y
    ymine = pl.ds(pl.multiple_of(y * half, half), half)
    yother = pl.ds(pl.multiple_of((1 - y) * half, half), half)

    def local(a, b, i):
        return pltpu.make_async_copy(a, b, lsem.at[i])

    def rows(ref, n, lead):
        def view(f, part):
            k = n if part == 2 else n // 2
            at = pl.ds(pl.multiple_of(f * n + (n // 2 if part == 1 else 0), k), k)
            return ref.at[:, at, :] if lead else ref.at[at, :]
        return view

    def smview(f, part):
        if part == 2:
            return smb.at[f]
        return smb.at[f, :, part * (D // 2):(part + 1) * (D // 2)]

    views = [smview, rows(wqkv_v, nd, True), rows(wp_v, nd, False), rows(w1_v, nd, False), rows(w2_v, nf, False)]
    ga, gq, gp, g1, g2 = [Gather(here, v, rsem.at[i], psem.at[i]) for i, v in enumerate(views)]
    own = pl.ds(pl.multiple_of(here.f * nd, nd), nd)
    ownf = pl.ds(pl.multiple_of(here.f * nf, nf), nf)
    loc = [local(sml, smb.at[here.f], 0)]
    loc += [local(w, wqkv_v.at[j, own, :], 1 + j) for j, w in enumerate((wq, wk, wv))]
    loc += [local(wp, wp_v.at[own, :], 4), local(w1, w1_v.at[own, :], 5), local(w2, w2_v.at[ownf, :], 6), local(clips.at[y], x_v.at[ymine, :], 7)]
    for c in loc:
        c.start()
    here.barrier()
    xsend = remote(clips.at[1 - y], x_v.at[ymine, :], xsem.at[0, 0], xsem.at[0, 1], here.across())
    xrecv = remote(clips.at[1 - y], x_v.at[yother, :], xsem.at[0, 0], xsem.at[0, 1], here.across())
    csend = remote(cot.at[1 - y], cot_o, xsem.at[1, 0], xsem.at[1, 1], here.across())
    xsend.start()
    csend.start()
    for c in loc[:4]:
        c.wait()
    ga.start()
    gq.start()
    for c in loc[4:]:
        c.wait()

    def ln1(i, c):
        r = pl.multiple_of(i * 256, 256)
        v = x_v[pl.ds(r, 256), :].astype(F32)
        m = jnp.mean(v, axis=-1, keepdims=True)
        d = v - m
        mid[pl.ds(r, 256), :] = d * lax.rsqrt(jnp.mean(d * d, axis=-1, keepdims=True) + norm_eps)
        return c

    per = half // 256
    lax.fori_loop(y * per, y * per + per, ln1, 0)
    for s in range(ga.last + 1):
        ga.step(s)
        gq.step(s)
        if s == ga.last - 1:
            gp.start()
            g1.start()
    xrecv.wait_recv()
    lax.fori_loop((1 - y) * per, (1 - y) * per + per, ln1, 0)
    ga.all_mates()
    sm_v[...] = jnp.sum(smb[...].astype(F32), axis=0)
    smt[...] = jnp.transpose(sm_v[...])

    def ln1b(i, c):
        r = pl.multiple_of(i * 256, 256)
        n1t[:, pl.ds(r, 256)] = jnp.transpose((mid[pl.ds(r, 256), :] * sm_v[0:1, :] + sm_v[1:2, :]).astype(BF16))
        return c

    lax.fori_loop(0, T // 256, ln1b, 0)
    gq.all_mates()
    outs = []

    def save(a, b):
        c = pltpu.make_async_copy(a, b, osem.at[len(outs)])
        outs.append(c)
        c.start()

    save(wqkv_v, wqkv_o)
    save(x_v, x_o)
    save(sm_v, sm_o)
    save(n1t, n1t_o)
    hd = D // 2
    for j in range(3):
        for o in range(2):
            v = dot(wqkv_v[j, :, o * hd:(o + 1) * hd], n1t[...], 0, 0)
            if j != 1:
                v = v + smt[o * hd:(o + 1) * hd, (2 if j == 0 else 3):(3 if j == 0 else 4)]
            qkvt[j, o * hd:(o + 1) * hd, :] = v.astype(BF16)
    save(qkvt, qkvt_o)
    qb = T // 2
    ones = jnp.ones((16, T), BF16)

    def head(h, c):
        r = pl.multiple_of(h * HD, HD)
        kh = qkvt[1, pl.ds(r, HD), :]
        vh = jnp.concatenate([qkvt[2, pl.ds(r, HD), :], ones], axis=0)
        for b in range(2):
            qh = qkvt[0, pl.ds(r, HD), b * qb:(b + 1) * qb]
            s = dot(kh, qh, 0, 0)
            m = jnp.max(s, axis=0, keepdims=True)
            p = jnp.exp2((s - m) * (log2_e * HD ** -0.5)).astype(BF16)
            o = dot(vh, p)
            total = o[HD:HD + 1, :]
            ot[pl.ds(r, HD), b * qb:(b + 1) * qb] = (o[:HD, :] / total).astype(BF16)
            lse_v[pl.ds(h, 1), b * qb:(b + 1) * qb] = m * HD ** -0.5 + jnp.log(total)
        return c

    cuts = (0, 3 * heads // 16, 10 * heads // 16, heads)
    for s in range(3):
        lax.fori_loop(cuts[s], cuts[s + 1], head, 0)
        gp.step(s)
        g1.step(s)
        if s == 1:
            g2.start()
    save(ot, ot_o)
    save(lse_v, lse_o)
    for s in range(3, gp.last + 1):
        gp.step(s)
    gp.all_mates()
    save(wp_v, wp_o)

    def proj(i, c):
        r = pl.multiple_of(i * 512, 512)
        v = dot(ot[:, pl.ds(r, 512)], wp_v[...], 0, 0) + x_v[pl.ds(r, 512), :].astype(F32) + sm_v[4:5, :]
        mid[pl.ds(r, 512), :] = v
        m = jnp.mean(v, axis=-1, keepdims=True)
        d = v - m
        s = d * lax.rsqrt(jnp.mean(d * d, axis=-1, keepdims=True) + norm_eps)
        n2[pl.ds(r, 512), :] = (s * sm_v[5:6, :] + sm_v[6:7, :]).astype(BF16)
        acc[pl.ds(r, 512), :] = v + sm_v[7:8, :]
        return c

    lax.fori_loop(0, T // 512, proj, 0)
    save(mid, mid_o)
    save(n2, n2_o)
    for k in range(FF // tile):
        kk = k * tile
        b1_v[k:k + 1, :] = sm_v[8 + kk // D:9 + kk // D, kk % D:kk % D + tile]
    for s in range(3, g1.last + 1):
        g1.step(s)
    g2.step(0)
    g1.all_mates()
    g2.own_mate()
    g2.step_mate(0)
    save(w1_v, w1_o)
    saves = {}
    order = [0]
    for k in range(1, here.count // 2):
        order += [-k, k]
    order.append(here.count // 2)

    def tcp(k, slot, t):
        return pltpu.make_async_copy((hst, gst)[k].at[slot], (h_o, g_o)[k].at[t], tsem.at[k, slot])

    def wcp(j, t):
        at = pl.ds(pl.multiple_of(t * tile, tile), tile)
        return pltpu.make_async_copy(w2_v.at[at, :], w2_o.at[at, :], tsem.at[2, j])

    for j, off in enumerate(order):
        t = here.chip(off)
        slot = j % 2
        if j >= 3 and j % 2 == 1:
            g2.step(j // 2)
            g2.step_mate(j // 2)
        wcp(j, t).start()
        if j >= 2:
            for k in range(2):
                tcp(k, slot, here.chip(order[j - 2])).wait()
        col = pl.multiple_of(t * tile, tile)

        def mlp(i, c, t=t, slot=slot, col=col):
            r = pl.multiple_of(i * 512, 512)
            u = dot(n2[pl.ds(r, 512), :], w1_v[:, pl.ds(col, tile)]) + b1_v[pl.ds(t, 1), :]
            cdf = 0.5 + 0.5 * lax.erf(u * root_half)
            hb = (u * cdf).astype(BF16)
            hst[slot, pl.ds(r, 512), :] = hb
            gst[slot, pl.ds(r, 512), :] = (cdf + (u * inv_root_tau) * jnp.exp2(u * u * (-0.5 * log2_e))).astype(BF16)
            acc[pl.ds(r, 512), :] += dot(hb, w2_v[pl.ds(col, tile), :])
            return c

        lax.fori_loop(0, T // 512, mlp, 0)
        for k in range(2):
            tcp(k, slot, t).start()
    for j in range(len(order) - 2, len(order)):
        for k in range(2):
            tcp(k, j % 2, here.chip(order[j])).wait()
    outs[3].wait()
    n1t[...] = acc[...].astype(BF16)
    save(n1t, out_o)
    for j, off in enumerate(order):
        wcp(j, here.chip(off)).wait()
    for i, c in enumerate(outs):
        if i != 3:
            c.wait()
    for g in (ga, gq, gp, g1, g2):
        g.drain()
    xsend.wait_send()
    csend.wait_send()
    remote(cot.at[1 - y], cot_o, xsem.at[1, 0], xsem.at[1, 1], here.across()).wait_recv()


S = jax.ShapeDtypeStruct
V = pltpu.VMEM


def fwd_call(size, T, D, FF):
    tile = 2 * FF // size
    heads = D // HD
    small = (16, D)
    dma = pltpu.SemaphoreType.DMA
    steps = size // 4
    return pl.pallas_call(
        functools.partial(fwd_body, size),
        name="forward",
        in_specs=[ANY] * 9,
        out_specs=[ANY] * 16,
        out_shape=[S((T, D), BF16), S((T // 2, D), BF16), S((T, D), BF16), S(small, F32), S((3, D, D), BF16), S((D, D), BF16), S((D, FF), BF16), S((FF, D), BF16),
                   S((D, T), BF16), S((3, D, T), BF16), S((D, T), BF16), S((heads, T), F32), S((T, D), F32), S((T, D), BF16), S((FF // tile, T, tile), BF16), S((FF // tile, T, tile), BF16)],
        scratch_shapes=[V((T, D), BF16), V((size,) + small, BF16), V(small, F32), V((3, D, D), BF16), V((D, D), BF16), V((D, FF), BF16), V((FF, D), BF16),
                        V((D, T), BF16), V((3, D, T), BF16), V((D, T), BF16), V((heads, T), F32), V((T, D), F32), V((T, D), BF16), V((T, D), F32),
                        V((2, T, tile), BF16), V((2, T, tile), BF16), V((FF // tile, tile), F32), V((D, 16), F32),
                        dma((5, 2, 2, steps)), dma((5, 2, 2 * steps + 1)), dma((2, 2)), dma((8,)), dma((12,)), dma((3, max(2, FF // tile)))],
        compiler_params=pltpu.CompilerParams(vmem_limit_bytes=63 << 20, collective_id=0, has_side_effects=True),
    )


def fold(dst, *srcs):
    def one(q, c):
        v = dst[q].astype(F32)
        for s in srcs:
            v = v + s[q].astype(F32)
        dst[q] = v.astype(dst.dtype)
        return c

    lax.fori_loop(0, dst.shape[0], one, 0)


def offset(j):
    odd = j % 2
    return odd * ((7 - j) // 2) - (1 - odd) * ((8 - j) // 2)


class Scatter:
    def __init__(self, here, land, rb, n, cols, msem, rsem, ysem, fin_o=None, y_o=None):
        self.pl, self.land, self.rb, self.n, self.cols = here, land, rb, n, cols
        self.msem, self.rsem, self.ysem, self.fin_o, self.y_o = msem, rsem, ysem, fin_o, y_o

    def cut(self, part):
        c0, w = self.cols
        return slice(c0, c0 + w) if part == 2 else slice(c0 + part * (w // 2), c0 + (part + 1) * (w // 2))

    def block(self, j, part=2):
        return self.land.at[j, 0:self.n, :, self.cut(part)]

    def came(self, d, s):
        return self.rb.at[d, s, 0:self.n, :, self.cut(d if s == 0 else 2)]

    def mate(self, j, src=None):
        dst = self.block(j)
        return remote(dst if src is None else src, dst, self.msem.at[0, j], self.msem.at[1, j], self.pl.partner())

    def settle(self, j, own):
        self.mate(j).wait_recv()
        fold(self.block(j), own)
        self.mate(j).wait_send()

    def ring(self, d, s):
        src = self.block(0, d) if s == 0 else self.block(2 * s - 1 + d)
        return remote(src, self.came(d, s), self.rsem.at[0, d, s], self.rsem.at[1, d, s], self.pl.side(d))

    def step(self, s):
        for d in range(2):
            if s:
                self.ring(d, s - 1).wait_recv()
                fold(self.block(2 * s - 1 + d, d if s == 1 else 2), self.came(d, s - 1))
            self.ring(d, s).start()

    def close(self):
        for d in range(2):
            self.ring(d, 3).wait_recv()
        fold(self.block(7), self.came(0, 3), self.came(1, 3))

    def view(self, ref):
        return ref.at[0:self.n, :, self.cut(2)]

    def over(self):
        return remote(self.block(7), self.view(self.y_o), self.ysem.at[0], self.ysem.at[1], self.pl.across())

    def keep(self):
        return pltpu.make_async_copy(self.block(7), self.view(self.fin_o), self.ysem.at[2])

    def finish(self):
        self.close()
        self.over().start()
        self.keep().start()

    def drain_ring(self):
        for s in range(4):
            for d in range(2):
                self.ring(d, s).wait_send()

    def drain(self):
        self.drain_ring()
        self.over().wait_send()
        self.keep().wait()


def bwd_body(size, valid, cotangent, cot_in, out, x, sm, wqkv, wp, w1, w2, n1t, qkvt, ot, lse, mid, n2, hs, gs,
             out_o, gx_o, gxr_o, dw2_o, dw2_y, dw1_o, dw1_y, dwp_o, dwp_y, dq_o, dq_y, sg_o,
             g_v, n2_v, gacc, h_v, pre_v, w1_v, w2_v, b1g, mid_v, qkvt_v, ot_v, lse_v, sm_v, sg_v, sgm_v, sgt_v, sgy_v,
             st_v, land_a, land_b, land_p, land_s, rb_a, rb_b, rb_p, rb_s,
             sem, tsem, wsem, mlsem, xsem, msem, rsem, ysem, ssem, gsem, free):
    here = Place(size)
    y, core = here.y, here.core
    half = T // 2
    ymine = pl.multiple_of(y * half, half)
    yother = pl.multiple_of((1 - y) * half, half)

    def cp(a, b, i):
        return pltpu.make_async_copy(a, b, sem.at[i])

    first = [cp(cotangent.at[y], g_v.at[pl.ds(ymine, half), :], 0), cp(cot_in, g_v.at[pl.ds(yother, half), :], 1), cp(n2, n2_v, 2), cp(sm, sm_v, 3)]
    later = [cp(qkvt, qkvt_v, 4), cp(ot, ot_v, 5), cp(lse, lse_v, 6)]
    last = [cp(x, h_v, 7), cp(n1t, w1_v, 8)]

    def chip(j):
        return here.chip(offset(j))

    def tl(t, s):
        c = pl.multiple_of(t * 512, 512)
        d = pl.multiple_of(s * 512, 512)
        return [
            pltpu.make_async_copy(hs.at[t], h_v.at[:, pl.ds(d, 512)], tsem.at[s, 0]),
            pltpu.make_async_copy(gs.at[t], pre_v.at[t], tsem.at[s, 1]),
            pltpu.make_async_copy(w1.at[:, pl.ds(c, 512)], w1_v.at[:, pl.ds(d, 512)], tsem.at[s, 2]),
            pltpu.make_async_copy(w2.at[pl.ds(c, 512), :], w2_v.at[pl.ds(d, 512), :], tsem.at[s, 3]),
        ]

    for c in first:
        c.start()
    for c in tl(chip(0), 0):
        c.start()
    for c in later:
        c.start()
    here.barrier()
    osend = remote(out.at[pl.ds(yother, half), :], out_o, gsem.at[0, 0], gsem.at[0, 1], here.across())
    osend.start()
    s2 = Scatter(here, land_a, rb_a, 4, (0, D), msem.at[0], rsem.at[0], ysem.at[0], dw2_o, dw2_y)
    s1 = Scatter(here, land_b, rb_b, 4, (0, D), msem.at[1], rsem.at[1], ysem.at[1], dw1_o, dw1_y)
    sp = Scatter(here, land_p, rb_p, 1, (0, D), msem.at[2], rsem.at[2], ysem.at[2], dwp_o, dwp_y)
    sq = [Scatter(here, land_a, rb_a, 3, (g * 512, 512), msem.at[3 + g], rsem.at[3 + g], ysem.at[3 + g], dq_o, dq_y) for g in range(2)]
    ss = Scatter(here, land_s, rb_s, 2, (0, 128), None, rsem.at[5], None)
    for c in first:
        c.wait()
    flag = valid[y].astype(F32)
    sg_v[...] = jnp.zeros_like(sg_v)

    def mask(i, c):
        r = pl.multiple_of(i * 256, 256)
        v = g_v[pl.ds(r, 256), :].astype(F32) * flag
        g_v[pl.ds(r, 256), :] = v.astype(BF16)
        sg_v[7:8, :] += jnp.sum(v, axis=0, keepdims=True)
        return c

    lax.fori_loop(0, T // 256, mask, 0)

    def st2(j, k):
        return st_v.at[0, pl.ds((j % 2) * 8 + k * 4, 4)]

    def tile(j, c):
        s = j % 2
        t = chip(j)

        @pl.when(j + 1 < NTILE)
        def _():
            for k in tl(chip(j + 1), 1 - s):
                k.start()

        for k in tl(t, s):
            k.wait()
        col = pl.ds(pl.multiple_of(s * 512, 512), 512)
        gb = g_v[...]
        st_v[0, pl.ds(s * 8, 8)] = dot(h_v[:, col], gb, 0, 0).astype(BF16).reshape(8, 64, D)
        s2.mate(j, st2(j, 1 - core)).start()
        pre = (dot(gb, w2_v[col, :], 1, 1) * pre_v[t].astype(F32)).astype(BF16)
        pre_v[t] = pre
        b1g[pl.ds(t, 1), :] = jnp.sum(pre.astype(F32), axis=0, keepdims=True)
        v = dot(pre, w1_v[:, col], 1, 1)

        @pl.when(j == 0)
        def _():
            gacc[...] = v

        @pl.when(j > 0)
        def _():
            gacc[...] += v
            s2.settle(j - 1, st2(j - 1, core))

        for k, n in enumerate((1, 3, 6)):
            @pl.when(j == n)
            def _(k=k):
                s2.step(k)

        return c

    lax.fori_loop(0, NTILE, tile, 0)
    for c in last:
        c.start()
    sg_v[8:16, 0:512] = b1g[...]

    def slots(q):
        return (2 * q + 7) % 8, 2 * q

    def st1(q, i, k):
        return st_v.at[1 + q % 2, pl.ds(i * 8 + k * 4, 4)]

    def settle1(q):
        for i, j in enumerate(slots(q)):
            s1.settle(j, st1(q, i, core))

    def pair1(q, c):
        at = [pl.ds(pl.multiple_of(chip(j) * 128, 128), 128) for j in slots(q)]
        left = jnp.concatenate([n2_v[:, a] for a in at], axis=1)
        for cb in range(4):
            for k in range(2):
                v = dot(left, pre_v[2 * cb + k], 0, 0).astype(BF16)
                for i in range(2):
                    for e in range(2):
                        st_v[1 + q % 2, i * 8 + e * 4 + cb, :, k * 512:(k + 1) * 512] = v[i * 128 + e * 64:i * 128 + e * 64 + 64]
        for i, j in enumerate(slots(q)):
            s1.mate(j, st1(q, i, 1 - core)).start()

        @pl.when(q == 0)
        def _():
            s2.settle(7, st2(7, core))

        @pl.when(q > 0)
        def _():
            settle1(q - 1)

        @pl.when(q == 2)
        def _():
            s2.step(3)
            s1.step(0)

        return c

    lax.fori_loop(0, 4, pair1, 0)
    wpl = [pltpu.make_async_copy(wp.at[:, i * 512:(i + 1) * 512], pre_v.at[6 + i], wsem.at[6 + i]) for i in range(2)]
    wl = [pltpu.make_async_copy(wqkv.at[j, :, i * 512:(i + 1) * 512], pre_v.at[2 * j + i], wsem.at[2 * j + i]) for j in range(3) for i in range(2)]
    for c in wpl + wl:
        c.start()
    settle1(3)

    def ml(i, s):
        return pltpu.make_async_copy(mid.at[pl.ds(pl.multiple_of(i * 256, 256), 256), :], mid_v.at[s], mlsem.at[s])

    ml(0, 0).start()

    def ln2(i, c):
        r = pl.multiple_of(i * 256, 256)
        s = i % 2

        @pl.when(i < 3)
        def _():
            ml(i + 1, 1 - s).start()

        ml(i, s).wait()
        back, dg, db = ln_back(gacc[pl.ds(r, 256), :], mid_v[s], sm_v[5:6, :])
        gm = g_v[pl.ds(r, 256), :].astype(F32) + back
        gacc[pl.ds(r, 256), :] = gm
        gb = gm.astype(BF16)
        g_v[pl.ds(r, 256), :] = gb
        sg_v[5:6, :] += dg
        sg_v[6:7, :] += db
        sg_v[4:5, :] += jnp.sum(gb.astype(F32), axis=0, keepdims=True)
        return c

    lax.fori_loop(0, 4, ln2, 0)
    for c in later + wpl:
        c.wait()
    for i in range(2):
        rows = slice(i * 512, (i + 1) * 512)
        st_v[0, i * 8:(i + 1) * 8] = dot(ot_v[rows, :], g_v[...]).astype(BF16).reshape(8, 64, D)
        w2_v[rows, :] = (dot(pre_v[6, rows, :], g_v[:, 0:512], 1, 1) + dot(pre_v[7, rows, :], g_v[:, 512:1024], 1, 1)).astype(BF16)

    def stp(j, k):
        return st_v.at[0, pl.ds(2 * chip(j) + k, 1)]

    def matep(j, c):
        sp.mate(j, stp(j, 1 - core)).start()
        return c

    def settlep(j, c):
        sp.settle(j, stp(j, core))
        return c

    lax.fori_loop(0, 8, matep, 0)
    s2.finish()
    s1.step(1)

    def stq(g, j, k):
        return st_v.at[:, 2 * chip(j) + k, :, g * 512:(g + 1) * 512]

    def dqkv(g):
        for j in range(3):
            for i in range(2):
                v = dot(w1_v[i * 512:(i + 1) * 512, :], qkvt_v[j, g * 512:(g + 1) * 512, :], 1, 1).astype(BF16)
                st_v[j, i * 8:(i + 1) * 8, :, g * 512:(g + 1) * 512] = v.reshape(8, 64, 512)

        def send(j, c):
            sq[g].mate(j, stq(g, j, 1 - core)).start()
            return c

        lax.fori_loop(0, 8, send, 0)

    def settleq(g):
        def one(j, c):
            sq[g].settle(j, stq(g, j, core))
            return c

        lax.fori_loop(0, 8, one, 0)

    def begin_p():
        lax.fori_loop(0, 8, settlep, 0)
        sp.step(0)

    def free_a():
        s2.drain()
        pl.semaphore_signal(free.at[0], inc=1, device_id=here.partner(), device_id_type=MESH)
        for d in range(2):
            pl.semaphore_signal(free.at[1], inc=1, device_id=here.side(d), device_id_type=MESH)

    def first_q():
        for c in last:
            c.wait()
        pl.semaphore_wait(free.at[0], 1)
        dqkv(0)

    def begin_q():
        settleq(0)
        pl.semaphore_wait(free.at[1], 2)
        sq[0].step(0)

    events = {
        0: [begin_p],
        3: [lambda: s1.step(2), lambda: sp.step(1), free_a],
        6: [lambda: s1.step(3), lambda: sp.step(2)],
        7: [first_q],
        8: [begin_q, lambda: sp.step(3)],
        10: [s1.finish],
        11: [sp.finish, lambda: sq[0].step(1)],
        14: [lambda: sq[0].step(2)],
    }

    def hd(h, c):
        bwd_head(h, qkvt_v, ot_v, w2_v, lse_v)
        for n, fns in events.items():
            @pl.when(h == n)
            def _(fns=fns):
                for fn in fns:
                    fn()
        return c

    lax.fori_loop(0, 16, hd, 0)
    dqkv(1)
    ones = jnp.ones((16, T), BF16)
    for j, row in ((0, 2), (2, 3)):
        sg_v[row:row + 1, :] = dot(ones, qkvt_v[j], 1, 1)[0:1, :]
    settleq(1)
    sq[1].step(0)
    for c in wl:
        c.wait()

    def row(i):
        return pl.multiple_of((1 - i // 2) * yother + (i // 2) * ymine + (i % 2) * 256, 256)

    def xsend(i):
        at = pl.ds(pl.multiple_of(i * 256, 256), 256)
        return remote(w2_v.at[at, :], gxr_o.at[at, :], xsem.at[0, i], xsem.at[1, i], here.across())

    def xkeep(i):
        return pltpu.make_async_copy(mid_v.at[i], gx_o.at[pl.ds(i * 256, 256), :], xsem.at[2, i])

    def fin(i, c):
        r = row(i)
        up = None
        for j in range(3):
            for k in range(2):
                v = dot(qkvt_v[j, k * 512:(k + 1) * 512, pl.ds(r, 256)], pre_v[2 * j + k], 0, 1)
                up = v if up is None else up + v
        back, dg, db = ln_back(up, h_v[pl.ds(r, 256), :].astype(F32), sm_v[0:1, :])
        v = gacc[pl.ds(r, 256), :] + back
        sg_v[0:1, :] += dg
        sg_v[1:2, :] += db

        @pl.when(i < 2)
        def _():
            w2_v[pl.ds(pl.multiple_of((i % 2) * 256, 256), 256), :] = v.astype(BF16)
            xsend(i % 2).start()

        @pl.when(i >= 2)
        def _():
            mid_v[i % 2] = v
            xkeep(i % 2).start()

        @pl.when(i == 0)
        def _():
            sq[0].step(3)

        @pl.when(i == 2)
        def _():
            sq[1].step(1)

        return c

    lax.fori_loop(0, 4, fin, 0)
    sg1 = remote(sg_v, sgm_v, ssem.at[0, 0], ssem.at[0, 1], here.partner())
    sg1.start()
    sq[0].finish()
    sg1.wait_recv()
    sgt_v[...] = sg_v[...] + sgm_v[...]
    sg2 = remote(sgt_v, sgy_v, ssem.at[1, 0], ssem.at[1, 1], here.across())
    sg2.start()
    sq[1].step(2)
    sg2.wait_recv()
    sg1.wait_send()
    sg_v[...] = sgt_v[...] + sgy_v[...]
    b1g[...] = sg_v[8:16, 0:512]
    for j in range(8):
        t = chip(j)
        land_s[j, 0] = sg_v[0:8, pl.ds(pl.multiple_of(t * 128, 128), 128)]
        land_s[j, 1, 4:8, :] = jnp.zeros((4, 128), F32)
        fb = b1g[pl.ds(t, 1), :]
        for q in range(4):
            land_s[j, 1, q:q + 1, :] = fb[:, q * 128:(q + 1) * 128]
    ss_steps(ss, 0)
    ss_steps(ss, 1)
    sq[1].step(3)
    ss_steps(ss, 2)
    ss_steps(ss, 3)
    for d in range(2):
        ss_ring(ss, d, 3).wait_recv()
    fold(land_s.at[7], rb_s.at[0, 3], rb_s.at[1, 3])
    skeep = pltpu.make_async_copy(land_s.at[7], sg_o, ssem.at[2, 0])
    skeep.start()
    sq[1].finish()
    for s in range(4):
        for d in range(2):
            ss_ring(ss, d, s).wait_send()
    sg2.wait_send()
    skeep.wait()
    for i in range(2):
        xsend(i).wait()
        xkeep(i).wait()
    osend.wait()
    for s in (s1, sp, sq[0], sq[1]):
        s.drain()
    for s in (s2, s1, sp, sq[0], sq[1]):
        s.over().wait_recv()


def ss_ring(ss, d, s):
    if s == 0:
        src, dst = ss.land.at[0, d], ss.rb.at[d, 0, d]
    else:
        src, dst = ss.land.at[2 * s - 1 + d], ss.rb.at[d, s]
    return remote(src, dst, ss.rsem.at[0, d, s], ss.rsem.at[1, d, s], ss.pl.side(d))


def ss_steps(ss, s):
    for d in range(2):
        if s:
            ss_ring(ss, d, s - 1).wait_recv()
            j = 2 * s - 1 + d
            if s == 1:
                ss.land[j, d] = ss.land[j, d] + ss.rb[d, 0, d]
            else:
                fold(ss.land.at[j], ss.rb.at[d, s - 1])
        ss_ring(ss, d, s).start()


def bwd_call(size):
    dma = pltpu.SemaphoreType.DMA
    block = S((4, 64, D), BF16)
    return pl.pallas_call(
        functools.partial(bwd_body, size),
        name="backward",
        in_specs=[pl.BlockSpec(memory_space=pltpu.SMEM)] + [ANY] * 17,
        out_specs=[ANY] * 12,
        out_shape=[S((T // 2, D), BF16), S((T // 2, D), F32), S((T // 2, D), BF16), block, block, block, block,
                   S((1, 64, D), BF16), S((1, 64, D), BF16), S((3, 64, D), BF16), S((3, 64, D), BF16), S((2, 8, 128), F32)],
        scratch_shapes=[V((T, D), BF16), V((T, D), BF16), V((T, D), F32), V((T, 1024), BF16), V((NTILE, T, 512), BF16), V((D, 1024), BF16), V((1024, D), BF16),
                        V((8, 512), F32), V((2, 256, D), F32), V((3, D, T), BF16), V((D, T), BF16), V((16, T), F32), V((16, D), F32), V((16, D), F32),
                        V((16, D), F32), V((16, D), F32), V((16, D), F32),
                        V((3, 16, 64, D), BF16), V((8, 4, 64, D), BF16), V((8, 4, 64, D), BF16), V((8, 1, 64, D), BF16), V((8, 2, 8, 128), F32),
                        V((2, 4, 4, 64, D), BF16), V((2, 4, 4, 64, D), BF16), V((2, 4, 1, 64, D), BF16), V((2, 4, 2, 8, 128), F32),
                        dma((9,)), dma((2, 4)), dma((8,)), dma((2,)), dma((3, 2)), dma((5, 2, 8)), dma((6, 2, 2, 4)), dma((5, 3)), dma((3, 2)), dma((1, 2)),
                        pltpu.SemaphoreType.REGULAR((2,))],
        compiler_params=pltpu.CompilerParams(vmem_limit_bytes=67043328, collective_id=1, has_side_effects=True),
    )


def fast_body(clips, cotangent, valid, *shards):
    size = lax.axis_size("fsdp")
    me = lax.axis_index("fsdp")
    mine = lax.axis_index("seq")
    (g1, b1, wq, wk, wv, bq, bv, wp, bp, g2, b2, w1, fb1, w2, fb2) = shards
    n, m = g1.shape[0], fb1.shape[0]
    vecs = jnp.stack([g1, b1, bq, bv, bp, g2, b2, fb2])
    sml = lax.dynamic_update_slice(jnp.zeros((8, D), vecs.dtype), vecs, (0, me * n))
    fsm = lax.dynamic_update_slice(jnp.zeros((FF,), vecs.dtype), fb1, (me * m,)).reshape(-1, D)
    sml = jnp.concatenate([sml, fsm, jnp.zeros((8 - FF // D, D), vecs.dtype)])
    out, cot_in, x, sm, wqkv, wp_all, w1_all, w2_all, *saved = fwd_call(size, T, D, FF)(clips, cotangent, sml, wq, wk, wv, wp, w1, w2)
    out_in, gx, gx_in, dw2, dw2y, dw1, dw1y, dwp, dwpy, dq, dqy, sg = bwd_call(size)(
        valid, cotangent, cot_in, out, x, sm, wqkv, wp_all, w1_all, w2_all, *saved)

    def both(a, b):
        return a.astype(F32) + b.astype(F32)

    def halves(own, other):
        return jnp.where(mine == 0, jnp.stack([own, other]), jnp.stack([other, own]))

    dw2 = both(dw2, dw2y).reshape(-1, D)
    dw1 = both(dw1, dw1y).transpose(1, 0, 2).reshape(n, -1)
    dq = both(dq, dqy)
    dwp = both(dwp, dwpy)[0]
    own = lax.dynamic_slice(sg[0], (0, me % 2 * n), (8, n))
    dfb1 = lax.dynamic_slice(sg[1, 0:4].reshape(-1), (me % 2 * m,), (m,))
    out = halves(lax.dynamic_slice(out, (mine * (T // 2), 0), (T // 2, D)), out_in)
    gx = halves(gx, gx_in.astype(F32))
    return (out, gx, own[0], own[1], dq[0], dq[1], dq[2], own[2], own[3], dwp, own[4], own[5], own[6], dw1, dfb1, dw2, own[7])


def solution(mesh):
    in_specs = (
        P("fsdp", "seq", None),
        P("fsdp", "seq", None),
        P("fsdp"),
        P("fsdp"),
        P("fsdp"),
        P("fsdp", None),
        P("fsdp", None),
        P("fsdp", None),
        P("fsdp"),
        P("fsdp"),
        P("fsdp", None),
        P("fsdp"),
        P("fsdp"),
        P("fsdp"),
        P("fsdp", None),
        P("fsdp"),
        P("fsdp", None),
        P("fsdp"),
    )
    out_specs = (
        P("fsdp", "seq", None),
        P("fsdp", "seq", None),
        P("fsdp"),
        P("fsdp"),
        P("fsdp", None),
        P("fsdp", None),
        P("fsdp", None),
        P("fsdp"),
        P("fsdp"),
        P("fsdp", None),
        P("fsdp"),
        P("fsdp"),
        P("fsdp"),
        P("fsdp", None),
        P("fsdp"),
        P("fsdp", None),
        P("fsdp"),
    )
    quick = mesh.shape["seq"] == 2 and mesh.shape["fsdp"] == 16
    return jax.shard_map(fast_body if quick else body, mesh=mesh, in_specs=in_specs, out_specs=out_specs, check_vma=False)
```

```python
import functools
import jax
import jax.numpy as jnp
from jax import lax
from jax.experimental import pallas as pl
from jax.experimental.pallas import tpu as pltpu
from jax.sharding import PartitionSpec as P

H = 16
QBLK = 512


norm_eps = 1e-06
root_half = 0.7071067811865476
inv_root_tau = 0.3989422804014327


def matmul(left, right):
    return jnp.dot(left, right, preferred_element_type=jnp.float32)


def matmul_nt(left, right):
    return lax.dot_general(
        left, right, (((1,), (1,)), ((), ())), preferred_element_type=jnp.float32
    )


def matmul_tn(left, right):
    return lax.dot_general(
        left, right, (((0,), (0,)), ((), ())), preferred_element_type=jnp.float32
    )


def layer_norm(values_in, gain, shift):
    row_mean = jnp.mean(values_in, axis=-1, keepdims=True)
    centred = values_in - row_mean
    inverse = lax.rsqrt(jnp.mean(centred * centred, axis=-1, keepdims=True) + norm_eps)
    scaled = centred * inverse
    return (scaled * gain + shift, scaled, inverse)


def layer_norm_back(upstream, scaled, inverse, gain):
    dscaled = upstream * gain
    inner = (
        dscaled
        - jnp.mean(dscaled, axis=-1, keepdims=True)
        - scaled * jnp.mean(dscaled * scaled, axis=-1, keepdims=True)
    )
    return (inverse * inner, jnp.sum(upstream * scaled, axis=0), jnp.sum(upstream, axis=0))


def gelu_value(pre_act):
    return 0.5 * pre_act * (1.0 + lax.erf(pre_act * root_half))


def gelu_slope(pre_act):
    return 0.5 * (1.0 + lax.erf(pre_act * root_half)) + pre_act * inv_root_tau * jnp.exp(
        -0.5 * pre_act * pre_act
    )


def attend(queries, keys_all, values_all, head_count):
    length = queries.shape[0]
    head_width = queries.shape[1] // head_count
    score_scale = head_width ** (-0.5)
    query_heads = queries.reshape(length // QBLK, QBLK, head_count, head_width)
    key_heads = keys_all.reshape(length, head_count, head_width)
    value_heads = values_all.reshape(length, head_count, head_width)

    def one_block(query_rows):
        scores = (
            jnp.einsum("qhd,khd->hqk", query_rows, key_heads, preferred_element_type=jnp.float32)
            * score_scale
        )
        peak = jnp.max(scores, axis=-1, keepdims=True)
        raised = jnp.exp(scores - peak)
        row_total = jnp.sum(raised, axis=-1, keepdims=True)
        weights = (raised / row_total).astype(jnp.bfloat16)
        mixed = jnp.einsum("hqk,khd->qhd", weights, value_heads, preferred_element_type=jnp.float32)
        return (mixed.astype(jnp.bfloat16), (peak + jnp.log(row_total))[:, :, 0])

    mixed, log_totals = lax.map(one_block, query_heads)
    return (mixed.reshape(length, head_count * head_width), log_totals)


def attend_back(queries, keys_all, values_all, log_totals, upstream, head_count):
    length = queries.shape[0]
    head_width = queries.shape[1] // head_count
    score_scale = head_width ** (-0.5)
    query_heads = queries.reshape(length // QBLK, QBLK, head_count, head_width)
    upstream_heads = upstream.reshape(length // QBLK, QBLK, head_count, head_width)
    key_heads = keys_all.reshape(length, head_count, head_width)
    value_heads = values_all.reshape(length, head_count, head_width)

    def one_block(running, block_item):
        key_grad, value_grad = running
        query_rows, log_rows, grad_rows = block_item
        scores = (
            jnp.einsum("qhd,khd->hqk", query_rows, key_heads, preferred_element_type=jnp.float32)
            * score_scale
        )
        weights = jnp.exp(scores - log_rows[:, :, None])
        weights_low = weights.astype(jnp.bfloat16)
        grad_weights = jnp.einsum(
            "qhd,khd->hqk", grad_rows, value_heads, preferred_element_type=jnp.float32
        )
        inner = jnp.sum(grad_weights * weights, axis=-1, keepdims=True)
        grad_scores = (weights * (grad_weights - inner)).astype(jnp.bfloat16)
        query_grad = (
            jnp.einsum("hqk,khd->qhd", grad_scores, key_heads, preferred_element_type=jnp.float32)
            * score_scale
        )
        key_grad = (
            key_grad
            + jnp.einsum(
                "hqk,qhd->khd", grad_scores, query_rows, preferred_element_type=jnp.float32
            )
            * score_scale
        )
        value_grad = value_grad + jnp.einsum(
            "hqk,qhd->khd", weights_low, grad_rows, preferred_element_type=jnp.float32
        )
        return ((key_grad, value_grad), query_grad.astype(jnp.bfloat16))

    zeros_heads = jnp.zeros((length, head_count, head_width), jnp.float32)
    (key_grad, value_grad), query_grad = lax.scan(
        one_block, (zeros_heads, zeros_heads), (query_heads, log_totals, upstream_heads)
    )
    width_all = head_count * head_width
    return (
        query_grad.reshape(length, width_all),
        key_grad.reshape(length, width_all).astype(jnp.bfloat16),
        value_grad.reshape(length, width_all).astype(jnp.bfloat16),
    )


def fetch(shards):
    return (
        lax.all_gather(shards[0], "fsdp", axis=0, tiled=True),
        lax.all_gather(shards[1], "fsdp", axis=0, tiled=True),
        lax.all_gather(shards[2], "fsdp", axis=0, tiled=True),
        lax.all_gather(shards[3], "fsdp", axis=0, tiled=True),
        lax.all_gather(shards[4], "fsdp", axis=0, tiled=True),
        lax.all_gather(shards[5], "fsdp", axis=0, tiled=True),
        lax.all_gather(shards[6], "fsdp", axis=0, tiled=True),
        lax.all_gather(shards[7], "fsdp", axis=0, tiled=True),
        lax.all_gather(shards[8], "fsdp", axis=0, tiled=True),
        lax.all_gather(shards[9], "fsdp", axis=0, tiled=True),
        lax.all_gather(shards[10], "fsdp", axis=0, tiled=True),
        lax.all_gather(shards[11], "fsdp", axis=0, tiled=True),
        lax.all_gather(shards[12], "fsdp", axis=0, tiled=True),
        lax.all_gather(shards[13], "fsdp", axis=0, tiled=True),
        lax.all_gather(shards[14], "fsdp", axis=0, tiled=True),
    )


def settle(grads):
    shares = (
        lax.psum_scatter(
            grads[0].astype(jnp.bfloat16), "fsdp", scatter_dimension=0, tiled=True
        ).astype(jnp.float32),
        lax.psum_scatter(
            grads[1].astype(jnp.bfloat16), "fsdp", scatter_dimension=0, tiled=True
        ).astype(jnp.float32),
        lax.psum_scatter(
            grads[2].astype(jnp.bfloat16), "fsdp", scatter_dimension=0, tiled=True
        ).astype(jnp.float32),
        lax.psum_scatter(
            grads[3].astype(jnp.bfloat16), "fsdp", scatter_dimension=0, tiled=True
        ).astype(jnp.float32),
        lax.psum_scatter(
            grads[4].astype(jnp.bfloat16), "fsdp", scatter_dimension=0, tiled=True
        ).astype(jnp.float32),
        lax.psum_scatter(
            grads[5].astype(jnp.bfloat16), "fsdp", scatter_dimension=0, tiled=True
        ).astype(jnp.float32),
        lax.psum_scatter(
            grads[6].astype(jnp.bfloat16), "fsdp", scatter_dimension=0, tiled=True
        ).astype(jnp.float32),
        lax.psum_scatter(
            grads[7].astype(jnp.bfloat16), "fsdp", scatter_dimension=0, tiled=True
        ).astype(jnp.float32),
        lax.psum_scatter(
            grads[8].astype(jnp.bfloat16), "fsdp", scatter_dimension=0, tiled=True
        ).astype(jnp.float32),
        lax.psum_scatter(
            grads[9].astype(jnp.bfloat16), "fsdp", scatter_dimension=0, tiled=True
        ).astype(jnp.float32),
        lax.psum_scatter(
            grads[10].astype(jnp.bfloat16), "fsdp", scatter_dimension=0, tiled=True
        ).astype(jnp.float32),
        lax.psum_scatter(
            grads[11].astype(jnp.bfloat16), "fsdp", scatter_dimension=0, tiled=True
        ).astype(jnp.float32),
        lax.psum_scatter(
            grads[12].astype(jnp.bfloat16), "fsdp", scatter_dimension=0, tiled=True
        ).astype(jnp.float32),
        lax.psum_scatter(
            grads[13].astype(jnp.bfloat16), "fsdp", scatter_dimension=0, tiled=True
        ).astype(jnp.float32),
        lax.psum_scatter(
            grads[14].astype(jnp.bfloat16), "fsdp", scatter_dimension=0, tiled=True
        ).astype(jnp.float32),
    )
    return (
        lax.psum(shares[0].astype(jnp.bfloat16), "seq").astype(jnp.float32),
        lax.psum(shares[1].astype(jnp.bfloat16), "seq").astype(jnp.float32),
        lax.psum(shares[2].astype(jnp.bfloat16), "seq").astype(jnp.float32),
        lax.psum(shares[3].astype(jnp.bfloat16), "seq").astype(jnp.float32),
        lax.psum(shares[4].astype(jnp.bfloat16), "seq").astype(jnp.float32),
        lax.psum(shares[5].astype(jnp.bfloat16), "seq").astype(jnp.float32),
        lax.psum(shares[6].astype(jnp.bfloat16), "seq").astype(jnp.float32),
        lax.psum(shares[7].astype(jnp.bfloat16), "seq").astype(jnp.float32),
        lax.psum(shares[8].astype(jnp.bfloat16), "seq").astype(jnp.float32),
        lax.psum(shares[9].astype(jnp.bfloat16), "seq").astype(jnp.float32),
        lax.psum(shares[10].astype(jnp.bfloat16), "seq").astype(jnp.float32),
        lax.psum(shares[11].astype(jnp.bfloat16), "seq").astype(jnp.float32),
        lax.psum(shares[12].astype(jnp.bfloat16), "seq").astype(jnp.float32),
        lax.psum(shares[13].astype(jnp.bfloat16), "seq").astype(jnp.float32),
        lax.psum(shares[14].astype(jnp.bfloat16), "seq").astype(jnp.float32),
    )


def one_clip(clip_in, clip_cot, clip_flag, gathered, head_count):
    (
        norm1_gain,
        norm1_bias,
        query_weight,
        key_weight,
        value_weight,
        query_bias,
        value_bias,
        proj_weight,
        proj_bias,
        norm2_gain,
        norm2_bias,
        fc1_weight,
        fc1_bias,
        fc2_weight,
        fc2_bias,
    ) = gathered
    gain_one = norm1_gain.astype(jnp.float32)
    gain_two = norm2_gain.astype(jnp.float32)
    tokens_in = clip_in.astype(jnp.float32)
    normed, scaled_one, inverse_one = layer_norm(
        tokens_in, gain_one, norm1_bias.astype(jnp.float32)
    )
    normed_low = normed.astype(jnp.bfloat16)
    queries = (matmul(normed_low, query_weight) + query_bias.astype(jnp.float32)).astype(
        jnp.bfloat16
    )
    keys_all = matmul(normed_low, key_weight).astype(jnp.bfloat16)
    values_all = (matmul(normed_low, value_weight) + value_bias.astype(jnp.float32)).astype(
        jnp.bfloat16
    )
    query_heads, key_heads, value_heads = (
        lax.all_to_all(queries, "seq", split_axis=1, concat_axis=0, tiled=True),
        lax.all_to_all(keys_all, "seq", split_axis=1, concat_axis=0, tiled=True),
        lax.all_to_all(values_all, "seq", split_axis=1, concat_axis=0, tiled=True),
    )
    mixed_heads, log_totals = attend(query_heads, key_heads, value_heads, head_count)
    attended = lax.all_to_all(mixed_heads, "seq", split_axis=0, concat_axis=1, tiled=True)
    middle = tokens_in + matmul(attended, proj_weight) + proj_bias.astype(jnp.float32)
    normed_two, scaled_two, inverse_two = layer_norm(
        middle, gain_two, norm2_bias.astype(jnp.float32)
    )
    normed_two_low = normed_two.astype(jnp.bfloat16)
    hidden_pre = matmul(normed_two_low, fc1_weight) + fc1_bias.astype(jnp.float32)
    hidden_low = gelu_value(hidden_pre).astype(jnp.bfloat16)
    output = middle + matmul(hidden_low, fc2_weight) + fc2_bias.astype(jnp.float32)
    grad_out = clip_cot.astype(jnp.float32) * clip_flag.astype(jnp.float32)
    grad_mlp = grad_out.astype(jnp.bfloat16)
    grad_fc2_weight = matmul_tn(hidden_low, grad_mlp)
    grad_fc2_bias = jnp.sum(grad_mlp.astype(jnp.float32), axis=0)
    grad_pre = (matmul_nt(grad_mlp, fc2_weight) * gelu_slope(hidden_pre)).astype(jnp.bfloat16)
    grad_fc1_weight = matmul_tn(normed_two_low, grad_pre)
    grad_fc1_bias = jnp.sum(grad_pre.astype(jnp.float32), axis=0)
    grad_norm_two = matmul_nt(grad_pre, fc1_weight)
    grad_ln_two, grad_norm2_gain, grad_norm2_bias = layer_norm_back(
        grad_norm_two, scaled_two, inverse_two, gain_two
    )
    grad_middle = grad_out + grad_ln_two
    grad_branch = grad_middle.astype(jnp.bfloat16)
    grad_proj_weight = matmul_tn(attended, grad_branch)
    grad_proj_bias = jnp.sum(grad_branch.astype(jnp.float32), axis=0)
    grad_att = matmul_nt(grad_branch, proj_weight).astype(jnp.bfloat16)
    grad_att_heads = lax.all_to_all(grad_att, "seq", split_axis=1, concat_axis=0, tiled=True)
    query_grad, key_grad, value_grad = attend_back(
        query_heads, key_heads, value_heads, log_totals, grad_att_heads, head_count
    )
    grad_queries, grad_keys, grad_values = (
        lax.all_to_all(query_grad, "seq", split_axis=0, concat_axis=1, tiled=True),
        lax.all_to_all(key_grad, "seq", split_axis=0, concat_axis=1, tiled=True),
        lax.all_to_all(value_grad, "seq", split_axis=0, concat_axis=1, tiled=True),
    )
    grad_query_weight = matmul_tn(normed_low, grad_queries)
    grad_key_weight = matmul_tn(normed_low, grad_keys)
    grad_value_weight = matmul_tn(normed_low, grad_values)
    grad_query_bias = jnp.sum(grad_queries.astype(jnp.float32), axis=0)
    grad_value_bias = jnp.sum(grad_values.astype(jnp.float32), axis=0)
    grad_norm_one = (
        matmul_nt(grad_queries, query_weight)
        + matmul_nt(grad_keys, key_weight)
        + matmul_nt(grad_values, value_weight)
    )
    grad_ln_one, grad_norm1_gain, grad_norm1_bias = layer_norm_back(
        grad_norm_one, scaled_one, inverse_one, gain_one
    )
    grad_in = grad_middle + grad_ln_one
    grads = (
        grad_norm1_gain,
        grad_norm1_bias,
        grad_query_weight,
        grad_key_weight,
        grad_value_weight,
        grad_query_bias,
        grad_value_bias,
        grad_proj_weight,
        grad_proj_bias,
        grad_norm2_gain,
        grad_norm2_bias,
        grad_fc1_weight,
        grad_fc1_bias,
        grad_fc2_weight,
        grad_fc2_bias,
    )
    return (output.astype(jnp.bfloat16), grad_in, grads)


def body(
    clips,
    cotangent,
    valid,
    norm1_gain,
    norm1_bias,
    query_weight,
    key_weight,
    value_weight,
    query_bias,
    value_bias,
    proj_weight,
    proj_bias,
    norm2_gain,
    norm2_bias,
    fc1_weight,
    fc1_bias,
    fc2_weight,
    fc2_bias,
):
    shards = (
        norm1_gain,
        norm1_bias,
        query_weight,
        key_weight,
        value_weight,
        query_bias,
        value_bias,
        proj_weight,
        proj_bias,
        norm2_gain,
        norm2_bias,
        fc1_weight,
        fc1_bias,
        fc2_weight,
        fc2_bias,
    )
    slot_count = clips.shape[0]
    head_count = H // lax.axis_size("seq")
    summed = None
    outputs = []
    grad_list = []
    for batch_slot in range(slot_count):
        gathered = fetch(shards)
        output, grad_in, grads = one_clip(
            clips[batch_slot], cotangent[batch_slot], valid[batch_slot], gathered, head_count
        )
        summed = (
            grads
            if summed is None
            else tuple((older + newer for older, newer in zip(summed, grads)))
        )
        outputs.append(output)
        grad_list.append(grad_in)
    summed = settle(summed)
    return (
        jnp.stack(outputs),
        jnp.stack(grad_list),
        summed[0],
        summed[1],
        summed[2],
        summed[3],
        summed[4],
        summed[5],
        summed[6],
        summed[7],
        summed[8],
        summed[9],
        summed[10],
        summed[11],
        summed[12],
        summed[13],
        summed[14],
    )


T, D, FF, NTILE = 1024, 1024, 4096, 8

log2_e = 1.4426950408889634
HD = 64
F32, BF16 = jnp.float32, jnp.bfloat16
ANY = pl.BlockSpec(memory_space=pl.ANY)


def dot(left, right, cl=1, cr=0):
    return lax.dot_general(left, right, (((cl,), (cr,)), ((), ())), preferred_element_type=F32)


def split3(v):
    hi = v.astype(BF16)
    r = v - hi.astype(F32)
    md = r.astype(BF16)
    lo = (r - md.astype(F32)).astype(BF16)
    return hi, md, lo


def aug_rows(v):
    hi, md, lo = split3(v)
    z = jnp.zeros((13, v.shape[1]), BF16)
    return jnp.concatenate([hi, md, lo, z], axis=0)


def ln_back(up, v, gain):
    m = jnp.mean(v, axis=-1, keepdims=True)
    d = v - m
    r = lax.rsqrt(jnp.mean(d * d, axis=-1, keepdims=True) + norm_eps)
    xh = d * r
    s = up * gain
    back = r * (s - jnp.mean(s, axis=-1, keepdims=True) - xh * jnp.mean(s * xh, axis=-1, keepdims=True))
    return back, jnp.sum(up * xh, axis=0, keepdims=True), jnp.sum(up, axis=0, keepdims=True)


def bwd_head(h, qkvt, ot, dot_v, lse_v):
    T = ot.shape[1]
    qb = T // 2
    scale = HD ** -0.5
    r = pl.multiple_of(h * HD, HD)
    rows = pl.ds(r, HD)
    ones = jnp.ones((16, T), BF16)
    kh = qkvt[1, rows, :]
    ka = jnp.concatenate([kh, ones], axis=0)
    va = jnp.concatenate([qkvt[2, rows, :], ones], axis=0)
    dk = dv = None
    for b in range(2):
        cols = slice(b * qb, (b + 1) * qb)
        qh = qkvt[0, rows, cols] * jnp.asarray(scale, BF16)
        do = dot_v[rows, cols]
        delta = jnp.sum(do.astype(F32) * ot[rows, cols].astype(F32), axis=0, keepdims=True)
        qa = jnp.concatenate([qh, aug_rows(-lse_v[pl.ds(h, 1), cols])], axis=0)
        da = jnp.concatenate([do, aug_rows(-delta)], axis=0)
        p = jnp.exp2(dot(qa, ka, 0, 0) * log2_e)
        ds = (p * dot(da, va, 0, 0)).astype(BF16)
        ndv = dot(do, p.astype(BF16))
        ndk = dot(qh, ds)
        dv = ndv if dv is None else dv + ndv
        dk = ndk if dk is None else dk + ndk
        qkvt[0, rows, cols] = (dot(kh, ds, 1, 1) * scale).astype(BF16)
    qkvt[1, rows, :] = dk.astype(BF16)
    qkvt[2, rows, :] = dv.astype(BF16)


MESH = pl.DeviceIdType.MESH


class Place:
    def __init__(self, size):
        f = lax.axis_index("fsdp")
        self.f, self.core, chip = f, f % 2, f // 2
        self.deep, self.count = size // 4, size // 2
        x, z = chip % 2, chip // 2
        self.pos = z + x * (2 * self.deep - 1 - 2 * z)
        self.mate = f + 1 - 2 * self.core
        self.y = lax.axis_index("seq")

    def chip(self, off):
        pos = (self.pos + self.count + off) % self.count
        hi = pos // self.deep
        return 2 * (pos + hi * (2 * self.deep - 1 - 2 * pos)) + hi

    def side(self, d):
        return {"fsdp": 2 * self.chip((1, -1)[d]) + self.core}

    def partner(self):
        return {"fsdp": self.mate}

    def across(self):
        return {"seq": 1 - self.y}

    def barrier(self):
        sem = pltpu.get_barrier_semaphore()
        for dev in (self.side(0), self.side(1), self.partner(), self.across()):
            pl.semaphore_signal(sem, inc=1, device_id=dev, device_id_type=MESH)
        pl.semaphore_wait(sem, 4)


def remote(src, dst, ss, rs, dev):
    return pltpu.make_async_remote_copy(src_ref=src, dst_ref=dst, send_sem=ss, recv_sem=rs, device_id=dev, device_id_type=MESH)


class Gather:
    def __init__(self, place, view, rsem, psem):
        self.pl, self.view, self.rsem, self.psem = place, view, rsem, psem
        self.last = place.count // 2 - 1

    def part(self, d, s):
        return d if s == self.last else 2

    def block(self, d, s, ahead):
        k = s + ahead
        return self.pl.chip(-k if d == 0 else k)

    def ring(self, d, s, ahead=0):
        v = self.view(2 * self.block(d, s, ahead) + self.pl.core, self.part(d, s))
        return remote(v, v, self.rsem.at[0, d, s], self.rsem.at[1, d, s], self.pl.side(d))

    def mate(self, slot, chip, part, core):
        v = self.view(2 * chip + core, part)
        return remote(v, v, self.psem.at[0, slot], self.psem.at[1, slot], self.pl.partner())

    def slots(self, s):
        return [(1 + 2 * s + d, self.block(d, s, 1), self.part(d, s)) for d in range(2)]

    def start(self):
        for d in range(2):
            self.ring(d, 0).start()
        self.mate(0, self.pl.chip(0), 2, self.pl.core).start()

    def step(self, s):
        for d in range(2):
            self.ring(d, s, 1).wait_recv()
            if s < self.last:
                self.ring(d, s + 1).start()
        for slot, chip, part in self.slots(s):
            self.mate(slot, chip, part, self.pl.core).start()

    def own_mate(self):
        self.mate(0, self.pl.chip(0), 2, 1 - self.pl.core).wait_recv()

    def step_mate(self, s):
        for slot, chip, part in self.slots(s):
            self.mate(slot, chip, part, 1 - self.pl.core).wait_recv()

    def all_mates(self):
        self.own_mate()
        for s in range(self.last + 1):
            self.step_mate(s)

    def drain(self):
        for s in range(self.last + 1):
            for d in range(2):
                self.ring(d, s).wait_send()
            for slot, chip, part in self.slots(s):
                self.mate(slot, chip, part, self.pl.core).wait_send()
        self.mate(0, self.pl.chip(0), 2, self.pl.core).wait_send()


class GatherY(Gather):
    def __init__(self, place, half, whole, rsem, psem, qsem, asem):
        super().__init__(place, lambda f, part: half(f, part, place.y), rsem, psem)
        self.half, self.whole, self.qsem, self.asem = half, whole, qsem, asem

    def mate(self, slot, chip, part, core):
        if slot:
            return super().mate(slot, chip, part, core)
        v = self.whole(2 * chip + core)
        return remote(v, v, self.psem.at[0, 0], self.psem.at[1, 0], self.pl.partner())

    def over(self, slot, chip, part, y):
        v = self.half(2 * chip + self.pl.core, part, y)
        return remote(v, v, self.asem.at[0, slot], self.asem.at[1, slot], self.pl.across())

    def relay(self, slot, chip, part, core):
        v = self.half(2 * chip + core, part, 1 - self.pl.y)
        return remote(v, v, self.qsem.at[0, slot], self.qsem.at[1, slot], self.pl.partner())

    def step(self, s):
        for d in range(2):
            self.ring(d, s, 1).wait_recv()
            if s < self.last:
                self.ring(d, s + 1).start()
        for slot, chip, part in self.slots(s):
            self.over(slot, chip, part, self.pl.y).start()
            self.mate(slot, chip, part, self.pl.core).start()

    def step_over(self, s):
        for slot, chip, part in self.slots(s):
            self.over(slot, chip, part, 1 - self.pl.y).wait_recv()
            self.relay(slot, chip, part, self.pl.core).start()

    def step_mate(self, s):
        super().step_mate(s)
        for slot, chip, part in self.slots(s):
            self.relay(slot, chip, part, 1 - self.pl.core).wait_recv()

    def drain(self):
        super().drain()
        for s in range(self.last + 1):
            for slot, chip, part in self.slots(s):
                self.over(slot, chip, part, self.pl.y).wait_send()
                self.relay(slot, chip, part, self.pl.core).wait_send()


def fwd_body(size, clips, cot, sml, wq, wk, wv, wp, w1, w2,
             out_o, cot_o, x_o, sm_o, wqkv_o, wp_o, w1_o, w2_o, n1t_o, qkvt_o, ot_o, lse_o, mid_o, n2_o, h_o, g_o,
             x_v, smb, sm_v, wqkv_v, wp_v, w1_v, w2_v, n1t, qkvt, ot, lse_v, mid, n2, acc, hst, gst, b1_v, smt,
             rsem, psem, qsem, asem, xsem, lsem, osem, tsem):
    here = Place(size)
    T, D = x_v.shape
    FF = w1_v.shape[1]
    tile = hst.shape[2]
    heads = D // HD
    half = T // 2
    nd, nf = D // size, FF // size
    y = here.y
    ymine = pl.ds(pl.multiple_of(y * half, half), half)
    yother = pl.ds(pl.multiple_of((1 - y) * half, half), half)

    def local(a, b, i):
        return pltpu.make_async_copy(a, b, lsem.at[i])

    def rows(ref, n, lead):
        def view(f, part):
            k = n if part == 2 else n // 2
            at = pl.ds(pl.multiple_of(f * n + (n // 2 if part == 1 else 0), k), k)
            return ref.at[:, at, :] if lead else ref.at[at, :]
        return view

    def smview(f, part):
        if part == 2:
            return smb.at[f]
        return smb.at[f, :, part * (D // 2):(part + 1) * (D // 2)]

    def part_rows(ref, n, c0, w):
        def half_view(f, part, yy):
            k = n if part == 2 else n // 2
            at = pl.ds(pl.multiple_of(f * n + (n // 2 if part == 1 else 0), k), k)
            return ref.at[at, pl.ds(pl.multiple_of(c0 + yy * (w // 2), w // 2), w // 2)]

        def whole_view(f):
            return ref.at[pl.ds(pl.multiple_of(f * n, n), n), c0:c0 + w]

        return half_view, whole_view

    def first_rows(f, part):
        return rows(w1_v, nd, False)(f, part).at[:, 0:FF // 2]

    views = [smview, rows(wqkv_v, nd, True), rows(wp_v, nd, False), first_rows]
    ga, gq, gp, g1 = [Gather(here, v, rsem.at[i], psem.at[i]) for i, v in enumerate(views)]
    g3 = GatherY(here, *part_rows(w1_v, nd, FF // 2, FF // 2), rsem.at[4], psem.at[4], qsem.at[0], asem.at[0])
    g2 = GatherY(here, *part_rows(w2_v, nf, 0, D), rsem.at[5], psem.at[5], qsem.at[1], asem.at[1])
    own = pl.ds(pl.multiple_of(here.f * nd, nd), nd)
    ownf = pl.ds(pl.multiple_of(here.f * nf, nf), nf)
    loc = [local(sml, smb.at[here.f], 0)]
    loc += [local(w, wqkv_v.at[j, own, :], 1 + j) for j, w in enumerate((wq, wk, wv))]
    loc += [local(wp, wp_v.at[own, :], 4), local(w1, w1_v.at[own, :], 5), local(w2, w2_v.at[ownf, :], 6), local(clips.at[y], x_v.at[ymine, :], 7)]
    for c in loc:
        c.start()
    here.barrier()
    xsend = remote(clips.at[1 - y], x_v.at[ymine, :], xsem.at[0, 0], xsem.at[0, 1], here.across())
    xrecv = remote(clips.at[1 - y], x_v.at[yother, :], xsem.at[0, 0], xsem.at[0, 1], here.across())
    csend = remote(cot.at[1 - y], cot_o, xsem.at[1, 0], xsem.at[1, 1], here.across())
    xsend.start()
    csend.start()
    for c in loc[:4]:
        c.wait()
    ga.start()
    gq.start()
    for c in loc[4:]:
        c.wait()

    def ln1(i, c):
        r = pl.multiple_of(i * 256, 256)
        v = x_v[pl.ds(r, 256), :].astype(F32)
        m = jnp.mean(v, axis=-1, keepdims=True)
        d = v - m
        mid[pl.ds(r, 256), :] = d * lax.rsqrt(jnp.mean(d * d, axis=-1, keepdims=True) + norm_eps)
        return c

    per = half // 256
    lax.fori_loop(y * per, y * per + per, ln1, 0)
    for s in range(ga.last + 1):
        ga.step(s)
        gq.step(s)
        if s == ga.last - 1:
            gp.start()
            g1.start()
            g3.start()
    xrecv.wait_recv()
    lax.fori_loop((1 - y) * per, (1 - y) * per + per, ln1, 0)
    ga.all_mates()
    sm_v[...] = jnp.sum(smb[...].astype(F32), axis=0)
    smt[...] = jnp.transpose(sm_v[...])

    def ln1b(i, c):
        r = pl.multiple_of(i * 256, 256)
        n1t[:, pl.ds(r, 256)] = jnp.transpose((mid[pl.ds(r, 256), :] * sm_v[0:1, :] + sm_v[1:2, :]).astype(BF16))
        return c

    lax.fori_loop(0, T // 256, ln1b, 0)
    gq.all_mates()
    outs = []

    def save(a, b):
        c = pltpu.make_async_copy(a, b, osem.at[len(outs)])
        outs.append(c)
        c.start()

    save(wqkv_v, wqkv_o)
    save(x_v, x_o)
    save(sm_v, sm_o)
    save(n1t, n1t_o)
    hd = D // 2
    for j in range(3):
        for o in range(2):
            v = dot(wqkv_v[j, :, o * hd:(o + 1) * hd], n1t[...], 0, 0)
            if j != 1:
                v = v + smt[o * hd:(o + 1) * hd, (2 if j == 0 else 3):(3 if j == 0 else 4)]
            qkvt[j, o * hd:(o + 1) * hd, :] = v.astype(BF16)
    save(qkvt, qkvt_o)
    qb = T // 2
    ones = jnp.ones((16, T), BF16)

    def head(h, c):
        r = pl.multiple_of(h * HD, HD)
        kh = qkvt[1, pl.ds(r, HD), :]
        vh = jnp.concatenate([qkvt[2, pl.ds(r, HD), :], ones], axis=0)
        for b in range(2):
            qh = qkvt[0, pl.ds(r, HD), b * qb:(b + 1) * qb]
            s = dot(kh, qh, 0, 0)
            m = jnp.max(s, axis=0, keepdims=True)
            p = jnp.exp2((s - m) * (log2_e * HD ** -0.5)).astype(BF16)
            o = dot(vh, p)
            total = o[HD:HD + 1, :]
            ot[pl.ds(r, HD), b * qb:(b + 1) * qb] = (o[:HD, :] / total).astype(BF16)
            lse_v[pl.ds(h, 1), b * qb:(b + 1) * qb] = m * HD ** -0.5 + jnp.log(total)
        for s, n in enumerate((2, 8, 14)):
            @pl.when(h == n)
            def _(s=s):
                gp.step(s)
                g1.step(s)
                g3.step(s)
                if s:
                    g3.step_over(s - 1)
                if s == 2:
                    g2.start()
        return c

    lax.fori_loop(0, heads, head, 0)
    save(ot, ot_o)
    save(lse_v, lse_o)
    for s in range(3, gp.last + 1):
        gp.step(s)
    gp.all_mates()
    save(wp_v, wp_o)

    def proj(i, c):
        r = pl.multiple_of(i * 512, 512)
        v = dot(ot[:, pl.ds(r, 512)], wp_v[...], 0, 0) + x_v[pl.ds(r, 512), :].astype(F32) + sm_v[4:5, :]
        mid[pl.ds(r, 512), :] = v
        m = jnp.mean(v, axis=-1, keepdims=True)
        d = v - m
        s = d * lax.rsqrt(jnp.mean(d * d, axis=-1, keepdims=True) + norm_eps)
        n2[pl.ds(r, 512), :] = (s * sm_v[5:6, :] + sm_v[6:7, :]).astype(BF16)
        acc[pl.ds(r, 512), :] = v + sm_v[7:8, :]
        return c

    lax.fori_loop(0, T // 512, proj, 0)
    save(mid, mid_o)
    save(n2, n2_o)
    for k in range(FF // tile):
        kk = k * tile
        b1_v[k:k + 1, :] = sm_v[8 + kk // D:9 + kk // D, kk % D:kk % D + tile]
    for s in range(3, g1.last + 1):
        g1.step(s)
        g3.step(s)
        g3.step_over(s - 1)
    g3.step_over(g3.last)
    g2.step(0)
    g1.all_mates()
    g3.all_mates()
    g2.own_mate()
    save(w1_v, w1_o)
    saves = {}
    order = [0]
    for k in range(1, here.count // 2):
        order += [-k, k]
    order.append(here.count // 2)

    def tcp(k, slot, t):
        return pltpu.make_async_copy((hst, gst)[k].at[slot], (h_o, g_o)[k].at[t], tsem.at[k, slot])

    def wcp(j, t):
        at = pl.ds(pl.multiple_of(t * tile, tile), tile)
        return pltpu.make_async_copy(w2_v.at[at, :], w2_o.at[at, :], tsem.at[2, j])

    for j, off in enumerate(order):
        t = here.chip(off)
        slot = j % 2
        if j % 2 == 1:
            g2.step_over(j // 2)
            if j // 2 < g2.last:
                g2.step(j // 2 + 1)
            g2.step_mate(j // 2)
        wcp(j, t).start()
        if j >= 2:
            for k in range(2):
                tcp(k, slot, here.chip(order[j - 2])).wait()
        col = pl.multiple_of(t * tile, tile)

        def mlp(i, c, t=t, slot=slot, col=col):
            r = pl.multiple_of(i * 512, 512)
            u = dot(n2[pl.ds(r, 512), :], w1_v[:, pl.ds(col, tile)]) + b1_v[pl.ds(t, 1), :]
            cdf = 0.5 + 0.5 * lax.erf(u * root_half)
            hb = (u * cdf).astype(BF16)
            hst[slot, pl.ds(r, 512), :] = hb
            gst[slot, pl.ds(r, 512), :] = (cdf + (u * inv_root_tau) * jnp.exp2(u * u * (-0.5 * log2_e))).astype(BF16)
            acc[pl.ds(r, 512), :] += dot(hb, w2_v[pl.ds(col, tile), :])
            return c

        lax.fori_loop(0, T // 512, mlp, 0)
        for k in range(2):
            tcp(k, slot, t).start()
    for j in range(len(order) - 2, len(order)):
        for k in range(2):
            tcp(k, j % 2, here.chip(order[j])).wait()
    outs[3].wait()
    n1t[...] = acc[...].astype(BF16)
    save(n1t, out_o)
    for j, off in enumerate(order):
        wcp(j, here.chip(off)).wait()
    for i, c in enumerate(outs):
        if i != 3:
            c.wait()
    for g in (ga, gq, gp, g1, g3, g2):
        g.drain()
    xsend.wait_send()
    csend.wait_send()
    remote(cot.at[1 - y], cot_o, xsem.at[1, 0], xsem.at[1, 1], here.across()).wait_recv()


S = jax.ShapeDtypeStruct
V = pltpu.VMEM


def fwd_call(size, T, D, FF):
    tile = 2 * FF // size
    heads = D // HD
    small = (16, D)
    dma = pltpu.SemaphoreType.DMA
    steps = size // 4
    return pl.pallas_call(
        functools.partial(fwd_body, size),
        name="forward",
        in_specs=[ANY] * 9,
        out_specs=[ANY] * 16,
        out_shape=[S((T, D), BF16), S((T // 2, D), BF16), S((T, D), BF16), S(small, F32), S((3, D, D), BF16), S((D, D), BF16), S((D, FF), BF16), S((FF, D), BF16),
                   S((D, T), BF16), S((3, D, T), BF16), S((D, T), BF16), S((heads, T), F32), S((T, D), F32), S((T, D), BF16), S((FF // tile, T, tile), BF16), S((FF // tile, T, tile), BF16)],
        scratch_shapes=[V((T, D), BF16), V((size,) + small, BF16), V(small, F32), V((3, D, D), BF16), V((D, D), BF16), V((D, FF), BF16), V((FF, D), BF16),
                        V((D, T), BF16), V((3, D, T), BF16), V((D, T), BF16), V((heads, T), F32), V((T, D), F32), V((T, D), BF16), V((T, D), F32),
                        V((2, T, tile), BF16), V((2, T, tile), BF16), V((FF // tile, tile), F32), V((D, 16), F32),
                        dma((6, 2, 2, steps)), dma((6, 2, 2 * steps + 1)), dma((2, 2, 2 * steps + 1)), dma((2, 2, 2 * steps + 1)), dma((2, 2)), dma((8,)), dma((12,)), dma((3, max(2, FF // tile)))],
        compiler_params=pltpu.CompilerParams(vmem_limit_bytes=63 << 20, collective_id=0, has_side_effects=True),
    )


def fold(dst, *srcs):
    def one(q, c):
        if len(srcs) == 1:
            dst[q] = dst[q] + srcs[0][q]
            return c
        v = dst[q].astype(F32)
        for s in srcs:
            v = v + s[q].astype(F32)
        dst[q] = v.astype(dst.dtype)
        return c

    lax.fori_loop(0, dst.shape[0], one, 0)


def offset(j):
    odd = j % 2
    return odd * ((7 - j) // 2) - (1 - odd) * ((8 - j) // 2)


class Scatter:
    def __init__(self, here, land, rb, n, cols, msem, rsem, ysem, fin_o=None, y_o=None):
        self.pl, self.land, self.rb, self.n, self.cols = here, land, rb, n, cols
        self.msem, self.rsem, self.ysem, self.fin_o, self.y_o = msem, rsem, ysem, fin_o, y_o

    def cut(self, part):
        c0, w = self.cols
        return slice(c0, c0 + w) if part == 2 else slice(c0 + part * (w // 2), c0 + (part + 1) * (w // 2))

    def block(self, j, part=2):
        return self.land.at[j, 0:self.n, :, self.cut(part)]

    def came(self, d, s):
        return self.rb.at[d, s, 0:self.n, :, self.cut(d if s == 0 else 2)]

    def mate(self, j, src=None):
        dst = self.block(j)
        return remote(dst if src is None else src.at[:, :, self.cut(2)], dst, self.msem.at[0, j], self.msem.at[1, j], self.pl.partner())

    def settle(self, j, own):
        self.mate(j).wait_recv()
        fold(self.block(j), own.at[:, :, self.cut(2)])
        self.mate(j).wait_send()

    def ring(self, d, s):
        src = self.block(0, d) if s == 0 else self.block(2 * s - 1 + d)
        return remote(src, self.came(d, s), self.rsem.at[0, d, s], self.rsem.at[1, d, s], self.pl.side(d))

    def step(self, s):
        for d in range(2):
            if s:
                self.ring(d, s - 1).wait_recv()
                fold(self.block(2 * s - 1 + d, d if s == 1 else 2), self.came(d, s - 1))
            self.ring(d, s).start()

    def close(self):
        for d in range(2):
            self.ring(d, 3).wait_recv()
        fold(self.block(7), self.came(0, 3), self.came(1, 3))

    def view(self, ref):
        return ref.at[0:self.n, :, self.cut(2)]

    def over(self):
        return remote(self.block(7), self.view(self.y_o), self.ysem.at[0], self.ysem.at[1], self.pl.across())

    def keep(self):
        return pltpu.make_async_copy(self.block(7), self.view(self.fin_o), self.ysem.at[2])

    def finish(self):
        self.close()
        self.over().start()
        self.keep().start()

    def drain_ring(self):
        for s in range(4):
            for d in range(2):
                self.ring(d, s).wait_send()

    def drain(self):
        self.drain_ring()
        self.over().wait_send()
        self.keep().wait()


class Group:
    def __init__(self, *parts):
        self.parts = parts

    def send(self, j, src):
        for p in self.parts:
            p.mate(j, src).start()

    def settle(self, j, own):
        for p in self.parts:
            p.settle(j, own)

    def step(self, s):
        for p in self.parts:
            p.step(s)

    def finish(self):
        for p in self.parts:
            p.finish()

    def drain(self):
        for p in self.parts:
            p.drain()

    def arrive(self):
        for p in self.parts:
            p.over().wait_recv()


def bwd_body(size, valid, cotangent, cot_in, out, x, sm, wqkv, wp, w1, w2, n1t, qkvt, ot, lse, mid, n2, hs, gs,
             out_o, gx_o, gxr_o, dw2_o, dw2_y, dw1_o, dw1_y, dwp_o, dwp_y, dq_o, dq_y, sg_o,
             g_v, n2_v, gacc, h_v, pre_v, w1_v, w2_v, b1g, mid_v, qkvt_v, ot_v, lse_v, sm_v, sg_v, sgm_v, sgy_v,
             st_v, land_a, land_b, land_p, land_s, rb_a, rb_b, rb_p, rb_s,
             sem, tsem, wsem, mlsem, xsem, msem, rsem, ysem, ssem, gsem, free):
    here = Place(size)
    y, core = here.y, here.core
    half = T // 2
    ymine = pl.multiple_of(y * half, half)
    yother = pl.multiple_of((1 - y) * half, half)

    def cp(a, b, i):
        return pltpu.make_async_copy(a, b, sem.at[i])

    first = [cp(cotangent.at[y], g_v.at[pl.ds(ymine, half), :], 0), cp(cot_in, g_v.at[pl.ds(yother, half), :], 1), cp(n2, n2_v, 2), cp(sm, sm_v, 3)]
    later = [cp(qkvt, qkvt_v, 4), cp(ot, ot_v, 5), cp(lse, lse_v, 6)]
    last = [cp(x, h_v, 7), cp(n1t, w1_v, 8)]

    def chip(j):
        return here.chip(offset(j))

    def tl(t, s):
        c = pl.multiple_of(t * 512, 512)
        d = pl.multiple_of(s * 512, 512)
        return [
            pltpu.make_async_copy(hs.at[t], h_v.at[:, pl.ds(d, 512)], tsem.at[s, 0]),
            pltpu.make_async_copy(gs.at[t], pre_v.at[t], tsem.at[s, 1]),
            pltpu.make_async_copy(w1.at[:, pl.ds(c, 512)], w1_v.at[:, pl.ds(d, 512)], tsem.at[s, 2]),
            pltpu.make_async_copy(w2.at[pl.ds(c, 512), :], w2_v.at[pl.ds(d, 512), :], tsem.at[s, 3]),
        ]

    for c in first:
        c.start()
    for c in tl(chip(0), 0):
        c.start()
    for c in later:
        c.start()
    here.barrier()
    osend = remote(out.at[pl.ds(yother, half), :], out_o, gsem.at[0, 0], gsem.at[0, 1], here.across())
    osend.start()
    def scatter(i, land, rb, n, c0, w, fin_o, y_o):
        return Scatter(here, land, rb, n, (c0, w), msem.at[i], rsem.at[i], ysem.at[i], fin_o, y_o)

    s2 = Group(*[scatter(i, land_a, rb_a, 4, i * 512, 512, dw2_o, dw2_y) for i in range(2)])
    s1 = Group(*[scatter(2 + i, land_b, rb_b, 4, i * 512, 512, dw1_o, dw1_y) for i in range(2)])
    sp = Group(scatter(4, land_p, rb_p, 1, 0, D, dwp_o, dwp_y))
    qcols = ((0, 512), (512, 256), (768, 256))
    sq = [Group(scatter(5 + g, land_a, rb_a, 3, c0, w, dq_o, dq_y)) for g, (c0, w) in enumerate(qcols)]
    ss = Scatter(here, land_s, rb_s, 2, (0, 128), None, rsem.at[8], None)
    for c in first:
        c.wait()
    flag = valid[y].astype(F32)
    sg_v[...] = jnp.zeros_like(sg_v)

    def mask(i, c):
        r = pl.multiple_of(i * 256, 256)
        v = g_v[pl.ds(r, 256), :].astype(F32) * flag
        g_v[pl.ds(r, 256), :] = v.astype(BF16)
        sg_v[7:8, :] += jnp.sum(v, axis=0, keepdims=True)
        return c

    lax.fori_loop(0, T // 256, mask, 0)

    def st2(j, k):
        return st_v.at[0, pl.ds((j % 2) * 8 + k * 4, 4)]

    def tile(j, c):
        s = j % 2
        t = chip(j)

        @pl.when(j + 1 < NTILE)
        def _():
            for k in tl(chip(j + 1), 1 - s):
                k.start()

        for k in tl(t, s):
            k.wait()
        col = pl.ds(pl.multiple_of(s * 512, 512), 512)
        gb = g_v[...]
        st_v[0, pl.ds(s * 8, 8)] = dot(h_v[:, col], gb, 0, 0).astype(BF16).reshape(8, 64, D)
        s2.send(j, st2(j, 1 - core))
        pre = (dot(gb, w2_v[col, :], 1, 1) * pre_v[t].astype(F32)).astype(BF16)
        pre_v[t] = pre
        b1g[pl.ds(t, 1), :] = jnp.sum(pre.astype(F32), axis=0, keepdims=True)
        v = dot(pre, w1_v[:, col], 1, 1)

        @pl.when(j == 0)
        def _():
            gacc[...] = v

        @pl.when(j > 0)
        def _():
            gacc[...] += v

        s2.settle(j, st2(j, core))
        for k, n in enumerate((0, 2, 4)):
            @pl.when(j == n)
            def _(k=k):
                s2.step(k)

        return c

    lax.fori_loop(0, NTILE, tile, 0)
    for c in last:
        c.start()
    sg_v[8:16, 0:512] = b1g[...]

    def slots(q):
        return (2 * q + 7) % 8, 2 * q

    def st1(q, i, k):
        return st_v.at[1 + q % 2, pl.ds(i * 8 + k * 4, 4)]

    def settle1(q):
        for i, j in enumerate(slots(q)):
            s1.settle(j, st1(q, i, core))

    def pair1(q, c):
        at = [pl.ds(pl.multiple_of(chip(j) * 128, 128), 128) for j in slots(q)]
        left = jnp.concatenate([n2_v[:, a] for a in at], axis=1)
        for cb in range(4):
            for k in range(2):
                v = dot(left, pre_v[2 * cb + k], 0, 0).astype(BF16)
                for i in range(2):
                    for e in range(2):
                        st_v[1 + q % 2, i * 8 + e * 4 + cb, :, k * 512:(k + 1) * 512] = v[i * 128 + e * 64:i * 128 + e * 64 + 64]
        for i, j in enumerate(slots(q)):
            s1.send(j, st1(q, i, 1 - core))

        @pl.when(q > 0)
        def _():
            settle1(q - 1)

        @pl.when(q == 1)
        def _():
            s2.step(3)
            s1.step(0)

        return c

    lax.fori_loop(0, 4, pair1, 0)
    wpl = [pltpu.make_async_copy(wp.at[:, i * 512:(i + 1) * 512], pre_v.at[6 + i], wsem.at[6 + i]) for i in range(2)]
    wl = [pltpu.make_async_copy(wqkv.at[j, :, i * 512:(i + 1) * 512], pre_v.at[2 * j + i], wsem.at[2 * j + i]) for j in range(3) for i in range(2)]
    for c in wpl + wl:
        c.start()
    settle1(3)

    def ml(i, s):
        return pltpu.make_async_copy(mid.at[pl.ds(pl.multiple_of(i * 256, 256), 256), :], mid_v.at[s], mlsem.at[s])

    ml(0, 0).start()

    def ln2(i, c):
        r = pl.multiple_of(i * 256, 256)
        s = i % 2

        @pl.when(i < 3)
        def _():
            ml(i + 1, 1 - s).start()

        ml(i, s).wait()
        back, dg, db = ln_back(gacc[pl.ds(r, 256), :], mid_v[s], sm_v[5:6, :])
        gm = g_v[pl.ds(r, 256), :].astype(F32) + back
        gacc[pl.ds(r, 256), :] = gm
        gb = gm.astype(BF16)
        g_v[pl.ds(r, 256), :] = gb
        sg_v[5:6, :] += dg
        sg_v[6:7, :] += db
        sg_v[4:5, :] += jnp.sum(gb.astype(F32), axis=0, keepdims=True)
        return c

    lax.fori_loop(0, 4, ln2, 0)
    for c in later + wpl:
        c.wait()
    for i in range(2):
        rows = slice(i * 512, (i + 1) * 512)
        st_v[0, i * 8:(i + 1) * 8] = dot(ot_v[rows, :], g_v[...]).astype(BF16).reshape(8, 64, D)
        w2_v[rows, :] = (dot(pre_v[6, rows, :], g_v[:, 0:512], 1, 1) + dot(pre_v[7, rows, :], g_v[:, 512:1024], 1, 1)).astype(BF16)

    def stp(j, k):
        return st_v.at[0, pl.ds(2 * chip(j) + k, 1)]

    def matep(j, c):
        sp.send(j, stp(j, 1 - core))
        return c

    def settlep(j, c):
        sp.settle(j, stp(j, core))
        return c

    lax.fori_loop(0, 8, matep, 0)
    s2.finish()
    s1.step(1)

    def stq(j, k):
        return st_v.at[:, 2 * chip(j) + k]

    def dqkv(g):
        c0, w = qcols[g]
        for j in range(3):
            for i in range(2):
                v = dot(w1_v[i * 512:(i + 1) * 512, :], qkvt_v[j, c0:c0 + w, :], 1, 1).astype(BF16)
                st_v[j, i * 8:(i + 1) * 8, :, c0:c0 + w] = v.reshape(8, 64, w)

        def send(j, c):
            sq[g].send(j, stq(j, 1 - core))
            return c

        lax.fori_loop(0, 8, send, 0)

    def settleq(g):
        def one(j, c):
            sq[g].settle(j, stq(j, core))
            return c

        lax.fori_loop(0, 8, one, 0)

    def begin_p():
        lax.fori_loop(0, 8, settlep, 0)
        sp.step(0)

    def free_a():
        s2.drain()
        pl.semaphore_signal(free.at[0], inc=1, device_id=here.partner(), device_id_type=MESH)
        for d in range(2):
            pl.semaphore_signal(free.at[1], inc=1, device_id=here.side(d), device_id_type=MESH)

    def first_q():
        for c in last:
            c.wait()
        pl.semaphore_wait(free.at[0], 1)
        dqkv(0)

    def begin_q():
        settleq(0)
        pl.semaphore_wait(free.at[1], 2)
        sq[0].step(0)

    def second_q():
        settleq(1)
        sq[1].step(0)

    events = {
        0: [begin_p],
        2: [lambda: s1.step(2), lambda: sp.step(1), free_a],
        6: [lambda: s1.step(3), lambda: sp.step(2)],
        7: [first_q],
        8: [begin_q, lambda: sp.step(3)],
        10: [s1.finish, lambda: sq[0].step(1)],
        11: [sp.finish, lambda: dqkv(1)],
        12: [second_q, lambda: sq[0].step(2)],
        14: [lambda: sq[1].step(1), lambda: sq[0].step(3)],
    }

    def hd(h, c):
        bwd_head(h, qkvt_v, ot_v, w2_v, lse_v)
        for n, fns in events.items():
            @pl.when(h == n)
            def _(fns=fns):
                for fn in fns:
                    fn()
        return c

    lax.fori_loop(0, 16, hd, 0)
    for c in wl:
        c.wait()

    def row(i):
        return pl.multiple_of((1 - i // 2) * yother + (i // 2) * ymine + (i % 2) * 256, 256)

    def xsend(i):
        at = pl.ds(pl.multiple_of(i * 256, 256), 256)
        return remote(w2_v.at[at, :], gxr_o.at[at, :], xsem.at[0, i], xsem.at[1, i], here.across())

    def xkeep(i):
        return pltpu.make_async_copy(mid_v.at[i], gx_o.at[pl.ds(i * 256, 256), :], xsem.at[2, i])

    def fin(i, c):
        r = row(i)
        up = None
        for j in range(3):
            for k in range(2):
                v = dot(qkvt_v[j, k * 512:(k + 1) * 512, pl.ds(r, 256)], pre_v[2 * j + k], 0, 1)
                up = v if up is None else up + v
        back, dg, db = ln_back(up, h_v[pl.ds(r, 256), :].astype(F32), sm_v[0:1, :])
        v = gacc[pl.ds(r, 256), :] + back
        sg_v[0:1, :] += dg
        sg_v[1:2, :] += db

        @pl.when(i < 2)
        def _():
            w2_v[pl.ds(pl.multiple_of((i % 2) * 256, 256), 256), :] = v.astype(BF16)
            xsend(i % 2).start()

        @pl.when(i >= 2)
        def _():
            mid_v[i % 2] = v
            xkeep(i % 2).start()

        return c

    lax.fori_loop(0, 2, fin, 0)
    dqkv(2)
    sq[1].step(2)
    ones = jnp.ones((16, T), BF16)
    for j, row in ((0, 2), (2, 3)):
        sg_v[row:row + 1, :] = dot(ones, qkvt_v[j], 1, 1)[0:1, :]
    settleq(2)
    sq[2].step(0)
    sq[0].finish()
    lax.fori_loop(2, 4, fin, 0)
    sg1 = remote(sg_v, sgm_v, ssem.at[0, 0], ssem.at[0, 1], here.partner())
    sg1.start()
    sq[2].step(1)
    sq[1].step(3)
    sg1.wait_recv()
    sg1.wait_send()
    sg_v[...] = sg_v[...] + sgm_v[...]
    b1g[...] = sg_v[8:16, 0:512]
    for j in range(8):
        t = chip(j)
        land_s[j, 0] = sg_v[0:8, pl.ds(pl.multiple_of(t * 128, 128), 128)]
        land_s[j, 1, 4:8, :] = jnp.zeros((4, 128), F32)
        fb = b1g[pl.ds(t, 1), :]
        for q in range(4):
            land_s[j, 1, q:q + 1, :] = fb[:, q * 128:(q + 1) * 128]
    ss_steps(ss, 0)
    ss_steps(ss, 1)
    sq[2].step(2)
    ss_steps(ss, 2)
    sq[1].finish()
    ss_steps(ss, 3)
    sq[2].step(3)
    for d in range(2):
        ss_ring(ss, d, 3).wait_recv()
    fold(land_s.at[7], rb_s.at[0, 3], rb_s.at[1, 3])
    sg2 = remote(land_s.at[7], sgy_v, ssem.at[1, 0], ssem.at[1, 1], here.across())
    sg2.start()
    sq[2].finish()
    sg2.wait_recv()
    sg2.wait_send()
    fold(land_s.at[7], sgy_v)
    skeep = pltpu.make_async_copy(land_s.at[7], sg_o, ssem.at[2, 0])
    skeep.start()
    for s in range(4):
        for d in range(2):
            ss_ring(ss, d, s).wait_send()
    skeep.wait()
    for i in range(2):
        xsend(i).wait()
        xkeep(i).wait()
    osend.wait()
    for s in (s1, sp, *sq):
        s.drain()
    for s in (s2, s1, sp, *sq):
        s.arrive()


def ss_ring(ss, d, s):
    if s == 0:
        src, dst = ss.land.at[0, d], ss.rb.at[d, 0, d]
    else:
        src, dst = ss.land.at[2 * s - 1 + d], ss.rb.at[d, s]
    return remote(src, dst, ss.rsem.at[0, d, s], ss.rsem.at[1, d, s], ss.pl.side(d))


def ss_steps(ss, s):
    for d in range(2):
        if s:
            ss_ring(ss, d, s - 1).wait_recv()
            j = 2 * s - 1 + d
            if s == 1:
                ss.land[j, d] = ss.land[j, d] + ss.rb[d, 0, d]
            else:
                fold(ss.land.at[j], ss.rb.at[d, s - 1])
        ss_ring(ss, d, s).start()


def bwd_call(size):
    dma = pltpu.SemaphoreType.DMA
    block = S((4, 64, D), BF16)
    return pl.pallas_call(
        functools.partial(bwd_body, size),
        name="backward",
        in_specs=[pl.BlockSpec(memory_space=pltpu.SMEM)] + [ANY] * 17,
        out_specs=[ANY] * 12,
        out_shape=[S((T // 2, D), BF16), S((T // 2, D), F32), S((T // 2, D), BF16), block, block, block, block,
                   S((1, 64, D), BF16), S((1, 64, D), BF16), S((3, 64, D), BF16), S((3, 64, D), BF16), S((2, 8, 128), F32)],
        scratch_shapes=[V((T, D), BF16), V((T, D), BF16), V((T, D), F32), V((T, 1024), BF16), V((NTILE, T, 512), BF16), V((D, 1024), BF16), V((1024, D), BF16),
                        V((8, 512), F32), V((2, 256, D), F32), V((3, D, T), BF16), V((D, T), BF16), V((16, T), F32), V((16, D), F32), V((16, D), F32),
                        V((16, D), F32), V((2, 8, 128), F32),
                        V((3, 16, 64, D), BF16), V((8, 4, 64, D), BF16), V((8, 4, 64, D), BF16), V((8, 1, 64, D), BF16), V((8, 2, 8, 128), F32),
                        V((2, 4, 4, 64, D), BF16), V((2, 4, 4, 64, D), BF16), V((2, 4, 1, 64, D), BF16), V((2, 4, 2, 8, 128), F32),
                        dma((9,)), dma((2, 4)), dma((8,)), dma((2,)), dma((3, 2)), dma((8, 2, 8)), dma((9, 2, 2, 4)), dma((8, 3)), dma((3, 2)), dma((1, 2)),
                        pltpu.SemaphoreType.REGULAR((2,))],
        compiler_params=pltpu.CompilerParams(vmem_limit_bytes=67043328, collective_id=1, has_side_effects=True),
    )


def fast_body(clips, cotangent, valid, *shards):
    size = lax.axis_size("fsdp")
    me = lax.axis_index("fsdp")
    mine = lax.axis_index("seq")
    (g1, b1, wq, wk, wv, bq, bv, wp, bp, g2, b2, w1, fb1, w2, fb2) = shards
    n, m = g1.shape[0], fb1.shape[0]
    vecs = jnp.stack([g1, b1, bq, bv, bp, g2, b2, fb2])
    sml = lax.dynamic_update_slice(jnp.zeros((8, D), vecs.dtype), vecs, (0, me * n))
    fsm = lax.dynamic_update_slice(jnp.zeros((FF,), vecs.dtype), fb1, (me * m,)).reshape(-1, D)
    sml = jnp.concatenate([sml, fsm, jnp.zeros((8 - FF // D, D), vecs.dtype)])
    out, cot_in, x, sm, wqkv, wp_all, w1_all, w2_all, *saved = fwd_call(size, T, D, FF)(clips, cotangent, sml, wq, wk, wv, wp, w1, w2)
    out_in, gx, gx_in, dw2, dw2y, dw1, dw1y, dwp, dwpy, dq, dqy, sg = bwd_call(size)(
        valid, cotangent, cot_in, out, x, sm, wqkv, wp_all, w1_all, w2_all, *saved)

    def both(a, b):
        return a.astype(F32) + b.astype(F32)

    def halves(own, other):
        return jnp.where(mine == 0, jnp.stack([own, other]), jnp.stack([other, own]))

    dw2 = both(dw2, dw2y).reshape(-1, D)
    dw1 = both(dw1, dw1y).transpose(1, 0, 2).reshape(n, -1)
    dq = both(dq, dqy)
    dwp = both(dwp, dwpy)[0]
    own = lax.dynamic_slice(sg[0], (0, me % 2 * n), (8, n))
    dfb1 = lax.dynamic_slice(sg[1, 0:4].reshape(-1), (me % 2 * m,), (m,))
    out = halves(lax.dynamic_slice(out, (mine * (T // 2), 0), (T // 2, D)), out_in)
    gx = halves(gx, gx_in.astype(F32))
    return (out, gx, own[0], own[1], dq[0], dq[1], dq[2], own[2], own[3], dwp, own[4], own[5], own[6], dw1, dfb1, dw2, own[7])


def solution(mesh):
    in_specs = (
        P("fsdp", "seq", None),
        P("fsdp", "seq", None),
        P("fsdp"),
        P("fsdp"),
        P("fsdp"),
        P("fsdp", None),
        P("fsdp", None),
        P("fsdp", None),
        P("fsdp"),
        P("fsdp"),
        P("fsdp", None),
        P("fsdp"),
        P("fsdp"),
        P("fsdp"),
        P("fsdp", None),
        P("fsdp"),
        P("fsdp", None),
        P("fsdp"),
    )
    out_specs = (
        P("fsdp", "seq", None),
        P("fsdp", "seq", None),
        P("fsdp"),
        P("fsdp"),
        P("fsdp", None),
        P("fsdp", None),
        P("fsdp", None),
        P("fsdp"),
        P("fsdp"),
        P("fsdp", None),
        P("fsdp"),
        P("fsdp"),
        P("fsdp"),
        P("fsdp", None),
        P("fsdp"),
        P("fsdp", None),
        P("fsdp"),
    )
    quick = mesh.shape["seq"] == 2 and mesh.shape["fsdp"] == 16
    return jax.shard_map(fast_body if quick else body, mesh=mesh, in_specs=in_specs, out_specs=out_specs, check_vma=False)
```

```python
import functools
import jax
import jax.numpy as jnp
from jax import lax
from jax.experimental import pallas as pl
from jax.experimental.pallas import tpu as pltpu
from jax.sharding import PartitionSpec as P

H = 16
QBLK = 512


norm_eps = 1e-06
root_half = 0.7071067811865476
inv_root_tau = 0.3989422804014327


def matmul(left, right):
    return jnp.dot(left, right, preferred_element_type=jnp.float32)


def matmul_nt(left, right):
    return lax.dot_general(
        left, right, (((1,), (1,)), ((), ())), preferred_element_type=jnp.float32
    )


def matmul_tn(left, right):
    return lax.dot_general(
        left, right, (((0,), (0,)), ((), ())), preferred_element_type=jnp.float32
    )


def layer_norm(values_in, gain, shift):
    row_mean = jnp.mean(values_in, axis=-1, keepdims=True)
    centred = values_in - row_mean
    inverse = lax.rsqrt(jnp.mean(centred * centred, axis=-1, keepdims=True) + norm_eps)
    scaled = centred * inverse
    return (scaled * gain + shift, scaled, inverse)


def layer_norm_back(upstream, scaled, inverse, gain):
    dscaled = upstream * gain
    inner = (
        dscaled
        - jnp.mean(dscaled, axis=-1, keepdims=True)
        - scaled * jnp.mean(dscaled * scaled, axis=-1, keepdims=True)
    )
    return (inverse * inner, jnp.sum(upstream * scaled, axis=0), jnp.sum(upstream, axis=0))


def gelu_value(pre_act):
    return 0.5 * pre_act * (1.0 + lax.erf(pre_act * root_half))


def gelu_slope(pre_act):
    return 0.5 * (1.0 + lax.erf(pre_act * root_half)) + pre_act * inv_root_tau * jnp.exp(
        -0.5 * pre_act * pre_act
    )


def attend(queries, keys_all, values_all, head_count):
    length = queries.shape[0]
    head_width = queries.shape[1] // head_count
    score_scale = head_width ** (-0.5)
    query_heads = queries.reshape(length // QBLK, QBLK, head_count, head_width)
    key_heads = keys_all.reshape(length, head_count, head_width)
    value_heads = values_all.reshape(length, head_count, head_width)

    def one_block(query_rows):
        scores = (
            jnp.einsum("qhd,khd->hqk", query_rows, key_heads, preferred_element_type=jnp.float32)
            * score_scale
        )
        peak = jnp.max(scores, axis=-1, keepdims=True)
        raised = jnp.exp(scores - peak)
        row_total = jnp.sum(raised, axis=-1, keepdims=True)
        weights = (raised / row_total).astype(jnp.bfloat16)
        mixed = jnp.einsum("hqk,khd->qhd", weights, value_heads, preferred_element_type=jnp.float32)
        return (mixed.astype(jnp.bfloat16), (peak + jnp.log(row_total))[:, :, 0])

    mixed, log_totals = lax.map(one_block, query_heads)
    return (mixed.reshape(length, head_count * head_width), log_totals)


def attend_back(queries, keys_all, values_all, log_totals, upstream, head_count):
    length = queries.shape[0]
    head_width = queries.shape[1] // head_count
    score_scale = head_width ** (-0.5)
    query_heads = queries.reshape(length // QBLK, QBLK, head_count, head_width)
    upstream_heads = upstream.reshape(length // QBLK, QBLK, head_count, head_width)
    key_heads = keys_all.reshape(length, head_count, head_width)
    value_heads = values_all.reshape(length, head_count, head_width)

    def one_block(running, block_item):
        key_grad, value_grad = running
        query_rows, log_rows, grad_rows = block_item
        scores = (
            jnp.einsum("qhd,khd->hqk", query_rows, key_heads, preferred_element_type=jnp.float32)
            * score_scale
        )
        weights = jnp.exp(scores - log_rows[:, :, None])
        weights_low = weights.astype(jnp.bfloat16)
        grad_weights = jnp.einsum(
            "qhd,khd->hqk", grad_rows, value_heads, preferred_element_type=jnp.float32
        )
        inner = jnp.sum(grad_weights * weights, axis=-1, keepdims=True)
        grad_scores = (weights * (grad_weights - inner)).astype(jnp.bfloat16)
        query_grad = (
            jnp.einsum("hqk,khd->qhd", grad_scores, key_heads, preferred_element_type=jnp.float32)
            * score_scale
        )
        key_grad = (
            key_grad
            + jnp.einsum(
                "hqk,qhd->khd", grad_scores, query_rows, preferred_element_type=jnp.float32
            )
            * score_scale
        )
        value_grad = value_grad + jnp.einsum(
            "hqk,qhd->khd", weights_low, grad_rows, preferred_element_type=jnp.float32
        )
        return ((key_grad, value_grad), query_grad.astype(jnp.bfloat16))

    zeros_heads = jnp.zeros((length, head_count, head_width), jnp.float32)
    (key_grad, value_grad), query_grad = lax.scan(
        one_block, (zeros_heads, zeros_heads), (query_heads, log_totals, upstream_heads)
    )
    width_all = head_count * head_width
    return (
        query_grad.reshape(length, width_all),
        key_grad.reshape(length, width_all).astype(jnp.bfloat16),
        value_grad.reshape(length, width_all).astype(jnp.bfloat16),
    )


def fetch(shards):
    return (
        lax.all_gather(shards[0], "fsdp", axis=0, tiled=True),
        lax.all_gather(shards[1], "fsdp", axis=0, tiled=True),
        lax.all_gather(shards[2], "fsdp", axis=0, tiled=True),
        lax.all_gather(shards[3], "fsdp", axis=0, tiled=True),
        lax.all_gather(shards[4], "fsdp", axis=0, tiled=True),
        lax.all_gather(shards[5], "fsdp", axis=0, tiled=True),
        lax.all_gather(shards[6], "fsdp", axis=0, tiled=True),
        lax.all_gather(shards[7], "fsdp", axis=0, tiled=True),
        lax.all_gather(shards[8], "fsdp", axis=0, tiled=True),
        lax.all_gather(shards[9], "fsdp", axis=0, tiled=True),
        lax.all_gather(shards[10], "fsdp", axis=0, tiled=True),
        lax.all_gather(shards[11], "fsdp", axis=0, tiled=True),
        lax.all_gather(shards[12], "fsdp", axis=0, tiled=True),
        lax.all_gather(shards[13], "fsdp", axis=0, tiled=True),
        lax.all_gather(shards[14], "fsdp", axis=0, tiled=True),
    )


def settle(grads):
    shares = (
        lax.psum_scatter(
            grads[0].astype(jnp.bfloat16), "fsdp", scatter_dimension=0, tiled=True
        ).astype(jnp.float32),
        lax.psum_scatter(
            grads[1].astype(jnp.bfloat16), "fsdp", scatter_dimension=0, tiled=True
        ).astype(jnp.float32),
        lax.psum_scatter(
            grads[2].astype(jnp.bfloat16), "fsdp", scatter_dimension=0, tiled=True
        ).astype(jnp.float32),
        lax.psum_scatter(
            grads[3].astype(jnp.bfloat16), "fsdp", scatter_dimension=0, tiled=True
        ).astype(jnp.float32),
        lax.psum_scatter(
            grads[4].astype(jnp.bfloat16), "fsdp", scatter_dimension=0, tiled=True
        ).astype(jnp.float32),
        lax.psum_scatter(
            grads[5].astype(jnp.bfloat16), "fsdp", scatter_dimension=0, tiled=True
        ).astype(jnp.float32),
        lax.psum_scatter(
            grads[6].astype(jnp.bfloat16), "fsdp", scatter_dimension=0, tiled=True
        ).astype(jnp.float32),
        lax.psum_scatter(
            grads[7].astype(jnp.bfloat16), "fsdp", scatter_dimension=0, tiled=True
        ).astype(jnp.float32),
        lax.psum_scatter(
            grads[8].astype(jnp.bfloat16), "fsdp", scatter_dimension=0, tiled=True
        ).astype(jnp.float32),
        lax.psum_scatter(
            grads[9].astype(jnp.bfloat16), "fsdp", scatter_dimension=0, tiled=True
        ).astype(jnp.float32),
        lax.psum_scatter(
            grads[10].astype(jnp.bfloat16), "fsdp", scatter_dimension=0, tiled=True
        ).astype(jnp.float32),
        lax.psum_scatter(
            grads[11].astype(jnp.bfloat16), "fsdp", scatter_dimension=0, tiled=True
        ).astype(jnp.float32),
        lax.psum_scatter(
            grads[12].astype(jnp.bfloat16), "fsdp", scatter_dimension=0, tiled=True
        ).astype(jnp.float32),
        lax.psum_scatter(
            grads[13].astype(jnp.bfloat16), "fsdp", scatter_dimension=0, tiled=True
        ).astype(jnp.float32),
        lax.psum_scatter(
            grads[14].astype(jnp.bfloat16), "fsdp", scatter_dimension=0, tiled=True
        ).astype(jnp.float32),
    )
    return (
        lax.psum(shares[0].astype(jnp.bfloat16), "seq").astype(jnp.float32),
        lax.psum(shares[1].astype(jnp.bfloat16), "seq").astype(jnp.float32),
        lax.psum(shares[2].astype(jnp.bfloat16), "seq").astype(jnp.float32),
        lax.psum(shares[3].astype(jnp.bfloat16), "seq").astype(jnp.float32),
        lax.psum(shares[4].astype(jnp.bfloat16), "seq").astype(jnp.float32),
        lax.psum(shares[5].astype(jnp.bfloat16), "seq").astype(jnp.float32),
        lax.psum(shares[6].astype(jnp.bfloat16), "seq").astype(jnp.float32),
        lax.psum(shares[7].astype(jnp.bfloat16), "seq").astype(jnp.float32),
        lax.psum(shares[8].astype(jnp.bfloat16), "seq").astype(jnp.float32),
        lax.psum(shares[9].astype(jnp.bfloat16), "seq").astype(jnp.float32),
        lax.psum(shares[10].astype(jnp.bfloat16), "seq").astype(jnp.float32),
        lax.psum(shares[11].astype(jnp.bfloat16), "seq").astype(jnp.float32),
        lax.psum(shares[12].astype(jnp.bfloat16), "seq").astype(jnp.float32),
        lax.psum(shares[13].astype(jnp.bfloat16), "seq").astype(jnp.float32),
        lax.psum(shares[14].astype(jnp.bfloat16), "seq").astype(jnp.float32),
    )


def one_clip(clip_in, clip_cot, clip_flag, gathered, head_count):
    (
        norm1_gain,
        norm1_bias,
        query_weight,
        key_weight,
        value_weight,
        query_bias,
        value_bias,
        proj_weight,
        proj_bias,
        norm2_gain,
        norm2_bias,
        fc1_weight,
        fc1_bias,
        fc2_weight,
        fc2_bias,
    ) = gathered
    gain_one = norm1_gain.astype(jnp.float32)
    gain_two = norm2_gain.astype(jnp.float32)
    tokens_in = clip_in.astype(jnp.float32)
    normed, scaled_one, inverse_one = layer_norm(
        tokens_in, gain_one, norm1_bias.astype(jnp.float32)
    )
    normed_low = normed.astype(jnp.bfloat16)
    queries = (matmul(normed_low, query_weight) + query_bias.astype(jnp.float32)).astype(
        jnp.bfloat16
    )
    keys_all = matmul(normed_low, key_weight).astype(jnp.bfloat16)
    values_all = (matmul(normed_low, value_weight) + value_bias.astype(jnp.float32)).astype(
        jnp.bfloat16
    )
    query_heads, key_heads, value_heads = (
        lax.all_to_all(queries, "seq", split_axis=1, concat_axis=0, tiled=True),
        lax.all_to_all(keys_all, "seq", split_axis=1, concat_axis=0, tiled=True),
        lax.all_to_all(values_all, "seq", split_axis=1, concat_axis=0, tiled=True),
    )
    mixed_heads, log_totals = attend(query_heads, key_heads, value_heads, head_count)
    attended = lax.all_to_all(mixed_heads, "seq", split_axis=0, concat_axis=1, tiled=True)
    middle = tokens_in + matmul(attended, proj_weight) + proj_bias.astype(jnp.float32)
    normed_two, scaled_two, inverse_two = layer_norm(
        middle, gain_two, norm2_bias.astype(jnp.float32)
    )
    normed_two_low = normed_two.astype(jnp.bfloat16)
    hidden_pre = matmul(normed_two_low, fc1_weight) + fc1_bias.astype(jnp.float32)
    hidden_low = gelu_value(hidden_pre).astype(jnp.bfloat16)
    output = middle + matmul(hidden_low, fc2_weight) + fc2_bias.astype(jnp.float32)
    grad_out = clip_cot.astype(jnp.float32) * clip_flag.astype(jnp.float32)
    grad_mlp = grad_out.astype(jnp.bfloat16)
    grad_fc2_weight = matmul_tn(hidden_low, grad_mlp)
    grad_fc2_bias = jnp.sum(grad_mlp.astype(jnp.float32), axis=0)
    grad_pre = (matmul_nt(grad_mlp, fc2_weight) * gelu_slope(hidden_pre)).astype(jnp.bfloat16)
    grad_fc1_weight = matmul_tn(normed_two_low, grad_pre)
    grad_fc1_bias = jnp.sum(grad_pre.astype(jnp.float32), axis=0)
    grad_norm_two = matmul_nt(grad_pre, fc1_weight)
    grad_ln_two, grad_norm2_gain, grad_norm2_bias = layer_norm_back(
        grad_norm_two, scaled_two, inverse_two, gain_two
    )
    grad_middle = grad_out + grad_ln_two
    grad_branch = grad_middle.astype(jnp.bfloat16)
    grad_proj_weight = matmul_tn(attended, grad_branch)
    grad_proj_bias = jnp.sum(grad_branch.astype(jnp.float32), axis=0)
    grad_att = matmul_nt(grad_branch, proj_weight).astype(jnp.bfloat16)
    grad_att_heads = lax.all_to_all(grad_att, "seq", split_axis=1, concat_axis=0, tiled=True)
    query_grad, key_grad, value_grad = attend_back(
        query_heads, key_heads, value_heads, log_totals, grad_att_heads, head_count
    )
    grad_queries, grad_keys, grad_values = (
        lax.all_to_all(query_grad, "seq", split_axis=0, concat_axis=1, tiled=True),
        lax.all_to_all(key_grad, "seq", split_axis=0, concat_axis=1, tiled=True),
        lax.all_to_all(value_grad, "seq", split_axis=0, concat_axis=1, tiled=True),
    )
    grad_query_weight = matmul_tn(normed_low, grad_queries)
    grad_key_weight = matmul_tn(normed_low, grad_keys)
    grad_value_weight = matmul_tn(normed_low, grad_values)
    grad_query_bias = jnp.sum(grad_queries.astype(jnp.float32), axis=0)
    grad_value_bias = jnp.sum(grad_values.astype(jnp.float32), axis=0)
    grad_norm_one = (
        matmul_nt(grad_queries, query_weight)
        + matmul_nt(grad_keys, key_weight)
        + matmul_nt(grad_values, value_weight)
    )
    grad_ln_one, grad_norm1_gain, grad_norm1_bias = layer_norm_back(
        grad_norm_one, scaled_one, inverse_one, gain_one
    )
    grad_in = grad_middle + grad_ln_one
    grads = (
        grad_norm1_gain,
        grad_norm1_bias,
        grad_query_weight,
        grad_key_weight,
        grad_value_weight,
        grad_query_bias,
        grad_value_bias,
        grad_proj_weight,
        grad_proj_bias,
        grad_norm2_gain,
        grad_norm2_bias,
        grad_fc1_weight,
        grad_fc1_bias,
        grad_fc2_weight,
        grad_fc2_bias,
    )
    return (output.astype(jnp.bfloat16), grad_in, grads)


def body(
    clips,
    cotangent,
    valid,
    norm1_gain,
    norm1_bias,
    query_weight,
    key_weight,
    value_weight,
    query_bias,
    value_bias,
    proj_weight,
    proj_bias,
    norm2_gain,
    norm2_bias,
    fc1_weight,
    fc1_bias,
    fc2_weight,
    fc2_bias,
):
    shards = (
        norm1_gain,
        norm1_bias,
        query_weight,
        key_weight,
        value_weight,
        query_bias,
        value_bias,
        proj_weight,
        proj_bias,
        norm2_gain,
        norm2_bias,
        fc1_weight,
        fc1_bias,
        fc2_weight,
        fc2_bias,
    )
    slot_count = clips.shape[0]
    head_count = H // lax.axis_size("seq")
    summed = None
    outputs = []
    grad_list = []
    for batch_slot in range(slot_count):
        gathered = fetch(shards)
        output, grad_in, grads = one_clip(
            clips[batch_slot], cotangent[batch_slot], valid[batch_slot], gathered, head_count
        )
        summed = (
            grads
            if summed is None
            else tuple((older + newer for older, newer in zip(summed, grads)))
        )
        outputs.append(output)
        grad_list.append(grad_in)
    summed = settle(summed)
    return (
        jnp.stack(outputs),
        jnp.stack(grad_list),
        summed[0],
        summed[1],
        summed[2],
        summed[3],
        summed[4],
        summed[5],
        summed[6],
        summed[7],
        summed[8],
        summed[9],
        summed[10],
        summed[11],
        summed[12],
        summed[13],
        summed[14],
    )


T, D, FF, NTILE = 1024, 1024, 4096, 8

log2_e = 1.4426950408889634
HD = 64
F32, BF16 = jnp.float32, jnp.bfloat16
ANY = pl.BlockSpec(memory_space=pl.ANY)


def dot(left, right, cl=1, cr=0):
    return lax.dot_general(left, right, (((cl,), (cr,)), ((), ())), preferred_element_type=F32)


def split3(v):
    hi = v.astype(BF16)
    r = v - hi.astype(F32)
    md = r.astype(BF16)
    lo = (r - md.astype(F32)).astype(BF16)
    return hi, md, lo


def aug_rows(v):
    hi, md, lo = split3(v)
    z = jnp.zeros((13, v.shape[1]), BF16)
    return jnp.concatenate([hi, md, lo, z], axis=0)


def ln_back(up, v, gain):
    m = jnp.mean(v, axis=-1, keepdims=True)
    d = v - m
    r = lax.rsqrt(jnp.mean(d * d, axis=-1, keepdims=True) + norm_eps)
    xh = d * r
    s = up * gain
    back = r * (s - jnp.mean(s, axis=-1, keepdims=True) - xh * jnp.mean(s * xh, axis=-1, keepdims=True))
    return back, jnp.sum(up * xh, axis=0, keepdims=True), jnp.sum(up, axis=0, keepdims=True)


def bwd_head(h, qkvt, ot, dot_v, lse_v):
    T = ot.shape[1]
    qb = T // 2
    scale = HD ** -0.5
    r = pl.multiple_of(h * HD, HD)
    rows = pl.ds(r, HD)
    ones = jnp.ones((16, T), BF16)
    kh = qkvt[1, rows, :]
    ka = jnp.concatenate([kh, ones], axis=0)
    va = jnp.concatenate([qkvt[2, rows, :], ones], axis=0)
    dk = dv = None
    for b in range(2):
        cols = slice(b * qb, (b + 1) * qb)
        qh = qkvt[0, rows, cols] * jnp.asarray(scale, BF16)
        do = dot_v[rows, cols]
        delta = jnp.sum(do.astype(F32) * ot[rows, cols].astype(F32), axis=0, keepdims=True)
        qa = jnp.concatenate([qh, aug_rows(-lse_v[pl.ds(h, 1), cols])], axis=0)
        da = jnp.concatenate([do, aug_rows(-delta)], axis=0)
        p = jnp.exp2(dot(qa, ka, 0, 0) * log2_e)
        ds = (p * dot(da, va, 0, 0)).astype(BF16)
        ndv = dot(do, p.astype(BF16))
        ndk = dot(qh, ds)
        dv = ndv if dv is None else dv + ndv
        dk = ndk if dk is None else dk + ndk
        qkvt[0, rows, cols] = (dot(kh, ds, 1, 1) * scale).astype(BF16)
    qkvt[1, rows, :] = dk.astype(BF16)
    qkvt[2, rows, :] = dv.astype(BF16)


MESH = pl.DeviceIdType.MESH


class Place:
    def __init__(self, size):
        f = lax.axis_index("fsdp")
        self.f, self.core, chip = f, f % 2, f // 2
        self.deep, self.count = size // 4, size // 2
        x, z = chip % 2, chip // 2
        self.pos = z + x * (2 * self.deep - 1 - 2 * z)
        self.mate = f + 1 - 2 * self.core
        self.y = lax.axis_index("seq")

    def chip(self, off):
        pos = (self.pos + self.count + off) % self.count
        hi = pos // self.deep
        return 2 * (pos + hi * (2 * self.deep - 1 - 2 * pos)) + hi

    def side(self, d):
        return {"fsdp": 2 * self.chip((1, -1)[d]) + self.core}

    def partner(self):
        return {"fsdp": self.mate}

    def across(self):
        return {"seq": 1 - self.y}

    def barrier(self):
        sem = pltpu.get_barrier_semaphore()
        for dev in (self.side(0), self.side(1), self.partner(), self.across()):
            pl.semaphore_signal(sem, inc=1, device_id=dev, device_id_type=MESH)
        pl.semaphore_wait(sem, 4)


def remote(src, dst, ss, rs, dev):
    return pltpu.make_async_remote_copy(src_ref=src, dst_ref=dst, send_sem=ss, recv_sem=rs, device_id=dev, device_id_type=MESH)


class Gather:
    def __init__(self, place, view, rsem, psem):
        self.pl, self.view, self.rsem, self.psem = place, view, rsem, psem
        self.last = place.count // 2 - 1

    def part(self, d, s):
        return d if s == self.last else 2

    def block(self, d, s, ahead):
        k = s + ahead
        return self.pl.chip(-k if d == 0 else k)

    def ring(self, d, s, ahead=0):
        v = self.view(2 * self.block(d, s, ahead) + self.pl.core, self.part(d, s))
        return remote(v, v, self.rsem.at[0, d, s], self.rsem.at[1, d, s], self.pl.side(d))

    def mate(self, slot, chip, part, core):
        v = self.view(2 * chip + core, part)
        return remote(v, v, self.psem.at[0, slot], self.psem.at[1, slot], self.pl.partner())

    def slots(self, s):
        return [(1 + 2 * s + d, self.block(d, s, 1), self.part(d, s)) for d in range(2)]

    def start(self):
        for d in range(2):
            self.ring(d, 0).start()
        self.mate(0, self.pl.chip(0), 2, self.pl.core).start()

    def step(self, s):
        for d in range(2):
            self.ring(d, s, 1).wait_recv()
            if s < self.last:
                self.ring(d, s + 1).start()
        for slot, chip, part in self.slots(s):
            self.mate(slot, chip, part, self.pl.core).start()

    def own_mate(self):
        self.mate(0, self.pl.chip(0), 2, 1 - self.pl.core).wait_recv()

    def step_mate(self, s):
        for slot, chip, part in self.slots(s):
            self.mate(slot, chip, part, 1 - self.pl.core).wait_recv()

    def all_mates(self):
        self.own_mate()
        for s in range(self.last + 1):
            self.step_mate(s)

    def drain(self):
        for s in range(self.last + 1):
            for d in range(2):
                self.ring(d, s).wait_send()
            for slot, chip, part in self.slots(s):
                self.mate(slot, chip, part, self.pl.core).wait_send()
        self.mate(0, self.pl.chip(0), 2, self.pl.core).wait_send()


class GatherY(Gather):
    def __init__(self, place, half, whole, rsem, psem, qsem, asem):
        super().__init__(place, lambda f, part: half(f, part, place.y), rsem, psem)
        self.half, self.whole, self.qsem, self.asem = half, whole, qsem, asem

    def mate(self, slot, chip, part, core):
        if slot:
            return super().mate(slot, chip, part, core)
        v = self.whole(2 * chip + core)
        return remote(v, v, self.psem.at[0, 0], self.psem.at[1, 0], self.pl.partner())

    def over(self, slot, chip, part, y):
        v = self.half(2 * chip + self.pl.core, part, y)
        return remote(v, v, self.asem.at[0, slot], self.asem.at[1, slot], self.pl.across())

    def relay(self, slot, chip, part, core):
        v = self.half(2 * chip + core, part, 1 - self.pl.y)
        return remote(v, v, self.qsem.at[0, slot], self.qsem.at[1, slot], self.pl.partner())

    def step(self, s):
        for d in range(2):
            self.ring(d, s, 1).wait_recv()
            if s < self.last:
                self.ring(d, s + 1).start()
        for slot, chip, part in self.slots(s):
            self.over(slot, chip, part, self.pl.y).start()
            self.mate(slot, chip, part, self.pl.core).start()

    def step_over(self, s):
        for slot, chip, part in self.slots(s):
            self.over(slot, chip, part, 1 - self.pl.y).wait_recv()
            self.relay(slot, chip, part, self.pl.core).start()

    def step_mate(self, s):
        super().step_mate(s)
        for slot, chip, part in self.slots(s):
            self.relay(slot, chip, part, 1 - self.pl.core).wait_recv()

    def drain(self):
        super().drain()
        for s in range(self.last + 1):
            for slot, chip, part in self.slots(s):
                self.over(slot, chip, part, self.pl.y).wait_send()
                self.relay(slot, chip, part, self.pl.core).wait_send()


def fwd_body(size, clips, cot, sml, wq, wk, wv, wp, w1, w2,
             out_o, cot_o, x_o, sm_o, wqkv_o, wp_o, w1_o, w2_o, n1t_o, qkvt_o, ot_o, lse_o, mid_o, n2_o, h_o, g_o,
             x_v, smb, sm_v, wqkv_v, wp_v, w1_v, w2_v, n1t, qkvt, ot, lse_v, mid, n2, acc, hst, gst, b1_v, smt,
             rsem, psem, qsem, asem, xsem, lsem, osem, tsem):
    here = Place(size)
    T, D = x_v.shape
    FF = w1_v.shape[1]
    tile = hst.shape[2]
    heads = D // HD
    half = T // 2
    nd, nf = D // size, FF // size
    y = here.y
    ymine = pl.ds(pl.multiple_of(y * half, half), half)
    yother = pl.ds(pl.multiple_of((1 - y) * half, half), half)

    def local(a, b, i):
        return pltpu.make_async_copy(a, b, lsem.at[i])

    def rows(ref, n, lead):
        def view(f, part):
            k = n if part == 2 else n // 2
            at = pl.ds(pl.multiple_of(f * n + (n // 2 if part == 1 else 0), k), k)
            return ref.at[:, at, :] if lead else ref.at[at, :]
        return view

    def smview(f, part):
        if part == 2:
            return smb.at[f]
        return smb.at[f, :, part * (D // 2):(part + 1) * (D // 2)]

    def part_rows(ref, n, c0, w):
        def half_view(f, part, yy):
            k = n if part == 2 else n // 2
            at = pl.ds(pl.multiple_of(f * n + (n // 2 if part == 1 else 0), k), k)
            return ref.at[at, pl.ds(pl.multiple_of(c0 + yy * (w // 2), w // 2), w // 2)]

        def whole_view(f):
            return ref.at[pl.ds(pl.multiple_of(f * n, n), n), c0:c0 + w]

        return half_view, whole_view

    def first_rows(f, part):
        return rows(w1_v, nd, False)(f, part).at[:, 0:FF // 2]

    views = [smview, rows(wqkv_v, nd, True), rows(wp_v, nd, False), first_rows]
    ga, gq, gp, g1 = [Gather(here, v, rsem.at[i], psem.at[i]) for i, v in enumerate(views)]
    g3 = GatherY(here, *part_rows(w1_v, nd, FF // 2, FF // 2), rsem.at[4], psem.at[4], qsem.at[0], asem.at[0])
    g2 = GatherY(here, *part_rows(w2_v, nf, 0, D), rsem.at[5], psem.at[5], qsem.at[1], asem.at[1])
    own = pl.ds(pl.multiple_of(here.f * nd, nd), nd)
    ownf = pl.ds(pl.multiple_of(here.f * nf, nf), nf)
    loc = [local(sml, smb.at[here.f], 0)]
    loc += [local(w, wqkv_v.at[j, own, :], 1 + j) for j, w in enumerate((wq, wk, wv))]
    loc += [local(wp, wp_v.at[own, :], 4), local(w1, w1_v.at[own, :], 5), local(w2, w2_v.at[ownf, :], 6), local(clips.at[y], x_v.at[ymine, :], 7)]
    for c in loc:
        c.start()
    here.barrier()
    xsend = remote(clips.at[1 - y], x_v.at[ymine, :], xsem.at[0, 0], xsem.at[0, 1], here.across())
    xrecv = remote(clips.at[1 - y], x_v.at[yother, :], xsem.at[0, 0], xsem.at[0, 1], here.across())
    csend = remote(cot.at[1 - y], cot_o, xsem.at[1, 0], xsem.at[1, 1], here.across())
    xsend.start()
    csend.start()
    for c in loc[:4]:
        c.wait()
    ga.start()
    gq.start()
    for c in loc[4:]:
        c.wait()

    def ln1(i, c):
        r = pl.multiple_of(i * 256, 256)
        v = x_v[pl.ds(r, 256), :].astype(F32)
        m = jnp.mean(v, axis=-1, keepdims=True)
        d = v - m
        mid[pl.ds(r, 256), :] = d * lax.rsqrt(jnp.mean(d * d, axis=-1, keepdims=True) + norm_eps)
        return c

    per = half // 256
    lax.fori_loop(y * per, y * per + per, ln1, 0)
    for s in range(ga.last + 1):
        ga.step(s)
        gq.step(s)
        if s == ga.last - 1:
            gp.start()
            g1.start()
            g3.start()
    xrecv.wait_recv()
    lax.fori_loop((1 - y) * per, (1 - y) * per + per, ln1, 0)
    ga.all_mates()
    sm_v[...] = jnp.sum(smb[...].astype(F32), axis=0)
    smt[...] = jnp.transpose(sm_v[...])

    def ln1b(i, c):
        r = pl.multiple_of(i * 256, 256)
        n1t[:, pl.ds(r, 256)] = jnp.transpose((mid[pl.ds(r, 256), :] * sm_v[0:1, :] + sm_v[1:2, :]).astype(BF16))
        return c

    lax.fori_loop(0, T // 256, ln1b, 0)
    gq.all_mates()
    outs = []

    def save(a, b):
        c = pltpu.make_async_copy(a, b, osem.at[len(outs)])
        outs.append(c)
        c.start()

    save(wqkv_v, wqkv_o)
    save(x_v, x_o)
    save(sm_v, sm_o)
    save(n1t, n1t_o)
    hd = D // 2
    for j in range(3):
        for o in range(2):
            v = dot(wqkv_v[j, :, o * hd:(o + 1) * hd], n1t[...], 0, 0)
            if j != 1:
                v = v + smt[o * hd:(o + 1) * hd, (2 if j == 0 else 3):(3 if j == 0 else 4)]
            qkvt[j, o * hd:(o + 1) * hd, :] = v.astype(BF16)
    save(qkvt, qkvt_o)
    qb = T // 2
    ones = jnp.ones((16, T), BF16)

    def head(h, c):
        r = pl.multiple_of(h * HD, HD)
        kh = qkvt[1, pl.ds(r, HD), :]
        vh = jnp.concatenate([qkvt[2, pl.ds(r, HD), :], ones], axis=0)
        for b in range(2):
            qh = qkvt[0, pl.ds(r, HD), b * qb:(b + 1) * qb]
            s = dot(kh, qh, 0, 0)
            m = jnp.max(s, axis=0, keepdims=True)
            p = jnp.exp2((s - m) * (log2_e * HD ** -0.5)).astype(BF16)
            o = dot(vh, p)
            total = o[HD:HD + 1, :]
            ot[pl.ds(r, HD), b * qb:(b + 1) * qb] = (o[:HD, :] / total).astype(BF16)
            lse_v[pl.ds(h, 1), b * qb:(b + 1) * qb] = m * HD ** -0.5 + jnp.log(total)
        for s, n in enumerate((2, 8, 14)):
            @pl.when(h == n)
            def _(s=s):
                gp.step(s)
                g1.step(s)
                g3.step(s)
                if s:
                    g3.step_over(s - 1)
                if s == 2:
                    g2.start()
        return c

    lax.fori_loop(0, heads, head, 0)
    save(ot, ot_o)
    save(lse_v, lse_o)
    for s in range(3, gp.last + 1):
        gp.step(s)
    gp.all_mates()
    save(wp_v, wp_o)

    def proj(i, c):
        r = pl.multiple_of(i * 512, 512)
        v = dot(ot[:, pl.ds(r, 512)], wp_v[...], 0, 0) + x_v[pl.ds(r, 512), :].astype(F32) + sm_v[4:5, :]
        mid[pl.ds(r, 512), :] = v
        m = jnp.mean(v, axis=-1, keepdims=True)
        d = v - m
        s = d * lax.rsqrt(jnp.mean(d * d, axis=-1, keepdims=True) + norm_eps)
        n2[pl.ds(r, 512), :] = (s * sm_v[5:6, :] + sm_v[6:7, :]).astype(BF16)
        acc[pl.ds(r, 512), :] = v + sm_v[7:8, :]
        return c

    lax.fori_loop(0, T // 512, proj, 0)
    save(mid, mid_o)
    save(n2, n2_o)
    for k in range(FF // tile):
        kk = k * tile
        b1_v[k:k + 1, :] = sm_v[8 + kk // D:9 + kk // D, kk % D:kk % D + tile]
    for s in range(3, g1.last + 1):
        g1.step(s)
        g3.step(s)
        g3.step_over(s - 1)
    g3.step_over(g3.last)
    g2.step(0)
    g1.all_mates()
    g3.all_mates()
    g2.own_mate()
    save(w1_v, w1_o)
    saves = {}
    order = [0]
    for k in range(1, here.count // 2):
        order += [-k, k]
    order.append(here.count // 2)

    def tcp(k, slot, t):
        return pltpu.make_async_copy((hst, gst)[k].at[slot], (h_o, g_o)[k].at[t], tsem.at[k, slot])

    def wcp(j, t):
        at = pl.ds(pl.multiple_of(t * tile, tile), tile)
        return pltpu.make_async_copy(w2_v.at[at, :], w2_o.at[at, :], tsem.at[2, j])

    def turn(j):
        odd = j % 2
        return here.chip((1 - odd) * (j // 2) - odd * ((j + 1) // 2))

    def mlp_tile(j, c):
        t = turn(j)
        slot = j % 2
        for k in range(g2.last + 1):
            @pl.when(j == 2 * k + 1)
            def _(k=k):
                g2.step_over(k)
                if k < g2.last:
                    g2.step(k + 1)
                g2.step_mate(k)

        wcp(j, t).start()

        @pl.when(j >= 2)
        def _():
            for k in range(2):
                tcp(k, slot, turn(j - 2)).wait()

        col = pl.multiple_of(t * tile, tile)

        def mlp(i, c):
            r = pl.multiple_of(i * 512, 512)
            u = dot(n2[pl.ds(r, 512), :], w1_v[:, pl.ds(col, tile)]) + b1_v[pl.ds(t, 1), :]
            cdf = 0.5 + 0.5 * lax.erf(u * root_half)
            hb = (u * cdf).astype(BF16)
            hst[slot, pl.ds(r, 512), :] = hb
            gst[slot, pl.ds(r, 512), :] = (cdf + (u * inv_root_tau) * jnp.exp2(u * u * (-0.5 * log2_e))).astype(BF16)
            acc[pl.ds(r, 512), :] += dot(hb, w2_v[pl.ds(col, tile), :])
            return c

        lax.fori_loop(0, T // 512, mlp, 0)
        for k in range(2):
            tcp(k, slot, t).start()
        return c

    lax.fori_loop(0, len(order), mlp_tile, 0)
    for j in range(len(order) - 2, len(order)):
        for k in range(2):
            tcp(k, j % 2, here.chip(order[j])).wait()
    outs[3].wait()
    n1t[...] = acc[...].astype(BF16)
    save(n1t, out_o)
    for j, off in enumerate(order):
        wcp(j, here.chip(off)).wait()
    for i, c in enumerate(outs):
        if i != 3:
            c.wait()
    for g in (ga, gq, gp, g1, g3, g2):
        g.drain()
    xsend.wait_send()
    csend.wait_send()
    remote(cot.at[1 - y], cot_o, xsem.at[1, 0], xsem.at[1, 1], here.across()).wait_recv()


S = jax.ShapeDtypeStruct
V = pltpu.VMEM


def fwd_call(size, T, D, FF):
    tile = 2 * FF // size
    heads = D // HD
    small = (16, D)
    dma = pltpu.SemaphoreType.DMA
    steps = size // 4
    return pl.pallas_call(
        functools.partial(fwd_body, size),
        name="forward",
        in_specs=[ANY] * 9,
        out_specs=[ANY] * 16,
        out_shape=[S((T, D), BF16), S((T // 2, D), BF16), S((T, D), BF16), S(small, F32), S((3, D, D), BF16), S((D, D), BF16), S((D, FF), BF16), S((FF, D), BF16),
                   S((D, T), BF16), S((3, D, T), BF16), S((D, T), BF16), S((heads, T), F32), S((T, D), F32), S((T, D), BF16), S((FF // tile, T, tile), BF16), S((FF // tile, T, tile), BF16)],
        scratch_shapes=[V((T, D), BF16), V((size,) + small, BF16), V(small, F32), V((3, D, D), BF16), V((D, D), BF16), V((D, FF), BF16), V((FF, D), BF16),
                        V((D, T), BF16), V((3, D, T), BF16), V((D, T), BF16), V((heads, T), F32), V((T, D), F32), V((T, D), BF16), V((T, D), F32),
                        V((2, T, tile), BF16), V((2, T, tile), BF16), V((FF // tile, tile), F32), V((D, 16), F32),
                        dma((6, 2, 2, steps)), dma((6, 2, 2 * steps + 1)), dma((2, 2, 2 * steps + 1)), dma((2, 2, 2 * steps + 1)), dma((2, 2)), dma((8,)), dma((12,)), dma((3, max(2, FF // tile)))],
        compiler_params=pltpu.CompilerParams(vmem_limit_bytes=63 << 20, collective_id=0, has_side_effects=True),
    )


def fold(dst, *srcs):
    def one(q, c):
        if len(srcs) == 1:
            dst[q] = dst[q] + srcs[0][q]
            return c
        v = dst[q].astype(F32)
        for s in srcs:
            v = v + s[q].astype(F32)
        dst[q] = v.astype(dst.dtype)
        return c

    lax.fori_loop(0, dst.shape[0], one, 0)


def offset(j):
    odd = j % 2
    return odd * ((7 - j) // 2) - (1 - odd) * ((8 - j) // 2)


class Scatter:
    def __init__(self, here, land, rb, n, cols, msem, rsem, ysem, fin_o=None, y_o=None):
        self.pl, self.land, self.rb, self.n, self.cols = here, land, rb, n, cols
        self.msem, self.rsem, self.ysem, self.fin_o, self.y_o = msem, rsem, ysem, fin_o, y_o

    def cut(self, part):
        c0, w = self.cols
        return slice(c0, c0 + w) if part == 2 else slice(c0 + part * (w // 2), c0 + (part + 1) * (w // 2))

    def block(self, j, part=2):
        return self.land.at[j, 0:self.n, :, self.cut(part)]

    def came(self, d, s):
        return self.rb.at[d, s, 0:self.n, :, self.cut(d if s == 0 else 2)]

    def mate(self, j, src=None):
        dst = self.block(j)
        return remote(dst if src is None else src.at[:, :, self.cut(2)], dst, self.msem.at[0, j], self.msem.at[1, j], self.pl.partner())

    def settle(self, j, own):
        self.mate(j).wait_recv()
        fold(self.block(j), own.at[:, :, self.cut(2)])
        self.mate(j).wait_send()

    def ring(self, d, s):
        src = self.block(0, d) if s == 0 else self.block(2 * s - 1 + d)
        return remote(src, self.came(d, s), self.rsem.at[0, d, s], self.rsem.at[1, d, s], self.pl.side(d))

    def step(self, s):
        for d in range(2):
            if s:
                self.ring(d, s - 1).wait_recv()
                fold(self.block(2 * s - 1 + d, d if s == 1 else 2), self.came(d, s - 1))
            self.ring(d, s).start()

    def close(self):
        for d in range(2):
            self.ring(d, 3).wait_recv()
        fold(self.block(7), self.came(0, 3), self.came(1, 3))

    def view(self, ref):
        return ref.at[0:self.n, :, self.cut(2)]

    def over(self):
        return remote(self.block(7), self.view(self.y_o), self.ysem.at[0], self.ysem.at[1], self.pl.across())

    def keep(self):
        return pltpu.make_async_copy(self.block(7), self.view(self.fin_o), self.ysem.at[2])

    def finish(self):
        self.close()
        self.over().start()
        self.keep().start()

    def drain_ring(self):
        for s in range(4):
            for d in range(2):
                self.ring(d, s).wait_send()

    def drain(self):
        self.drain_ring()
        self.over().wait_send()
        self.keep().wait()


class Group:
    def __init__(self, *parts):
        self.parts = parts

    def send(self, j, src):
        for p in self.parts:
            p.mate(j, src).start()

    def settle(self, j, own):
        for p in self.parts:
            p.settle(j, own)

    def step(self, s):
        for p in self.parts:
            p.step(s)

    def finish(self):
        for p in self.parts:
            p.finish()

    def drain(self):
        for p in self.parts:
            p.drain()

    def arrive(self):
        for p in self.parts:
            p.over().wait_recv()


def bwd_body(size, valid, cotangent, cot_in, out, x, sm, wqkv, wp, w1, w2, n1t, qkvt, ot, lse, mid, n2, hs, gs,
             out_o, gx_o, gxr_o, dw2_o, dw2_y, dw1_o, dw1_y, dwp_o, dwp_y, dq_o, dq_y, sg_o,
             g_v, n2_v, gacc, h_v, pre_v, w1_v, w2_v, b1g, mid_v, qkvt_v, ot_v, lse_v, sm_v, sg_v, sgm_v, sgy_v,
             st_v, land_a, land_b, land_p, land_s, rb_a, rb_b, rb_p, rb_s,
             sem, tsem, wsem, mlsem, xsem, msem, rsem, ysem, ssem, gsem, free):
    here = Place(size)
    y, core = here.y, here.core
    half = T // 2
    ymine = pl.multiple_of(y * half, half)
    yother = pl.multiple_of((1 - y) * half, half)

    def cp(a, b, i):
        return pltpu.make_async_copy(a, b, sem.at[i])

    first = [cp(cotangent.at[y], g_v.at[pl.ds(ymine, half), :], 0), cp(cot_in, g_v.at[pl.ds(yother, half), :], 1), cp(n2, n2_v, 2), cp(sm, sm_v, 3)]
    later = [cp(qkvt, qkvt_v, 4), cp(ot, ot_v, 5), cp(lse, lse_v, 6)]
    last = [cp(x, h_v, 7), cp(n1t, w1_v, 8)]

    def chip(j):
        return here.chip(offset(j))

    def tl(t, s):
        c = pl.multiple_of(t * 512, 512)
        d = pl.multiple_of(s * 512, 512)
        return [
            pltpu.make_async_copy(hs.at[t], h_v.at[:, pl.ds(d, 512)], tsem.at[s, 0]),
            pltpu.make_async_copy(gs.at[t], pre_v.at[t], tsem.at[s, 1]),
            pltpu.make_async_copy(w1.at[:, pl.ds(c, 512)], w1_v.at[:, pl.ds(d, 512)], tsem.at[s, 2]),
            pltpu.make_async_copy(w2.at[pl.ds(c, 512), :], w2_v.at[pl.ds(d, 512), :], tsem.at[s, 3]),
        ]

    for c in first:
        c.start()
    for c in tl(chip(0), 0):
        c.start()
    for c in later:
        c.start()
    here.barrier()
    osend = remote(out.at[pl.ds(yother, half), :], out_o, gsem.at[0, 0], gsem.at[0, 1], here.across())
    osend.start()
    def scatter(i, land, rb, n, c0, w, fin_o, y_o):
        return Scatter(here, land, rb, n, (c0, w), msem.at[i], rsem.at[i], ysem.at[i], fin_o, y_o)

    s2 = Group(*[scatter(i, land_a, rb_a, 4, i * 512, 512, dw2_o, dw2_y) for i in range(2)])
    s1 = Group(*[scatter(2 + i, land_b, rb_b, 4, i * 512, 512, dw1_o, dw1_y) for i in range(2)])
    sp = Group(scatter(4, land_p, rb_p, 1, 0, D, dwp_o, dwp_y))
    qcols = ((0, 512), (512, 256), (768, 256))
    sq = [Group(scatter(5 + g, land_a, rb_a, 3, c0, w, dq_o, dq_y)) for g, (c0, w) in enumerate(qcols)]
    ss = Scatter(here, land_s, rb_s, 2, (0, 128), None, rsem.at[8], None)
    for c in first:
        c.wait()
    flag = valid[y].astype(F32)
    sg_v[...] = jnp.zeros_like(sg_v)

    def mask(i, c):
        r = pl.multiple_of(i * 256, 256)
        v = g_v[pl.ds(r, 256), :].astype(F32) * flag
        g_v[pl.ds(r, 256), :] = v.astype(BF16)
        sg_v[7:8, :] += jnp.sum(v, axis=0, keepdims=True)
        return c

    lax.fori_loop(0, T // 256, mask, 0)

    def st2(j, k):
        return st_v.at[0, pl.ds((j % 2) * 8 + k * 4, 4)]

    def tile(j, c):
        s = j % 2
        t = chip(j)

        @pl.when(j + 1 < NTILE)
        def _():
            for k in tl(chip(j + 1), 1 - s):
                k.start()

        for k in tl(t, s):
            k.wait()
        col = pl.ds(pl.multiple_of(s * 512, 512), 512)
        gb = g_v[...]
        st_v[0, pl.ds(s * 8, 8)] = dot(h_v[:, col], gb, 0, 0).astype(BF16).reshape(8, 64, D)
        s2.send(j, st2(j, 1 - core))
        pre = (dot(gb, w2_v[col, :], 1, 1) * pre_v[t].astype(F32)).astype(BF16)
        pre_v[t] = pre
        b1g[pl.ds(t, 1), :] = jnp.sum(pre.astype(F32), axis=0, keepdims=True)
        v = dot(pre, w1_v[:, col], 1, 1)

        @pl.when(j == 0)
        def _():
            gacc[...] = v

        @pl.when(j > 0)
        def _():
            gacc[...] += v

        s2.settle(j, st2(j, core))
        for k, n in enumerate((0, 2, 4)):
            @pl.when(j == n)
            def _(k=k):
                s2.step(k)

        return c

    lax.fori_loop(0, NTILE, tile, 0)
    for c in last:
        c.start()
    sg_v[8:16, 0:512] = b1g[...]

    def slots(q):
        return (2 * q + 7) % 8, 2 * q

    def st1(q, i, k):
        return st_v.at[1 + q % 2, pl.ds(i * 8 + k * 4, 4)]

    def settle1(q):
        for i, j in enumerate(slots(q)):
            s1.settle(j, st1(q, i, core))

    def pair1(q, c):
        at = [pl.ds(pl.multiple_of(chip(j) * 128, 128), 128) for j in slots(q)]
        left = jnp.concatenate([n2_v[:, a] for a in at], axis=1)
        for cb in range(4):
            for k in range(2):
                v = dot(left, pre_v[2 * cb + k], 0, 0).astype(BF16)
                for i in range(2):
                    for e in range(2):
                        st_v[1 + q % 2, i * 8 + e * 4 + cb, :, k * 512:(k + 1) * 512] = v[i * 128 + e * 64:i * 128 + e * 64 + 64]
        for i, j in enumerate(slots(q)):
            s1.send(j, st1(q, i, 1 - core))

        @pl.when(q > 0)
        def _():
            settle1(q - 1)

        @pl.when(q == 1)
        def _():
            s2.step(3)
            s1.step(0)

        return c

    lax.fori_loop(0, 4, pair1, 0)
    wpl = [pltpu.make_async_copy(wp.at[:, i * 512:(i + 1) * 512], pre_v.at[6 + i], wsem.at[6 + i]) for i in range(2)]
    wl = [pltpu.make_async_copy(wqkv.at[j, :, i * 512:(i + 1) * 512], pre_v.at[2 * j + i], wsem.at[2 * j + i]) for j in range(3) for i in range(2)]
    for c in wpl + wl:
        c.start()
    settle1(3)

    def ml(i, s):
        return pltpu.make_async_copy(mid.at[pl.ds(pl.multiple_of(i * 256, 256), 256), :], mid_v.at[s], mlsem.at[s])

    ml(0, 0).start()

    def ln2(i, c):
        r = pl.multiple_of(i * 256, 256)
        s = i % 2

        @pl.when(i < 3)
        def _():
            ml(i + 1, 1 - s).start()

        ml(i, s).wait()
        back, dg, db = ln_back(gacc[pl.ds(r, 256), :], mid_v[s], sm_v[5:6, :])
        gm = g_v[pl.ds(r, 256), :].astype(F32) + back
        gacc[pl.ds(r, 256), :] = gm
        gb = gm.astype(BF16)
        g_v[pl.ds(r, 256), :] = gb
        sg_v[5:6, :] += dg
        sg_v[6:7, :] += db
        sg_v[4:5, :] += jnp.sum(gb.astype(F32), axis=0, keepdims=True)
        return c

    lax.fori_loop(0, 4, ln2, 0)
    for c in later + wpl:
        c.wait()
    for i in range(2):
        rows = slice(i * 512, (i + 1) * 512)
        st_v[0, i * 8:(i + 1) * 8] = dot(ot_v[rows, :], g_v[...]).astype(BF16).reshape(8, 64, D)
        w2_v[rows, :] = (dot(pre_v[6, rows, :], g_v[:, 0:512], 1, 1) + dot(pre_v[7, rows, :], g_v[:, 512:1024], 1, 1)).astype(BF16)

    def stp(j, k):
        return st_v.at[0, pl.ds(2 * chip(j) + k, 1)]

    def matep(j, c):
        sp.send(j, stp(j, 1 - core))
        return c

    def settlep(j, c):
        sp.settle(j, stp(j, core))
        return c

    lax.fori_loop(0, 8, matep, 0)
    s2.finish()
    s1.step(1)

    def stq(j, k):
        return st_v.at[:, 2 * chip(j) + k]

    def dqkv(g):
        c0, w = qcols[g]

        def product(k, c):
            j, i = k // 2, k % 2
            v = dot(w1_v[pl.ds(pl.multiple_of(i * 512, 512), 512), :], qkvt_v[j, c0:c0 + w, :], 1, 1).astype(BF16)
            st_v[j, pl.ds(i * 8, 8), :, c0:c0 + w] = v.reshape(8, 64, w)
            return c

        lax.fori_loop(0, 6, product, 0)

        def send(j, c):
            sq[g].send(j, stq(j, 1 - core))
            return c

        lax.fori_loop(0, 8, send, 0)

    def settleq(g):
        def one(j, c):
            sq[g].settle(j, stq(j, core))
            return c

        lax.fori_loop(0, 8, one, 0)

    def begin_p():
        lax.fori_loop(0, 8, settlep, 0)
        sp.step(0)

    def free_a():
        s2.drain()
        pl.semaphore_signal(free.at[0], inc=1, device_id=here.partner(), device_id_type=MESH)
        for d in range(2):
            pl.semaphore_signal(free.at[1], inc=1, device_id=here.side(d), device_id_type=MESH)

    def first_q():
        for c in last:
            c.wait()
        pl.semaphore_wait(free.at[0], 1)
        dqkv(0)

    def begin_q():
        settleq(0)
        pl.semaphore_wait(free.at[1], 2)
        sq[0].step(0)

    def second_q():
        settleq(1)
        sq[1].step(0)

    events = {
        0: [begin_p],
        2: [lambda: s1.step(2), lambda: sp.step(1), free_a],
        6: [lambda: s1.step(3), lambda: sp.step(2)],
        7: [first_q],
        8: [begin_q, lambda: sp.step(3)],
        10: [s1.finish, lambda: sq[0].step(1)],
        11: [sp.finish, lambda: dqkv(1)],
        12: [second_q, lambda: sq[0].step(2)],
        14: [lambda: sq[1].step(1), lambda: sq[0].step(3)],
    }

    def hd(h, c):
        bwd_head(h, qkvt_v, ot_v, w2_v, lse_v)
        for n, fns in events.items():
            @pl.when(h == n)
            def _(fns=fns):
                for fn in fns:
                    fn()
        return c

    lax.fori_loop(0, 16, hd, 0)
    for c in wl:
        c.wait()

    def row(i):
        return pl.multiple_of((1 - i // 2) * yother + (i // 2) * ymine + (i % 2) * 256, 256)

    def xsend(i):
        at = pl.ds(pl.multiple_of(i * 256, 256), 256)
        return remote(w2_v.at[at, :], gxr_o.at[at, :], xsem.at[0, i], xsem.at[1, i], here.across())

    def xkeep(i):
        return pltpu.make_async_copy(mid_v.at[i], gx_o.at[pl.ds(i * 256, 256), :], xsem.at[2, i])

    def fin(i, c):
        r = row(i)
        up = None
        for j in range(3):
            for k in range(2):
                v = dot(qkvt_v[j, k * 512:(k + 1) * 512, pl.ds(r, 256)], pre_v[2 * j + k], 0, 1)
                up = v if up is None else up + v
        back, dg, db = ln_back(up, h_v[pl.ds(r, 256), :].astype(F32), sm_v[0:1, :])
        v = gacc[pl.ds(r, 256), :] + back
        sg_v[0:1, :] += dg
        sg_v[1:2, :] += db

        @pl.when(i < 2)
        def _():
            w2_v[pl.ds(pl.multiple_of((i % 2) * 256, 256), 256), :] = v.astype(BF16)
            xsend(i % 2).start()

        @pl.when(i >= 2)
        def _():
            mid_v[i % 2] = v
            xkeep(i % 2).start()

        return c

    lax.fori_loop(0, 2, fin, 0)
    dqkv(2)
    sq[1].step(2)
    ones = jnp.ones((16, T), BF16)
    for j, row in ((0, 2), (2, 3)):
        sg_v[row:row + 1, :] = dot(ones, qkvt_v[j], 1, 1)[0:1, :]
    settleq(2)
    sq[2].step(0)
    sq[0].finish()
    lax.fori_loop(2, 4, fin, 0)
    sg1 = remote(sg_v, sgm_v, ssem.at[0, 0], ssem.at[0, 1], here.partner())
    sg1.start()
    sq[2].step(1)
    sq[1].step(3)
    sg1.wait_recv()
    sg1.wait_send()
    sg_v[...] = sg_v[...] + sgm_v[...]
    b1g[...] = sg_v[8:16, 0:512]
    for j in range(8):
        t = chip(j)
        land_s[j, 0] = sg_v[0:8, pl.ds(pl.multiple_of(t * 128, 128), 128)]
        land_s[j, 1, 4:8, :] = jnp.zeros((4, 128), F32)
        fb = b1g[pl.ds(t, 1), :]
        for q in range(4):
            land_s[j, 1, q:q + 1, :] = fb[:, q * 128:(q + 1) * 128]
    ss_steps(ss, 0)
    ss_steps(ss, 1)
    sq[2].step(2)
    ss_steps(ss, 2)
    sq[1].finish()
    ss_steps(ss, 3)
    sq[2].step(3)
    for d in range(2):
        ss_ring(ss, d, 3).wait_recv()
    fold(land_s.at[7], rb_s.at[0, 3], rb_s.at[1, 3])
    sg2 = remote(land_s.at[7], sgy_v, ssem.at[1, 0], ssem.at[1, 1], here.across())
    sg2.start()
    sq[2].finish()
    sg2.wait_recv()
    sg2.wait_send()
    fold(land_s.at[7], sgy_v)
    skeep = pltpu.make_async_copy(land_s.at[7], sg_o, ssem.at[2, 0])
    skeep.start()
    for s in range(4):
        for d in range(2):
            ss_ring(ss, d, s).wait_send()
    skeep.wait()
    for i in range(2):
        xsend(i).wait()
        xkeep(i).wait()
    osend.wait()
    for s in (s1, sp, *sq):
        s.drain()
    for s in (s2, s1, sp, *sq):
        s.arrive()


def ss_ring(ss, d, s):
    if s == 0:
        src, dst = ss.land.at[0, d], ss.rb.at[d, 0, d]
    else:
        src, dst = ss.land.at[2 * s - 1 + d], ss.rb.at[d, s]
    return remote(src, dst, ss.rsem.at[0, d, s], ss.rsem.at[1, d, s], ss.pl.side(d))


def ss_steps(ss, s):
    for d in range(2):
        if s:
            ss_ring(ss, d, s - 1).wait_recv()
            j = 2 * s - 1 + d
            if s == 1:
                ss.land[j, d] = ss.land[j, d] + ss.rb[d, 0, d]
            else:
                fold(ss.land.at[j], ss.rb.at[d, s - 1])
        ss_ring(ss, d, s).start()


def bwd_call(size):
    dma = pltpu.SemaphoreType.DMA
    block = S((4, 64, D), BF16)
    return pl.pallas_call(
        functools.partial(bwd_body, size),
        name="backward",
        in_specs=[pl.BlockSpec(memory_space=pltpu.SMEM)] + [ANY] * 17,
        out_specs=[ANY] * 12,
        out_shape=[S((T // 2, D), BF16), S((T // 2, D), F32), S((T // 2, D), BF16), block, block, block, block,
                   S((1, 64, D), BF16), S((1, 64, D), BF16), S((3, 64, D), BF16), S((3, 64, D), BF16), S((2, 8, 128), F32)],
        scratch_shapes=[V((T, D), BF16), V((T, D), BF16), V((T, D), F32), V((T, 1024), BF16), V((NTILE, T, 512), BF16), V((D, 1024), BF16), V((1024, D), BF16),
                        V((8, 512), F32), V((2, 256, D), F32), V((3, D, T), BF16), V((D, T), BF16), V((16, T), F32), V((16, D), F32), V((16, D), F32),
                        V((16, D), F32), V((2, 8, 128), F32),
                        V((3, 16, 64, D), BF16), V((8, 4, 64, D), BF16), V((8, 4, 64, D), BF16), V((8, 1, 64, D), BF16), V((8, 2, 8, 128), F32),
                        V((2, 4, 4, 64, D), BF16), V((2, 4, 4, 64, D), BF16), V((2, 4, 1, 64, D), BF16), V((2, 4, 2, 8, 128), F32),
                        dma((9,)), dma((2, 4)), dma((8,)), dma((2,)), dma((3, 2)), dma((8, 2, 8)), dma((9, 2, 2, 4)), dma((8, 3)), dma((3, 2)), dma((1, 2)),
                        pltpu.SemaphoreType.REGULAR((2,))],
        compiler_params=pltpu.CompilerParams(vmem_limit_bytes=67043328, collective_id=1, has_side_effects=True),
    )


def fast_body(clips, cotangent, valid, *shards):
    size = lax.axis_size("fsdp")
    me = lax.axis_index("fsdp")
    mine = lax.axis_index("seq")
    (g1, b1, wq, wk, wv, bq, bv, wp, bp, g2, b2, w1, fb1, w2, fb2) = shards
    n, m = g1.shape[0], fb1.shape[0]
    vecs = jnp.stack([g1, b1, bq, bv, bp, g2, b2, fb2])
    sml = lax.dynamic_update_slice(jnp.zeros((8, D), vecs.dtype), vecs, (0, me * n))
    fsm = lax.dynamic_update_slice(jnp.zeros((FF,), vecs.dtype), fb1, (me * m,)).reshape(-1, D)
    sml = jnp.concatenate([sml, fsm, jnp.zeros((8 - FF // D, D), vecs.dtype)])
    out, cot_in, x, sm, wqkv, wp_all, w1_all, w2_all, *saved = fwd_call(size, T, D, FF)(clips, cotangent, sml, wq, wk, wv, wp, w1, w2)
    out_in, gx, gx_in, dw2, dw2y, dw1, dw1y, dwp, dwpy, dq, dqy, sg = bwd_call(size)(
        valid, cotangent, cot_in, out, x, sm, wqkv, wp_all, w1_all, w2_all, *saved)

    def both(a, b):
        return a.astype(F32) + b.astype(F32)

    def halves(own, other):
        return jnp.where(lax.broadcasted_iota(jnp.int32, (2, 1, 1), 0) == mine, own[None], other[None])

    dw2 = both(dw2, dw2y).reshape(-1, D)
    dw1 = both(dw1, dw1y).transpose(1, 0, 2).reshape(n, -1)
    dq = both(dq, dqy)
    dwp = both(dwp, dwpy)[0]
    own = lax.dynamic_slice(sg[0], (0, me % 2 * n), (8, n))
    dfb1 = lax.dynamic_slice(sg[1, 0:4].reshape(-1), (me % 2 * m,), (m,))
    out = halves(lax.dynamic_slice(out, (mine * (T // 2), 0), (T // 2, D)), out_in)
    gx = halves(gx, gx_in.astype(F32))
    return (out, gx, own[0], own[1], dq[0], dq[1], dq[2], own[2], own[3], dwp, own[4], own[5], own[6], dw1, dfb1, dw2, own[7])


def solution(mesh):
    in_specs = (
        P("fsdp", "seq", None),
        P("fsdp", "seq", None),
        P("fsdp"),
        P("fsdp"),
        P("fsdp"),
        P("fsdp", None),
        P("fsdp", None),
        P("fsdp", None),
        P("fsdp"),
        P("fsdp"),
        P("fsdp", None),
        P("fsdp"),
        P("fsdp"),
        P("fsdp"),
        P("fsdp", None),
        P("fsdp"),
        P("fsdp", None),
        P("fsdp"),
    )
    out_specs = (
        P("fsdp", "seq", None),
        P("fsdp", "seq", None),
        P("fsdp"),
        P("fsdp"),
        P("fsdp", None),
        P("fsdp", None),
        P("fsdp", None),
        P("fsdp"),
        P("fsdp"),
        P("fsdp", None),
        P("fsdp"),
        P("fsdp"),
        P("fsdp"),
        P("fsdp", None),
        P("fsdp"),
        P("fsdp", None),
        P("fsdp"),
    )
    quick = mesh.shape["seq"] == 2 and mesh.shape["fsdp"] == 16
    return jax.shard_map(fast_body if quick else body, mesh=mesh, in_specs=in_specs, out_specs=out_specs, check_vma=False)
```
